512 devices in a mesh: lat: 16 (over y_lo, x, core), lon: 32 (over y_hi, z).
Axes of the slice: x: 4, y: 8 (y_hi: 4, y_lo: 2; y = y_hi * 2 + y_lo), z: 8, core: 2. Of those that a mesh axis runs over, the one named last changes fastest.
Arguments:
- state_block: float32 [64, 1440, 256], P('lat', 'lon'), may hold values from -5 to 5
- stored_fields: bfloat16 [64, 1440, 1024], P('lat', 'lon'), may hold values from -14 to 14
- slope_fields: bfloat16 [64, 1440, 192], P('lat', 'lon'), may hold values from 0.5 to 1.5
- kernels: bfloat16 [3, 9, 64, 64], replicated, may hold values from -0.25 to 0.25
- spectral_gains: float32 [64, 721], replicated, may hold values from 0.25 to 4
Outputs:
- next_block: float32 [64, 1440, 256], P('lat', 'lon')
- diag_coef: float32 [4, 4], replicated
- stored_coef: float32 [16, 4], replicated
- norm_factor: float32 [4, 4], replicated
The draws below stay inside these ranges and needn't reach their ends.
All inputs are finite; a program needn't handle non-finite values.
Results may differ from the reference program's by a relative error of at most 0.0062.
Values may be sent and summed in bfloat16 or wider, within the bound.
No kernel may reach another device: no remote copies, remote signals or barrier semaphores. Data moves between devices by JAX's collectives and lax.ppermute only.
A program may use at most 64 MiB of HBM per device.

```python
import math
import jax
import jax.numpy as jnp
from jax import lax

C = 64
VECS = 4
STORED = 16
LAYERS = 3
NLAT = 64
NLON = 1440
K = 721


def shared_fields(key):
    field_shape = (NLAT, NLON, VECS, C)
    return jnp.clip(jax.random.normal(jax.random.fold_in(key, 11), field_shape, jnp.float32), -5.0, 5.0)


def draw_state_block(key, part):
    return shared_fields(key).reshape(NLAT, NLON, VECS * C).astype(jnp.float32)


def draw_stored_fields(key, part):
    shared = shared_fields(key)
    noise_part = jnp.clip(jax.random.normal(jax.random.fold_in(key, 12), (NLAT, NLON, STORED, C), jnp.float32), -5.0, 5.0)
    mixing = jnp.clip(jax.random.normal(jax.random.fold_in(key, 13), (STORED, VECS), jnp.float32), -2.0, 2.0) * 0.25
    summed = 0.7 * noise_part
    for vector in range(VECS):
        summed = summed + mixing[None, None, :, vector, None] * shared[:, :, vector:vector + 1, :]
    return summed.astype(jnp.bfloat16).reshape(NLAT, NLON, STORED * C)


def steps_of(own_key, extent, cuts, smallest, top_value):
    gain, own = 1.0, jax.random.fold_in(own_key, 6)
    for dim, parts in cuts:
        steps = jnp.exp(jax.random.uniform(jax.random.fold_in(own, dim), (parts,), jnp.float32, smallest / len(cuts), top_value / len(cuts)))
        gain = gain * jnp.repeat(steps, extent[dim] // parts).reshape([-1 if axis == dim else 1 for axis in range(len(extent))])
    return gain


def gaussian(stream_key, dims, scale, reach, kind=jnp.bfloat16):
    array = jax.random.normal(stream_key, dims, jnp.float32) * scale
    return jnp.minimum(jnp.maximum(array, -reach), reach).astype(kind)


def setup_inputs(seed: int = 0) -> dict:
    streams_of = jax.random.split(jax.random.key(seed), 6)
    state_block = draw_state_block(jax.random.fold_in(streams_of[5], 71), 0)
    stored_fields = draw_stored_fields(jax.random.fold_in(streams_of[5], 71), 0)
    slope_fields = jnp.clip(0.5 + 1.0 * jax.random.uniform(streams_of[2], (NLAT, NLON, LAYERS * C), jnp.float32) ** steps_of(streams_of[2], (NLAT, NLON, LAYERS * C), ((0, 16), (1, 32)), -0.2, 0.2), 0.5, 1.5).astype(jnp.bfloat16)
    kernels = gaussian(streams_of[3], (LAYERS, 9, C, C), (9 * C) ** -0.5, 0.25)
    spectral_gains = jnp.clip(jnp.exp(jax.random.uniform(streams_of[4], (C, K), jnp.float32, math.log(0.25), math.log(4.0))), 0.25, 4.0)
    return {"state_block": state_block, "stored_fields": stored_fields, "slope_fields": slope_fields, "kernels": kernels, "spectral_gains": spectral_gains}


highest = lax.Precision.HIGHEST

def upper_factor(gram_matrix):
    count = gram_matrix.shape[0]
    nothing = gram_matrix[0, 0] * 0.0
    entries = [[nothing for col in range(count)] for row in range(count)]
    for row in range(count):
        total = gram_matrix[row, row]
        for inner in range(row):
            total = total - entries[inner][row] * entries[inner][row]
        entries[row][row] = jnp.sqrt(total)
        for col in range(row + 1, count):
            value = gram_matrix[row, col]
            for inner in range(row):
                value = value - entries[inner][row] * entries[inner][col]
            entries[row][col] = value / entries[row][row]
    inverse = [[nothing for col in range(count)] for row in range(count)]
    for col in range(count):
        inverse[col][col] = 1.0 / entries[col][col]
        for row in range(col - 1, -1, -1):
            value = nothing
            for inner in range(row + 1, col + 1):
                value = value + entries[row][inner] * inverse[inner][col]
            inverse[row][col] = -value / entries[row][row]
    factor = jnp.stack([jnp.stack(line) for line in entries])
    inverted = jnp.stack([jnp.stack(line) for line in inverse])
    return (factor, inverted)

def area_weights():
    latitude = (jnp.arange(NLAT).astype(jnp.float32) + 0.5) / NLAT
    return jnp.cos(jnp.pi * (latitude - 0.5)).astype(jnp.float32)

def padded(field):
    field = jnp.pad(field, ((1, 1), (0, 0), (0, 0), (0, 0)))
    return jnp.concatenate([field[:, -1:], field, field[:, :1]], axis=1)

def convolve(field, kernel, adjoint):
    extended = padded(field).astype(jnp.float32)
    weights = kernel.astype(jnp.float32)
    summed = jnp.zeros(field.shape, jnp.float32)
    for row_step in range(3):
        for col_step in range(3):
            tap_index = 3 * row_step + col_step
            if adjoint:
                piece = extended[2 - row_step:2 - row_step + NLAT, 2 - col_step:2 - col_step + NLON]
                summed = summed + jnp.einsum('abvd,cd->abvc', piece, weights[tap_index], precision=highest)
            else:
                piece = extended[row_step:row_step + NLAT, col_step:col_step + NLON]
                summed = summed + jnp.einsum('abvc,cd->abvd', piece, weights[tap_index], precision=highest)
    return summed

def spectral_filter(field, spectral_gains, area_weight):
    weighted = field.astype(jnp.float32) * area_weight[:, None, None, None]
    spectrum = jnp.fft.rfft(weighted, axis=1)
    spectrum = spectrum * jnp.transpose(spectral_gains)[None, :, None, :]
    filtered = jnp.fft.irfft(spectrum, n=NLON, axis=1)
    return (filtered * area_weight[:, None, None, None]).astype(jnp.bfloat16)

def reference(state_block, stored_fields, slope_fields, kernels, spectral_gains):
    vectors = state_block.reshape(NLAT, NLON, VECS, C)
    stored = stored_fields.reshape(NLAT, NLON, STORED, C).astype(jnp.float32)
    slopes = slope_fields.reshape(NLAT, NLON, LAYERS, C).astype(jnp.float32)
    area_weight = area_weights()
    hidden = vectors.astype(jnp.bfloat16)
    for layer in range(LAYERS):
        summed = convolve(hidden, kernels[layer], False)
        hidden = (slopes[:, :, layer][:, :, None, :] * summed).astype(jnp.bfloat16)
    filtered = spectral_filter(hidden, spectral_gains, area_weight)
    adjoint = (slopes[:, :, LAYERS - 1][:, :, None, :] * filtered.astype(jnp.float32)).astype(jnp.bfloat16)
    for layer in range(LAYERS - 1, 0, -1):
        summed = convolve(adjoint, kernels[layer], True)
        adjoint = (slopes[:, :, layer - 1][:, :, None, :] * summed).astype(jnp.bfloat16)
    image = convolve(adjoint, kernels[0], True)
    weighting = 1.0 / (NLAT * NLON * C)
    diag_coef = jnp.einsum('abvc,abwc->vw', vectors, image, precision=highest) * weighting
    stored_coef = jnp.einsum('absc,abwc->sw', stored, image, precision=highest) * weighting
    residual = image - jnp.einsum('abvc,vw->abwc', vectors, diag_coef, precision=highest)
    residual = residual - jnp.einsum('absc,sw->abwc', stored, stored_coef, precision=highest)
    gram_matrix = jnp.einsum('abvc,abwc->vw', residual, residual, precision=highest) * weighting
    norm_factor, inverse = upper_factor(gram_matrix)
    next_fields = jnp.einsum('abvc,vw->abwc', residual, inverse, precision=highest)
    return (next_fields.reshape(NLAT, NLON, VECS * C), diag_coef, stored_coef, norm_factor)
```

```python
import functools

import jax
import jax.numpy as jnp
import numpy as np
from jax import lax
from jax.experimental import pallas as pl
from jax.experimental.pallas import tpu as pltpu
from jax.sharding import PartitionSpec as P

F32 = jnp.float32
BF16 = jnp.bfloat16
HIGHEST = lax.Precision.HIGHEST

ROWS, COLS, CH, VECS, STORED, LAYERS = 4, 45, 64, 4, 16, 3
NLAT, NLON, WAVES = 64, 1440, 721
LANES = VECS * CH
HALO = 3
EXT = ROWS + 2 * HALO
PITCH = 64
LEAD = 8
FLAT = LEAD + EXT * PITCH + 8
SLOTS = 32
FIELDS = VECS + STORED + VECS
VMEM = pl.BlockSpec(memory_space=pltpu.VMEM)


def lane_ids(shape):
    return lax.broadcasted_iota(jnp.int32, shape, len(shape) - 1)


def row_ids(shape):
    return lax.broadcasted_iota(jnp.int32, shape, len(shape) - 2)


def tables():
    wave = 4 * np.arange(192)[None, :] + np.arange(4)[:, None]
    live = wave < WAVES
    q, t, j = np.meshgrid(np.arange(3), np.arange(8), np.arange(16), indexing="ij")
    slot = (16 * q + j).reshape(-1)
    point = (45 * t).reshape(-1) + 3 + slot
    angle = 2 * np.pi * ((wave[:, :, None] * point) % NLON) / NLON
    keep = live[:, :, None] & (slot < COLS)
    ahead = np.concatenate([np.cos(angle) * keep, np.sin(angle) * keep], axis=2)
    q, t, j = np.meshgrid(np.arange(4), np.arange(8), np.arange(16), indexing="ij")
    slot = (16 * q + j).reshape(-1)
    point = (45 * t).reshape(-1) - 3 + slot
    angle = 2 * np.pi * ((wave[:, None, :] * point[None, :, None]) % NLON) / NLON
    keep = live[:, None, :] & (slot < COLS + 2 * HALO)[None, :, None]
    back = np.concatenate([np.cos(angle) * keep, np.sin(angle) * keep], axis=2)
    return ahead.astype(jnp.bfloat16), back.astype(jnp.bfloat16)


def edges_kernel(q_ref, s_ref, south_ref, north_ref):
    q = q_ref[...].astype(BF16)
    s = s_ref[...]
    south_ref[:, :, 0:LANES] = q[1:4]
    south_ref[:, :, LANES:] = s[1:4]
    north_ref[:, :, 0:LANES] = q[0:3]
    north_ref[:, :, LANES:] = s[0:3]


def sides_kernel(q_ref, s_ref, above_ref, below_ref, first_ref, last_ref):
    for row in range(EXT):
        if row < HALO:
            line = above_ref[row].astype(F32)
        elif row < HALO + ROWS:
            line = None
        else:
            line = below_ref[row - HALO - ROWS].astype(F32)
        if line is None:
            own_q = q_ref[row - HALO]
            own_s = s_ref[row - HALO].astype(F32)
            first_ref[row, :, 0:LANES] = own_q[0:8].astype(BF16)
            first_ref[row, :, LANES:] = own_s[0:8].astype(BF16)
            last_ref[row] = own_s[COLS - 8 : COLS].astype(BF16)
        else:
            first_ref[row] = line[0:8].astype(BF16)
            last_ref[row] = line[COLS - 8 : COLS, LANES:].astype(BF16)


def weights_kernel(plain_ref, turned_ref, ahead_ref, back_ref):
    shape = (LANES, LANES)
    same = (row_ids(shape) // CH) == (lane_ids(shape) // CH)

    def spread(block):
        block = block.astype(F32)
        wide = jnp.concatenate([block] * VECS, axis=1)
        return jnp.where(same, jnp.concatenate([wide] * VECS, axis=0), 0.0).astype(BF16)

    def tap(index, carry):
        ahead_ref[index] = spread(plain_ref[index])
        back_ref[index] = spread(turned_ref[index])
        return carry

    lax.fori_loop(0, LAYERS * 9, tap, 0)


def slope_lanes(slopes_ref, layer, start, count):
    pair = slopes_ref[pl.ds(start, count), (layer // 2) * 128 : (layer // 2) * 128 + 128]
    other = pltpu.roll(pair, 64, axis=1)
    low = lane_ids(pair.shape) < 64
    both = jnp.where(low, pair, other) if layer % 2 == 0 else jnp.where(low, other, pair)
    return jnp.concatenate([both, both], axis=1)


def convolve(field_ref, shifted_ref, weights_ref, layer, first, count):
    have = (count + 2) * PITCH
    start = LEAD + (first - 1) * PITCH
    for step in range(3):
        shifted_ref[0:have, step * LANES : (step + 1) * LANES] = field_ref[
            pl.ds(start + step - 1, have), :
        ].astype(BF16)
    total = None
    for step in range(3):
        part = jnp.dot(
            shifted_ref[step * PITCH : (step + count) * PITCH, :],
            weights_ref[layer * 3 + step],
            preferred_element_type=F32,
        )
        total = part if total is None else total + part
    return total


def forward_kernel(
    q_ref, s_ref, above_ref, below_ref, right_ref, weights_ref, send_ref, field_ref, slopes_ref, shifted_ref
):
    field_ref[...] = jnp.zeros((FLAT, LANES), F32)
    slopes_ref[...] = jnp.zeros((FLAT, LANES), F32)
    for row in range(EXT):
        at = LEAD + row * PITCH
        if row < HALO:
            field = above_ref[row, :, 0:LANES].astype(F32)
            slope = above_ref[row, :, LANES:].astype(F32)
        elif row < HALO + ROWS:
            field = q_ref[row - HALO].astype(BF16).astype(F32)
            slope = s_ref[row - HALO].astype(F32)
        else:
            field = below_ref[row - HALO - ROWS, :, 0:LANES].astype(F32)
            slope = below_ref[row - HALO - ROWS, :, LANES:].astype(F32)
        side = right_ref[row].astype(F32)
        field_ref[at : at + COLS, :] = field
        field_ref[at + COLS : at + COLS + 8, :] = side[:, 0:LANES]
        slopes_ref[at : at + COLS, 0:192] = slope
        slopes_ref[at + COLS : at + COLS + 8, 0:192] = side[:, LANES:]
    for layer in range(LAYERS):
        first = layer + 1
        count = EXT - 2 * first
        total = convolve(field_ref, shifted_ref, weights_ref, layer, first, count)
        start = LEAD + first * PITCH
        total = total * slope_lanes(slopes_ref, layer, start, count * PITCH)
        field_ref[start : start + count * PITCH, :] = total.astype(BF16).astype(F32)
    for row in range(ROWS):
        line = field_ref[pl.ds(LEAD + (HALO + row) * PITCH + HALO, 48), :]
        for group in range(8):
            pieces = [
                line[16 * q : 16 * q + 16, group * SLOTS : (group + 1) * SLOTS] for q in range(3)
            ]
            pieces.append(jnp.zeros((16, SLOTS), F32))
            send_ref[row * 8 + group] = jnp.concatenate(pieces, axis=1).astype(BF16)


def filter_kernel(got_ref, ahead_ref, back_ref, gains_ref, send_ref, work_ref):
    quarter = [
        got_ref[8 * part : 8 * part + 8].astype(F32).reshape(128, 128) for part in range(4)
    ]
    even, odd = quarter[0] + quarter[2], quarter[1] + quarter[3]
    across, along = quarter[0] - quarter[2], quarter[1] - quarter[3]
    real = [even + odd, across, even - odd, across]
    imag = [None, -along, None, along]
    low = lane_ids((128, 128)) < SLOTS

    def turn(value, shift):
        return value if shift % 128 == 0 else pltpu.roll(value, shift % 128, axis=1)

    for kind in range(4):
        for q in range(3):
            a = real[kind]
            b = imag[kind]
            left, right = turn(a, -SLOTS * q), turn(a, SLOTS - SLOTS * q)
            if b is None:
                top = jnp.where(low, left, 0.0)
                bottom = jnp.where(low, 0.0, -right)
            else:
                top = jnp.where(low, left, turn(b, SLOTS - SLOTS * q))
                bottom = jnp.where(low, turn(b, -SLOTS * q), -right)
            work_ref[128 * q : 128 * q + 128, :] = top.astype(BF16)
            work_ref[384 + 128 * q : 512 + 128 * q, :] = bottom.astype(BF16)
        spectrum = jnp.dot(ahead_ref[kind], work_ref[...], preferred_element_type=F32)
        weight = gains_ref[pl.ds(kind, 192, stride=4), :]
        spectrum = spectrum * weight
        below = jnp.where(
            lane_ids((192, 128)) < SLOTS, -turn(spectrum, -SLOTS), turn(spectrum, SLOTS)
        )
        packed = jnp.concatenate([spectrum, below], axis=0).astype(BF16)
        part = jnp.dot(back_ref[kind], packed, preferred_element_type=F32)
        if kind == 0:
            zero = part
        elif kind == 1:
            one = part
        elif kind == 2:
            two = part
        else:
            three = part
    plus, minus = zero + two, zero - two
    swing = one + three
    turned = turn(three - one, -SLOTS)
    result = [plus + swing, minus + turned, plus - swing, minus - turned]
    lane = lane_ids((128, 128))
    for part in range(4):
        packed = result[part][0:128]
        for q in range(1, 4):
            packed = jnp.where(
                lane >= SLOTS * q, turn(result[part][128 * q : 128 * q + 128], SLOTS * q), packed
            )
        send_ref[8 * part : 8 * part + 8] = packed.reshape(8, 16, 128).astype(BF16)


def twice(tile, half):
    other = pltpu.roll(tile, 64, axis=1)
    low = lane_ids(tile.shape) < 64
    return jnp.where(low, tile, other) if half == 0 else jnp.where(low, other, tile)


def gram_rows(first, rows_ref):
    total = None
    for index, count in first:
        shape = (24, 128)
        pick = (row_ids(shape) == 2 * index + (lane_ids(shape) // 64)).astype(F32)
        rows = rows_ref[index]
        part = lax.dot_general(
            pick, rows, (((1,), (1,)), ((), ())), precision=HIGHEST, preferred_element_type=F32
        )
        total = part if total is None else total + part
    return total


def stored_kernel(q_ref, p_ref, out_ref, rows_ref):
    rows_ref[...] = jnp.zeros(rows_ref.shape, F32)
    known = 10
    for right in range(known):
        for half in range(2):
            totals = [None] * (right + 1)
            for row in range(ROWS):
                tile = tile_of(q_ref, p_ref, None, row, right)
                doubled = twice(tile, half)
                for left in range(right + 1):
                    product = tile_of(q_ref, p_ref, None, row, left) * doubled
                    totals[left] = product if totals[left] is None else totals[left] + product
            for left in range(right + 1):
                rows_ref[left, 2 * right + half : 2 * right + half + 1, :] = jnp.sum(
                    totals[left], axis=0, keepdims=True
                )
    out_ref[...] = gram_rows([(index, 128) for index in range(known)], rows_ref)


def tile_of(q_ref, p_ref, u_ref, row, index):
    if index < 2:
        return q_ref[row, :, index * 128 : (index + 1) * 128]
    if index < 10:
        return p_ref[row, :, (index - 2) * 128 : (index - 1) * 128].astype(F32)
    return u_ref[row, :, (index - 10) * 128 : (index - 9) * 128]


def adjoint_kernel(
    q_ref,
    p_ref,
    s_ref,
    above_ref,
    below_ref,
    right_ref,
    left_ref,
    got_ref,
    gabove_ref,
    gbelow_ref,
    weights_ref,
    known_ref,
    u_ref,
    sums_ref,
    field_ref,
    slopes_ref,
    shifted_ref,
    rows_ref,
):
    field_ref[0:LEAD, :] = jnp.zeros((LEAD, LANES), F32)
    field_ref[FLAT - 8 : FLAT, :] = jnp.zeros((8, LANES), F32)
    slopes_ref[...] = jnp.zeros((FLAT, LANES), F32)
    for row in range(EXT):
        at = LEAD + row * PITCH
        if row < HALO:
            slope = above_ref[row, :, LANES:].astype(F32)
        elif row < HALO + ROWS:
            slope = s_ref[row - HALO].astype(F32)
        else:
            slope = below_ref[row - HALO - ROWS, :, LANES:].astype(F32)
        slopes_ref[at : at + HALO, 0:192] = left_ref[row].astype(F32)[8 - HALO : 8]
        slopes_ref[at + HALO : at + HALO + COLS, 0:192] = slope
        slopes_ref[at + HALO + COLS : at + HALO + COLS + HALO, 0:192] = right_ref[
            row, :, LANES:
        ].astype(F32)[0:HALO]
    for row in range(EXT):
        at = LEAD + row * PITCH
        if row < HALO:
            source, base = gabove_ref, row * 8
        elif row < HALO + ROWS:
            source, base = got_ref, (row - HALO) * 8
        else:
            source, base = gbelow_ref, (row - HALO - ROWS) * 8
        blocks = [source[base + group].astype(F32) for group in range(8)]
        for q in range(4):
            field_ref[at + 16 * q : at + 16 * q + 16, :] = jnp.concatenate(
                [block[:, q * SLOTS : (q + 1) * SLOTS] for block in blocks], axis=1
            )
    top = field_ref[LEAD : LEAD + EXT * PITCH, :] * slope_lanes(
        slopes_ref, LAYERS - 1, LEAD, EXT * PITCH
    )
    field_ref[LEAD : LEAD + EXT * PITCH, :] = top.astype(BF16).astype(F32)
    for layer in range(LAYERS - 1, -1, -1):
        first = LAYERS - layer
        count = EXT - 2 * first
        total = convolve(field_ref, shifted_ref, weights_ref, layer, first, count)
        start = LEAD + first * PITCH
        if layer > 0:
            total = total * slope_lanes(slopes_ref, layer - 1, start, count * PITCH)
            total = total.astype(BF16).astype(F32)
        field_ref[start : start + count * PITCH, :] = total
    for row in range(ROWS):
        u_ref[row] = field_ref[pl.ds(LEAD + (HALO + row) * PITCH + HALO, COLS), :]
    rows_ref[...] = jnp.zeros(rows_ref.shape, F32)
    for right in range(2):
        for half in range(2):
            totals = [None] * 12
            for row in range(ROWS):
                doubled = twice(tile_of(q_ref, p_ref, u_ref, row, 10 + right), half)
                for left in range(12):
                    product = tile_of(q_ref, p_ref, u_ref, row, left) * doubled
                    totals[left] = product if totals[left] is None else totals[left] + product
            for left in range(12):
                at = 20 + 2 * right + half
                rows_ref[left, at : at + 1, :] = jnp.sum(totals[left], axis=0, keepdims=True)
    gram = known_ref[...] + gram_rows([(index, 128) for index in range(12)], rows_ref)
    wide = jnp.concatenate([gram, jnp.zeros((24, 128 - 24), F32)], axis=1)
    sums_ref[...] = (
        wide[0:8]
        + pltpu.roll(wide[8:16], SLOTS, axis=1)
        + pltpu.roll(wide[16:24], 2 * SLOTS, axis=1)
    )


def finish_kernel(sums_ref, q_ref, p_ref, u_ref, next_ref, diag_ref, stored_ref, factor_ref):
    total = sums_ref[0]
    for index in range(1, sums_ref.shape[0]):
        total = total + sums_ref[index]
    total = total * (1.0 / (NLAT * NLON * CH))
    narrow = lane_ids((8, 128)) < SLOTS
    blocks = [
        jnp.where(narrow, total if k == 0 else pltpu.roll(total, 128 - SLOTS * k, axis=1), 0.0)
        for k in range(3)
    ]
    square = (128, 128)
    half = jnp.concatenate(blocks + [jnp.zeros((104, 128), F32)], axis=0)
    row, lane = row_ids(square), lane_ids(square)
    gram = jnp.where(row <= lane, half, jnp.transpose(half))
    known = VECS + STORED
    image = pltpu.roll(gram, 128 - known, axis=1)
    keep = lane < VECS
    coef = jnp.where(
        keep & (row < known), -image, jnp.where(keep & (row == lane + known), 1.0, 0.0)
    )
    diag_ref[...] = image[0:VECS, 0:VECS]
    stored_ref[...] = image[VECS:known, 0:VECS]
    applied = jnp.dot(gram, coef, precision=HIGHEST, preferred_element_type=F32)
    small = lax.dot_general(
        coef, applied, (((0,), (0,)), ((), ())), precision=HIGHEST, preferred_element_type=F32
    )
    entry = [[small[i : i + 1, j : j + 1] for j in range(VECS)] for i in range(VECS)]
    factor = [[None] * VECS for _ in range(VECS)]
    for i in range(VECS):
        value = entry[i][i]
        for k in range(i):
            value = value - factor[k][i] * factor[k][i]
        factor[i][i] = jnp.sqrt(value)
        for j in range(i + 1, VECS):
            value = entry[i][j]
            for k in range(i):
                value = value - factor[k][i] * factor[k][j]
            factor[i][j] = value / factor[i][i]
    inverse = [[None] * VECS for _ in range(VECS)]
    for j in range(VECS):
        inverse[j][j] = 1.0 / factor[j][j]
        for i in range(j - 1, -1, -1):
            value = None
            for k in range(i + 1, j + 1):
                term = factor[i][k] * inverse[k][j]
                value = term if value is None else value + term
            inverse[i][j] = -value / factor[i][i]
    upper = jnp.zeros(square, F32)
    solved = jnp.zeros(square, F32)
    for i in range(VECS):
        for j in range(i, VECS):
            here = (row == i) & (lane == j)
            upper = jnp.where(here, factor[i][j], upper)
            solved = jnp.where(here, inverse[i][j], solved)
    factor_ref[...] = upper[0:VECS, 0:VECS]
    mixed = jnp.dot(coef, solved, precision=HIGHEST, preferred_element_type=F32)
    low = lane_ids((1, 128)) < 64
    straight, crossed = [], []
    for out in range(2):
        choose = (row == 2 * out + lane // 64).astype(F32)
        lines = jnp.dot(mixed, choose, precision=HIGHEST, preferred_element_type=F32)
        straight.append([])
        crossed.append([])
        for index in range(12):
            a = lines[2 * index : 2 * index + 1]
            b = lines[2 * index + 1 : 2 * index + 2]
            straight[out].append(jnp.where(low, a, b))
            crossed[out].append(jnp.where(low, b, a))
    for at in range(ROWS):
        result = [None, None]
        for index in range(12):
            tile = tile_of(q_ref, p_ref, u_ref, at, index)
            other = pltpu.roll(tile, 64, axis=1)
            for out in range(2):
                part = tile * straight[out][index] + other * crossed[out][index]
                result[out] = part if result[out] is None else result[out] + part
        for out in range(2):
            next_ref[at, :, out * 128 : (out + 1) * 128] = result[out]


def call(kernel, outs, scratch=(), name=None):
    many = isinstance(outs, (list, tuple))
    return pl.pallas_call(
        kernel,
        out_shape=outs,
        out_specs=[VMEM] * len(outs) if many else VMEM,
        scratch_shapes=list(scratch),
        name=name,
    )


def shape(dims, kind):
    return jax.ShapeDtypeStruct(dims, kind)


def per_device(ahead_table, back_table, state_block, stored_fields, slope_fields, kernels, gains):
    lat_count, lon_count = lax.axis_size("lat"), lax.axis_size("lon")
    down = [(i, i + 1) for i in range(lat_count - 1)]
    up = [(i + 1, i) for i in range(lat_count - 1)]
    west = [((i + 1) % lon_count, i) for i in range(lon_count)]
    east = [(i, (i + 1) % lon_count) for i in range(lon_count)]
    width = LANES + LAYERS * CH

    south, north = call(edges_kernel, [shape((HALO, COLS, width), BF16)] * 2, name="edges")(
        state_block, slope_fields
    )
    above = lax.ppermute(south, "lat", down)
    below = lax.ppermute(north, "lat", up)
    first, last = call(
        sides_kernel, [shape((EXT, 8, width), BF16), shape((EXT, 8, LAYERS * CH), BF16)], name="sides"
    )(state_block, slope_fields, above, below)
    right = lax.ppermute(first, "lon", west)
    left = lax.ppermute(last, "lon", east)

    taps = kernels.reshape(LAYERS * 9, CH, CH)
    turned = jnp.transpose(kernels[:, ::-1], (0, 1, 3, 2)).reshape(LAYERS * 9, CH, CH)
    ahead_weights, back_weights = call(
        weights_kernel, [shape((LAYERS * 9, LANES, LANES), BF16)] * 2, name="weights"
    )(taps, turned)
    ahead_weights = ahead_weights.reshape(LAYERS * 3, 3 * LANES, LANES)
    back_weights = back_weights.reshape(LAYERS * 3, 3 * LANES, LANES)

    place = lax.axis_index("lon")
    row_index = lax.axis_index("lat") * ROWS + place // 8
    area = jnp.cos(jnp.pi * ((row_index.astype(F32) + 0.5) / NLAT - 0.5))
    wave = jnp.arange(768)
    wave_weight = jnp.where((wave == 0) | (wave == NLON // 2), 1.0 / NLON, 2.0 / NLON)
    wave_weight = jnp.where(wave < WAVES, wave_weight, 0.0).astype(F32)
    columns = jnp.pad(gains, ((0, 0), (0, 768 - WAVES))).T * wave_weight[:, None]
    chosen = jnp.where(place % 2 == 0, columns[:, 0:SLOTS], columns[:, SLOTS : 2 * SLOTS])
    chosen = chosen * (area * area)
    weight = jnp.concatenate([chosen] * 4, axis=1)

    known = call(
        stored_kernel, shape((24, 24), F32), [pltpu.VMEM((10, 24, 128), F32)], name="known"
    )(state_block, stored_fields)

    work = [
        pltpu.VMEM((FLAT, LANES), F32),
        pltpu.VMEM((FLAT, LANES), F32),
        pltpu.VMEM((EXT * PITCH, 3 * LANES), BF16),
    ]
    packed = call(forward_kernel, shape((32, 16, 128), BF16), work, name="forward")(
        state_block, slope_fields, above, below, right, ahead_weights
    )
    circles = lax.all_to_all(packed, "lon", 0, 0, tiled=True)
    filtered = call(
        filter_kernel, shape((32, 16, 128), BF16), [pltpu.VMEM((768, 128), BF16)], name="spectral"
    )(circles, ahead_table, back_table, weight)
    got = lax.all_to_all(filtered, "lon", 0, 0, tiled=True)
    gabove = lax.ppermute(got[8:32], "lat", down)
    gbelow = lax.ppermute(got[0:24], "lat", up)
    image, sums = call(
        adjoint_kernel,
        [shape((ROWS, COLS, LANES), F32), shape((8, 128), F32)],
        work + [pltpu.VMEM((12, 24, 128), F32)],
        name="adjoint",
    )(
        state_block,
        stored_fields,
        slope_fields,
        above,
        below,
        right,
        left,
        got,
        gabove,
        gbelow,
        back_weights,
        known,
    )
    spread = lax.all_to_all(
        jnp.broadcast_to(sums, (lat_count, 8, 128)), "lat", 0, 0, tiled=True
    )
    partial = spread.sum(0)
    spread = lax.all_to_all(
        jnp.broadcast_to(partial, (lon_count, 8, 128)), "lon", 0, 0, tiled=True
    )
    return call(
        finish_kernel,
        [
            shape((ROWS, COLS, LANES), F32),
            shape((VECS, VECS), F32),
            shape((STORED, VECS), F32),
            shape((VECS, VECS), F32),
        ],
        name="finish",
    )(spread, state_block, stored_fields, image)


def solution(mesh):
    ahead, back = tables()
    return jax.shard_map(
        functools.partial(per_device, jnp.asarray(ahead), jnp.asarray(back)),
        mesh=mesh,
        in_specs=(P("lat", "lon", None), P("lat", "lon", None), P("lat", "lon", None), P(), P()),
        out_specs=(P("lat", "lon", None), P(), P(), P()),
        check_vma=False,
    )
```

```python
import functools

import jax
import jax.numpy as jnp
import numpy as np
from jax import lax
from jax.experimental import pallas as pl
from jax.experimental.pallas import tpu as pltpu
from jax.sharding import PartitionSpec as P

F32 = jnp.float32
BF16 = jnp.bfloat16
HIGHEST = lax.Precision.HIGHEST

ROWS, COLS, CH, VECS, STORED, LAYERS = 4, 45, 64, 4, 16, 3
NLAT, NLON, WAVES = 64, 1440, 721
LANES = VECS * CH
HALO = 3
EXT = ROWS + 2 * HALO
PITCH = 64
LEAD = 8
SIDE = 8
FLAT = LEAD + EXT * PITCH + 8
SLOTS = 32
FIELDS = VECS + STORED + VECS
VMEM = pl.BlockSpec(memory_space=pltpu.VMEM)


def lane_ids(shape):
    return lax.broadcasted_iota(jnp.int32, shape, len(shape) - 1)


def row_ids(shape):
    return lax.broadcasted_iota(jnp.int32, shape, len(shape) - 2)


def tables():
    wave = 4 * np.arange(192)[None, :] + np.arange(4)[:, None]
    live = wave < WAVES
    q, t, j = np.meshgrid(np.arange(3), np.arange(8), np.arange(16), indexing="ij")
    slot = (16 * q + j).reshape(-1)
    point = (45 * t).reshape(-1) - 3 + slot
    angle = 2 * np.pi * ((wave[:, :, None] * point) % NLON) / NLON
    keep = live[:, :, None] & (slot < COLS)
    ahead = np.concatenate([np.cos(angle) * keep, np.sin(angle) * keep], axis=2)
    q, t, j = np.meshgrid(np.arange(4), np.arange(8), np.arange(16), indexing="ij")
    slot = (16 * q + j).reshape(-1)
    point = (45 * t).reshape(-1) - SIDE + slot
    angle = 2 * np.pi * ((wave[:, None, :] * point[None, :, None]) % NLON) / NLON
    held = (slot >= SIDE - HALO) & (slot < SIDE + COLS + HALO)
    keep = live[:, None, :] & held[None, :, None]
    back = np.concatenate([np.cos(angle) * keep, np.sin(angle) * keep], axis=2)
    return ahead.astype(jnp.bfloat16), back.astype(jnp.bfloat16)


def line_of(x_ref, above_ref, below_ref, row):
    if row < HALO:
        return above_ref[row + ROWS - HALO].astype(F32)
    if row < HALO + ROWS:
        return x_ref[row - HALO].astype(F32)
    return below_ref[row - HALO - ROWS].astype(F32)


def sides_kernel(x_ref, above_ref, below_ref, last_ref, first_ref):
    for row in range(EXT):
        line = line_of(x_ref, above_ref, below_ref, row)
        last_ref[row] = line[COLS - SIDE : COLS].astype(BF16)
        first_ref[row] = line[0:SIDE, LANES:].astype(BF16)


def weights_kernel(taps_ref, after_ref, ahead_ref, back_ref):
    none = jnp.zeros((CH, CH), F32)
    for layer in range(LAYERS):
        for up in range(3):
            for side in range(3):
                block = taps_ref[9 * layer + 3 * up + side].astype(F32)
                pair = jnp.concatenate(
                    [
                        jnp.concatenate([block, none], axis=1),
                        jnp.concatenate([none, block], axis=1),
                    ],
                    axis=0,
                ).astype(BF16)
                ahead_ref[3 * layer + up, 128 * side : 128 * side + 128, :] = pair
                back_ref[3 * layer + 2 - up, :, 256 - 128 * side : 384 - 128 * side] = pair


def slope_lanes(slopes_ref, layer, start, count):
    pair = slopes_ref[pl.ds(start, count), (layer // 2) * 128 : (layer // 2) * 128 + 128]
    other = pltpu.roll(pair, 64, axis=1)
    low = lane_ids(pair.shape) < 64
    both = jnp.where(low, pair, other) if layer % 2 == 0 else jnp.where(low, other, pair)
    return jnp.concatenate([both, both], axis=1)


def convolve(field_ref, shifted_ref, weights_ref, layer, first, count, turned):
    have = (count + 2) * PITCH
    start = LEAD + (first - 1) * PITCH
    for pair in range(2):
        for step in range(3):
            at = 384 * pair + 128 * step
            shifted_ref[0:have, at : at + 128] = field_ref[
                pl.ds(start + step - 1, have), 128 * pair : 128 * pair + 128
            ].astype(BF16)
    halves = []
    for pair in range(2):
        total = None
        for step in range(3):
            part = lax.dot_general(
                shifted_ref[step * PITCH : (step + count) * PITCH, 384 * pair : 384 * pair + 384],
                weights_ref[layer * 3 + step],
                (((1,), (1 if turned else 0,)), ((), ())),
                preferred_element_type=F32,
            )
            total = part if total is None else total + part
        halves.append(total)
    return jnp.concatenate(halves, axis=1)


def forward_kernel(
    x_ref, above_ref, below_ref, left_ref, weights_ref, send_ref, field_ref, slopes_ref, shifted_ref
):
    field_ref[...] = jnp.zeros((FLAT, LANES), F32)
    slopes_ref[...] = jnp.zeros((FLAT, LANES), F32)
    for row in range(EXT):
        at = LEAD + row * PITCH
        line = line_of(x_ref, above_ref, below_ref, row)
        side = left_ref[row].astype(F32)
        field_ref[at : at + SIDE, :] = side[:, 0:LANES]
        field_ref[at + SIDE : at + SIDE + COLS, :] = line[:, 0:LANES]
        slopes_ref[at : at + SIDE, 0:192] = side[:, LANES:]
        slopes_ref[at + SIDE : at + SIDE + COLS, 0:192] = line[:, LANES:]
    for layer in range(LAYERS):
        first = layer + 1
        count = EXT - 2 * first
        total = convolve(field_ref, shifted_ref, weights_ref, layer, first, count, False)
        start = LEAD + first * PITCH
        total = total * slope_lanes(slopes_ref, layer, start, count * PITCH)
        field_ref[start : start + count * PITCH, :] = total.astype(BF16).astype(F32)
    for row in range(ROWS):
        line = field_ref[pl.ds(LEAD + (HALO + row) * PITCH + SIDE - HALO, 48), :]
        for group in range(8):
            pieces = [
                line[16 * q : 16 * q + 16, group * SLOTS : (group + 1) * SLOTS] for q in range(3)
            ]
            pieces.append(jnp.zeros((16, SLOTS), F32))
            send_ref[row * 8 + group] = jnp.concatenate(pieces, axis=1).astype(BF16)


def filter_kernel(
    got_ref, ahead_ref, back_ref, gains_ref, known_ref, right_ref, send_ref, work_ref
):
    quarter = [
        got_ref[8 * part : 8 * part + 8].astype(F32).reshape(128, 128) for part in range(4)
    ]
    even, odd = quarter[0] + quarter[2], quarter[1] + quarter[3]
    across, along = quarter[0] - quarter[2], quarter[1] - quarter[3]
    real = [even + odd, across, even - odd, across]
    imag = [None, -along, None, along]
    low = lane_ids((128, 128)) < SLOTS

    def turn(value, shift):
        return value if shift % 128 == 0 else pltpu.roll(value, shift % 128, axis=1)

    for kind in range(4):
        for q in range(3):
            a = real[kind]
            b = imag[kind]
            left, right = turn(a, -SLOTS * q), turn(a, SLOTS - SLOTS * q)
            if b is None:
                top = jnp.where(low, left, 0.0)
                bottom = jnp.where(low, 0.0, -right)
            else:
                top = jnp.where(low, left, turn(b, SLOTS - SLOTS * q))
                bottom = jnp.where(low, turn(b, -SLOTS * q), -right)
            work_ref[128 * q : 128 * q + 128, :] = top.astype(BF16)
            work_ref[384 + 128 * q : 512 + 128 * q, :] = bottom.astype(BF16)
        spectrum = jnp.dot(ahead_ref[kind], work_ref[...], preferred_element_type=F32)
        weight = gains_ref[pl.ds(kind, 192, stride=4), :]
        spectrum = spectrum * weight
        below = jnp.where(
            lane_ids((192, 128)) < SLOTS, -turn(spectrum, -SLOTS), turn(spectrum, SLOTS)
        )
        packed = jnp.concatenate([spectrum, below], axis=0).astype(BF16)
        part = jnp.dot(back_ref[kind], packed, preferred_element_type=F32)
        if kind == 0:
            zero = part
        elif kind == 1:
            one = part
        elif kind == 2:
            two = part
        else:
            three = part
    plus, minus = zero + two, zero - two
    swing = one + three
    turned = turn(three - one, -SLOTS)
    result = [plus + swing, minus + turned, plus - swing, minus - turned]
    lane = lane_ids((128, 128))
    for part in range(4):
        packed = result[part][0:128]
        for q in range(1, 4):
            packed = jnp.where(
                lane >= SLOTS * q, turn(result[part][128 * q : 128 * q + 128], SLOTS * q), packed
            )
        send_ref[8 * part : 8 * part + 8] = packed.reshape(8, 16, 128).astype(BF16)


def twice(tile, half):
    other = pltpu.roll(tile, 64, axis=1)
    low = lane_ids(tile.shape) < 64
    return jnp.where(low, tile, other) if half == 0 else jnp.where(low, other, tile)


def gram_rows(first, rows_ref):
    total = None
    for index, count in first:
        shape = (24, 128)
        pick = (row_ids(shape) == 2 * index + (lane_ids(shape) // 64)).astype(F32)
        rows = rows_ref[index]
        part = lax.dot_general(
            pick, rows, (((1,), (1,)), ((), ())), precision=HIGHEST, preferred_element_type=F32
        )
        total = part if total is None else total + part
    return total


def stored_kernel(q_ref, p_ref, after_ref, out_ref, rows_ref):
    rows_ref[...] = jnp.zeros(rows_ref.shape, F32)
    known = 10
    for right in range(known):
        for half in range(2):
            totals = [None] * (right + 1)
            for row in range(ROWS):
                tile = tile_of(q_ref, p_ref, None, row, right)
                doubled = twice(tile, half)
                for left in range(right + 1):
                    product = tile_of(q_ref, p_ref, None, row, left) * doubled
                    totals[left] = product if totals[left] is None else totals[left] + product
            for left in range(right + 1):
                rows_ref[left, 2 * right + half : 2 * right + half + 1, :] = jnp.sum(
                    totals[left], axis=0, keepdims=True
                )
    out_ref[...] = gram_rows([(index, 128) for index in range(known)], rows_ref)


def tile_of(q_ref, p_ref, u_ref, row, index):
    if index < 2:
        return q_ref[:, row, index * 128 : (index + 1) * 128]
    if index < 10:
        return p_ref[row, :, (index - 2) * 128 : (index - 1) * 128].astype(F32)
    return u_ref[row, :, (index - 10) * 128 : (index - 9) * 128]


def adjoint_kernel(
    q_ref,
    p_ref,
    x_ref,
    above_ref,
    below_ref,
    left_ref,
    right_ref,
    got_ref,
    gabove_ref,
    gbelow_ref,
    weights_ref,
    known_ref,
    u_ref,
    sums_ref,
    field_ref,
    slopes_ref,
    shifted_ref,
    rows_ref,
):
    field_ref[0:LEAD, :] = jnp.zeros((LEAD, LANES), F32)
    field_ref[FLAT - 8 : FLAT, :] = jnp.zeros((8, LANES), F32)
    slopes_ref[...] = jnp.zeros((FLAT, LANES), F32)
    for row in range(EXT):
        at = LEAD + row * PITCH
        line = line_of(x_ref, above_ref, below_ref, row)
        slopes_ref[at : at + SIDE, 0:192] = left_ref[row, :, LANES:].astype(F32)
        slopes_ref[at + SIDE : at + SIDE + COLS, 0:192] = line[:, LANES:]
        slopes_ref[at + SIDE + COLS : at + SIDE + COLS + 8, 0:192] = right_ref[row].astype(F32)
    for row in range(EXT):
        at = LEAD + row * PITCH
        if row < HALO:
            source, base = gabove_ref, row * 8
        elif row < HALO + ROWS:
            source, base = got_ref, (row - HALO) * 8
        else:
            source, base = gbelow_ref, (row - HALO - ROWS) * 8
        blocks = [source[base + group].astype(F32) for group in range(8)]
        for q in range(4):
            field_ref[at + 16 * q : at + 16 * q + 16, :] = jnp.concatenate(
                [block[:, q * SLOTS : (q + 1) * SLOTS] for block in blocks], axis=1
            )
    top = field_ref[LEAD : LEAD + EXT * PITCH, :] * slope_lanes(
        slopes_ref, LAYERS - 1, LEAD, EXT * PITCH
    )
    field_ref[LEAD : LEAD + EXT * PITCH, :] = top.astype(BF16).astype(F32)
    for layer in range(LAYERS - 1, -1, -1):
        first = LAYERS - layer
        count = EXT - 2 * first
        total = convolve(field_ref, shifted_ref, weights_ref, layer, first, count, True)
        start = LEAD + first * PITCH
        if layer > 0:
            total = total * slope_lanes(slopes_ref, layer - 1, start, count * PITCH)
            total = total.astype(BF16).astype(F32)
        field_ref[start : start + count * PITCH, :] = total
    for row in range(ROWS):
        u_ref[row] = field_ref[pl.ds(LEAD + (HALO + row) * PITCH + SIDE, COLS), :]
    rows_ref[...] = jnp.zeros(rows_ref.shape, F32)
    for right in range(2):
        for half in range(2):
            totals = [None] * 12
            for row in range(ROWS):
                doubled = twice(tile_of(q_ref, p_ref, u_ref, row, 10 + right), half)
                for left in range(12):
                    product = tile_of(q_ref, p_ref, u_ref, row, left) * doubled
                    totals[left] = product if totals[left] is None else totals[left] + product
            for left in range(12):
                at = 20 + 2 * right + half
                rows_ref[left, at : at + 1, :] = jnp.sum(totals[left], axis=0, keepdims=True)
    gram = known_ref[...] + gram_rows([(index, 128) for index in range(12)], rows_ref)
    wide = jnp.concatenate([gram, jnp.zeros((24, 128 - 24), F32)], axis=1)
    sums_ref[...] = (
        wide[0:8]
        + pltpu.roll(wide[8:16], SLOTS, axis=1)
        + pltpu.roll(wide[16:24], 2 * SLOTS, axis=1)
    )


def finish_kernel(sums_ref, q_ref, p_ref, u_ref, next_ref, diag_ref, stored_ref, factor_ref):
    total = sums_ref[0]
    for index in range(1, sums_ref.shape[0]):
        total = total + sums_ref[index]
    total = total * (1.0 / (NLAT * NLON * CH))
    narrow = lane_ids((8, 128)) < SLOTS
    blocks = [
        jnp.where(narrow, total if k == 0 else pltpu.roll(total, 128 - SLOTS * k, axis=1), 0.0)
        for k in range(3)
    ]
    square = (128, 128)
    half = jnp.concatenate(blocks + [jnp.zeros((104, 128), F32)], axis=0)
    row, lane = row_ids(square), lane_ids(square)
    gram = jnp.where(row <= lane, half, jnp.transpose(half))
    known = VECS + STORED
    image = pltpu.roll(gram, 128 - known, axis=1)
    keep = lane < VECS
    coef = jnp.where(
        keep & (row < known), -image, jnp.where(keep & (row == lane + known), 1.0, 0.0)
    )
    diag_ref[...] = image[0:VECS, 0:VECS]
    stored_ref[...] = jnp.transpose(image)[0:VECS, VECS:known]
    applied = jnp.dot(gram, coef, precision=HIGHEST, preferred_element_type=F32)
    small = lax.dot_general(
        coef, applied, (((0,), (0,)), ((), ())), precision=HIGHEST, preferred_element_type=F32
    )
    entry = [[small[i : i + 1, j : j + 1] for j in range(VECS)] for i in range(VECS)]
    factor = [[None] * VECS for _ in range(VECS)]
    for i in range(VECS):
        value = entry[i][i]
        for k in range(i):
            value = value - factor[k][i] * factor[k][i]
        factor[i][i] = jnp.sqrt(value)
        for j in range(i + 1, VECS):
            value = entry[i][j]
            for k in range(i):
                value = value - factor[k][i] * factor[k][j]
            factor[i][j] = value / factor[i][i]
    inverse = [[None] * VECS for _ in range(VECS)]
    for j in range(VECS):
        inverse[j][j] = 1.0 / factor[j][j]
        for i in range(j - 1, -1, -1):
            value = None
            for k in range(i + 1, j + 1):
                term = factor[i][k] * inverse[k][j]
                value = term if value is None else value + term
            inverse[i][j] = -value / factor[i][i]
    upper = jnp.zeros(square, F32)
    solved = jnp.zeros(square, F32)
    for i in range(VECS):
        for j in range(i, VECS):
            here = (row == i) & (lane == j)
            upper = jnp.where(here, factor[i][j], upper)
            solved = jnp.where(here, inverse[i][j], solved)
    factor_ref[...] = upper[0:VECS, 0:VECS]
    mixed = jnp.dot(coef, solved, precision=HIGHEST, preferred_element_type=F32)
    low = lane_ids((1, 128)) < 64
    straight, crossed = [], []
    for out in range(2):
        choose = (row == 2 * out + lane // 64).astype(F32)
        lines = jnp.dot(mixed, choose, precision=HIGHEST, preferred_element_type=F32)
        straight.append([])
        crossed.append([])
        for index in range(12):
            a = lines[2 * index : 2 * index + 1]
            b = lines[2 * index + 1 : 2 * index + 2]
            straight[out].append(jnp.where(low, a, b))
            crossed[out].append(jnp.where(low, b, a))
    for at in range(ROWS):
        result = [None, None]
        for index in range(12):
            tile = tile_of(q_ref, p_ref, u_ref, at, index)
            other = pltpu.roll(tile, 64, axis=1)
            for out in range(2):
                part = tile * straight[out][index] + other * crossed[out][index]
                result[out] = part if result[out] is None else result[out] + part
        for out in range(2):
            next_ref[:, at, out * 128 : (out + 1) * 128] = result[out]


def call(kernel, outs, scratch=(), name=None, final=False, far=()):
    kinds = [shape(o.shape, o.dtype) if final else pltpu.VMEM(o.shape, o.dtype) for o in outs]

    def run(*args):
        placed = [
            a if k in far else pltpu.with_memory_space_constraint(a, pltpu.VMEM)
            for k, a in enumerate(args)
        ]
        return pl.pallas_call(
            kernel,
            out_shape=kinds,
            in_specs=[pl.BlockSpec() if k in far else VMEM for k in range(len(args))],
            out_specs=[VMEM] * len(outs),
            scratch_shapes=list(scratch),
            name=name,
        )(*placed)

    return run


def shape(dims, kind):
    return jax.ShapeDtypeStruct(dims, kind)


def per_device(ahead_table, back_table, state_block, stored_fields, slope_fields, kernels, gains):
    lat_count, lon_count = lax.axis_size("lat"), lax.axis_size("lon")
    down = [(i, i + 1) for i in range(lat_count - 1)]
    up = [(i + 1, i) for i in range(lat_count - 1)]
    west = [((i + 1) % lon_count, i) for i in range(lon_count)]
    east = [(i, (i + 1) % lon_count) for i in range(lon_count)]
    width = LANES + LAYERS * CH

    both = jnp.concatenate([state_block.astype(BF16), slope_fields], axis=2)
    native = jnp.transpose(state_block, (1, 0, 2))
    above = lax.ppermute(both, "lat", down)
    below = lax.ppermute(both, "lat", up)
    last, first = call(
        sides_kernel,
        [shape((EXT, SIDE, width), BF16), shape((EXT, SIDE, LAYERS * CH), BF16)],
        name="sides",
    )(both, above, below)
    left = lax.ppermute(last, "lon", east)
    ahead_weights, back_weights = call(
        weights_kernel,
        [
            shape((LAYERS * 3, 3 * 128, 128), BF16),
            shape((LAYERS * 3, 128, 3 * 128), BF16),
        ],
        name="weights",
    )(kernels.reshape(LAYERS * 9, CH, CH), last)

    place = lax.axis_index("lon")
    row_index = lax.axis_index("lat") * ROWS + place // 8
    area = jnp.cos(jnp.pi * ((row_index.astype(F32) + 0.5) / NLAT - 0.5))
    wave = jnp.arange(768)
    wave_weight = jnp.where((wave == 0) | (wave == NLON // 2), 1.0 / NLON, 2.0 / NLON)
    wave_weight = jnp.where(wave < WAVES, wave_weight, 0.0).astype(F32)
    columns = jnp.pad(gains, ((0, 0), (0, 768 - WAVES))).T * wave_weight[:, None]
    chosen = jnp.where(place % 2 == 0, columns[:, 0:SLOTS], columns[:, SLOTS : 2 * SLOTS])
    chosen = chosen * (area * area)
    weight = jnp.concatenate([chosen] * 4, axis=1)

    work = [
        pltpu.VMEM((FLAT, LANES), F32),
        pltpu.VMEM((FLAT, LANES), F32),
        pltpu.VMEM((EXT * PITCH, 3 * LANES), BF16),
    ]
    (packed,) = call(forward_kernel, [shape((32, 16, 128), BF16)], work, name="forward")(
        both, above, below, left, ahead_weights
    )
    circles = lax.all_to_all(packed, "lon", 0, 0, tiled=True)
    first, _ = lax.optimization_barrier((first, packed))
    right = lax.ppermute(first, "lon", west)
    (known,) = call(
        stored_kernel, [shape((24, 24), F32)], [pltpu.VMEM((10, 24, 128), F32)], name="known"
    )(native, stored_fields, packed)
    (filtered,) = call(
        filter_kernel, [shape((32, 16, 128), BF16)], [pltpu.VMEM((768, 128), BF16)], name="spectral", far=(0, 1, 2)
    )(circles, ahead_table, back_table, weight, known, right)
    got = lax.all_to_all(filtered, "lon", 0, 0, tiled=True)
    gabove = lax.ppermute(got[8:32], "lat", down)
    gbelow = lax.ppermute(got[0:24], "lat", up)
    image, sums = call(
        adjoint_kernel,
        [shape((ROWS, COLS, LANES), F32), shape((8, 128), F32)],
        work + [pltpu.VMEM((12, 24, 128), F32)],
        name="adjoint",
        far=(0, 1, 2, 3, 4, 5, 10),
    )(
        native,
        stored_fields,
        both,
        above,
        below,
        left,
        right,
        got,
        gabove,
        gbelow,
        back_weights,
        known,
    )
    spread = lax.all_to_all(
        jnp.broadcast_to(sums, (lat_count, 8, 128)), "lat", 0, 0, tiled=True
    )
    partial = spread.sum(0)
    spread = lax.all_to_all(
        jnp.broadcast_to(partial, (lon_count, 8, 128)), "lon", 0, 0, tiled=True
    )
    following, diag, stored, factor = call(
        finish_kernel,
        [
            shape((COLS, ROWS, LANES), F32),
            shape((VECS, VECS), F32),
            shape((VECS, STORED), F32),
            shape((VECS, VECS), F32),
        ],
        name="finish",
        final=True,
    )(spread, native, stored_fields, image)
    return jnp.transpose(following, (1, 0, 2)), diag, stored.T, factor


def solution(mesh):
    ahead, back = tables()
    return jax.shard_map(
        functools.partial(per_device, jnp.asarray(ahead), jnp.asarray(back)),
        mesh=mesh,
        in_specs=(P("lat", "lon", None), P("lat", "lon", None), P("lat", "lon", None), P(), P()),
        out_specs=(P("lat", "lon", None), P(), P(), P()),
        check_vma=False,
    )
```

```python
import functools

import jax
import jax.numpy as jnp
import numpy as np
from jax import lax
from jax.experimental import pallas as pl
from jax.experimental.pallas import tpu as pltpu
from jax.sharding import PartitionSpec as P

F32 = jnp.float32
BF16 = jnp.bfloat16
HIGHEST = lax.Precision.HIGHEST

ROWS, COLS, CH, VECS, STORED, LAYERS = 4, 45, 64, 4, 16, 3
NLAT, NLON, WAVES = 64, 1440, 721
LANES = VECS * CH
HALO = 3
EXT = ROWS + 2 * HALO
PITCH = 64
LEAD = 8
SIDE = 8
FLAT = LEAD + EXT * PITCH + 8
SLOTS = 32
FIELDS = VECS + STORED + VECS
VMEM = pl.BlockSpec(memory_space=pltpu.VMEM)


def lane_ids(shape):
    return lax.broadcasted_iota(jnp.int32, shape, len(shape) - 1)


def row_ids(shape):
    return lax.broadcasted_iota(jnp.int32, shape, len(shape) - 2)


def tables():
    wave = 4 * np.arange(192)[None, :] + np.arange(4)[:, None]
    live = wave < WAVES
    q, t, j = np.meshgrid(np.arange(3), np.arange(8), np.arange(16), indexing="ij")
    slot = (16 * q + j).reshape(-1)
    point = (45 * t).reshape(-1) - 3 + slot
    angle = 2 * np.pi * ((wave[:, :, None] * point) % NLON) / NLON
    keep = live[:, :, None] & (slot < COLS)
    ahead = np.concatenate([np.cos(angle) * keep, np.sin(angle) * keep], axis=2)
    q, t, j = np.meshgrid(np.arange(4), np.arange(8), np.arange(16), indexing="ij")
    slot = (16 * q + j).reshape(-1)
    point = (45 * t).reshape(-1) - SIDE + slot
    angle = 2 * np.pi * ((wave[:, None, :] * point[None, :, None]) % NLON) / NLON
    held = (slot >= SIDE - HALO) & (slot < SIDE + COLS + HALO)
    keep = live[:, None, :] & held[None, :, None]
    back = np.concatenate([np.cos(angle) * keep, np.sin(angle) * keep], axis=2)
    return ahead.astype(jnp.bfloat16), back.astype(jnp.bfloat16)


def line_of(x_ref, above_ref, below_ref, row):
    if row < HALO:
        return above_ref[row + ROWS - HALO].astype(F32)
    if row < HALO + ROWS:
        return x_ref[row - HALO].astype(F32)
    return below_ref[row - HALO - ROWS].astype(F32)


def sides_kernel(x_ref, above_ref, below_ref, last_ref):
    for row in range(EXT):
        line = line_of(x_ref, above_ref, below_ref, row)
        last_ref[row] = line[COLS - SIDE : COLS].astype(BF16)


def weights_kernel(taps_ref, after_ref, ahead_ref, back_ref):
    none = jnp.zeros((CH, CH), F32)
    for layer in range(LAYERS):
        for up in range(3):
            for side in range(3):
                block = taps_ref[9 * layer + 3 * up + side].astype(F32)
                pair = jnp.concatenate(
                    [
                        jnp.concatenate([block, none], axis=1),
                        jnp.concatenate([none, block], axis=1),
                    ],
                    axis=0,
                ).astype(BF16)
                ahead_ref[3 * layer + up, 128 * side : 128 * side + 128, :] = pair
                back_ref[3 * layer + 2 - up, :, 256 - 128 * side : 384 - 128 * side] = pair


def slope_lanes(slopes_ref, layer, start, count):
    pair = slopes_ref[pl.ds(start, count), (layer // 2) * 128 : (layer // 2) * 128 + 128]
    other = pltpu.roll(pair, 64, axis=1)
    low = lane_ids(pair.shape) < 64
    both = jnp.where(low, pair, other) if layer % 2 == 0 else jnp.where(low, other, pair)
    return jnp.concatenate([both, both], axis=1)


def convolve(field_ref, shifted_ref, weights_ref, layer, first, count, turned):
    have = (count + 2) * PITCH
    start = LEAD + (first - 1) * PITCH
    for pair in range(2):
        for step in range(3):
            at = 384 * pair + 128 * step
            shifted_ref[0:have, at : at + 128] = field_ref[
                pl.ds(start + step - 1, have), 128 * pair : 128 * pair + 128
            ].astype(BF16)
    halves = []
    for pair in range(2):
        total = None
        for step in range(3):
            part = lax.dot_general(
                shifted_ref[step * PITCH : (step + count) * PITCH, 384 * pair : 384 * pair + 384],
                weights_ref[layer * 3 + step],
                (((1,), (1 if turned else 0,)), ((), ())),
                preferred_element_type=F32,
            )
            total = part if total is None else total + part
        halves.append(total)
    return jnp.concatenate(halves, axis=1)


def parcel(slopes_ref, index):
    if index >= EXT * LAYERS:
        return jnp.zeros((16, SLOTS), F32)
    row, layer = index // LAYERS, index % LAYERS
    at = LEAD + row * PITCH + SIDE
    block = slopes_ref[at : at + 8, (layer // 2) * 128 : (layer // 2) * 128 + 128]
    base = 64 * (layer % 2)
    return jnp.concatenate(
        [
            jnp.zeros((8, SLOTS), F32),
            block[0:4, base : base + SLOTS],
            block[0:4, base + SLOTS : base + 2 * SLOTS],
        ],
        axis=0,
    )


def forward_kernel(
    x_ref, above_ref, below_ref, left_ref, weights_ref, send_ref, field_ref, slopes_ref, shifted_ref
):
    field_ref[...] = jnp.zeros((FLAT, LANES), F32)
    slopes_ref[...] = jnp.zeros((FLAT, LANES), F32)
    for row in range(EXT):
        at = LEAD + row * PITCH
        line = line_of(x_ref, above_ref, below_ref, row)
        side = left_ref[row].astype(F32)
        field_ref[at : at + SIDE, :] = side[:, 0:LANES]
        field_ref[at + SIDE : at + SIDE + COLS, :] = line[:, 0:LANES]
        slopes_ref[at : at + SIDE, 0:192] = side[:, LANES:]
        slopes_ref[at + SIDE : at + SIDE + COLS, 0:192] = line[:, LANES:]
    for layer in range(LAYERS):
        first = layer + 1
        count = EXT - 2 * first
        total = convolve(field_ref, shifted_ref, weights_ref, layer, first, count, False)
        start = LEAD + first * PITCH
        total = total * slope_lanes(slopes_ref, layer, start, count * PITCH)
        field_ref[start : start + count * PITCH, :] = total.astype(BF16).astype(F32)
    for row in range(ROWS):
        line = field_ref[pl.ds(LEAD + (HALO + row) * PITCH + SIDE - HALO, 48), :]
        for group in range(8):
            pieces = [
                line[16 * q : 16 * q + 16, group * SLOTS : (group + 1) * SLOTS] for q in range(3)
            ]
            pieces.append(parcel(slopes_ref, row * 8 + group))
            send_ref[row * 8 + group] = jnp.concatenate(pieces, axis=1).astype(BF16)


def filter_kernel(
    got_ref, ahead_ref, back_ref, gains_ref, known_ref, send_ref, work_ref
):
    quarter = [
        got_ref[8 * part : 8 * part + 8].astype(F32).reshape(128, 128) for part in range(4)
    ]
    even, odd = quarter[0] + quarter[2], quarter[1] + quarter[3]
    across, along = quarter[0] - quarter[2], quarter[1] - quarter[3]
    real = [even + odd, across, even - odd, across]
    imag = [None, -along, None, along]
    low = lane_ids((128, 128)) < SLOTS

    def turn(value, shift):
        return value if shift % 128 == 0 else pltpu.roll(value, shift % 128, axis=1)

    for kind in range(4):
        for q in range(3):
            a = real[kind]
            b = imag[kind]
            left, right = turn(a, -SLOTS * q), turn(a, SLOTS - SLOTS * q)
            if b is None:
                top = jnp.where(low, left, 0.0)
                bottom = jnp.where(low, 0.0, -right)
            else:
                top = jnp.where(low, left, turn(b, SLOTS - SLOTS * q))
                bottom = jnp.where(low, turn(b, -SLOTS * q), -right)
            work_ref[128 * q : 128 * q + 128, :] = top.astype(BF16)
            work_ref[384 + 128 * q : 512 + 128 * q, :] = bottom.astype(BF16)
        spectrum = jnp.dot(ahead_ref[kind], work_ref[...], preferred_element_type=F32)
        weight = gains_ref[pl.ds(kind, 192, stride=4), :]
        spectrum = spectrum * weight
        below = jnp.where(
            lane_ids((192, 128)) < SLOTS, -turn(spectrum, -SLOTS), turn(spectrum, SLOTS)
        )
        packed = jnp.concatenate([spectrum, below], axis=0).astype(BF16)
        part = jnp.dot(back_ref[kind], packed, preferred_element_type=F32)
        if kind == 0:
            zero = part
        elif kind == 1:
            one = part
        elif kind == 2:
            two = part
        else:
            three = part
    plus, minus = zero + two, zero - two
    swing = one + three
    turned = turn(three - one, -SLOTS)
    result = [plus + swing, minus + turned, plus - swing, minus - turned]
    lane = lane_ids((128, 128))
    for part in range(4):
        packed = result[part][0:128]
        for q in range(1, 4):
            packed = jnp.where(
                lane >= SLOTS * q, turn(result[part][128 * q : 128 * q + 128], SLOTS * q), packed
            )
        if part < 3:
            passing = got_ref[8 * part + 1 : 8 * part + 9]
        else:
            passing = jnp.concatenate([got_ref[25:32], got_ref[0:1]], axis=0)
        carried = (lane >= 96) & (row_ids((128, 128)) % 16 >= 8)
        packed = jnp.where(carried, passing.astype(F32).reshape(128, 128), packed)
        send_ref[8 * part : 8 * part + 8] = packed.reshape(8, 16, 128).astype(BF16)


def twice(tile, half):
    other = pltpu.roll(tile, 64, axis=1)
    low = lane_ids(tile.shape) < 64
    return jnp.where(low, tile, other) if half == 0 else jnp.where(low, other, tile)


def gram_rows(first, rows_ref):
    total = None
    for index, count in first:
        shape = (24, 128)
        pick = (row_ids(shape) == 2 * index + (lane_ids(shape) // 64)).astype(F32)
        rows = rows_ref[index]
        part = lax.dot_general(
            pick, rows, (((1,), (1,)), ((), ())), precision=HIGHEST, preferred_element_type=F32
        )
        total = part if total is None else total + part
    return total


def stored_kernel(q_ref, p_ref, after_ref, out_ref, rows_ref):
    rows_ref[...] = jnp.zeros(rows_ref.shape, F32)
    known = 10
    for right in range(known):
        for half in range(2):
            totals = [None] * (right + 1)
            for row in range(ROWS):
                tile = tile_of(q_ref, p_ref, None, row, right)
                doubled = twice(tile, half)
                for left in range(right + 1):
                    product = tile_of(q_ref, p_ref, None, row, left) * doubled
                    totals[left] = product if totals[left] is None else totals[left] + product
            for left in range(right + 1):
                rows_ref[left, 2 * right + half : 2 * right + half + 1, :] = jnp.sum(
                    totals[left], axis=0, keepdims=True
                )
    out_ref[...] = gram_rows([(index, 128) for index in range(known)], rows_ref)


def tile_of(q_ref, p_ref, u_ref, row, index):
    if index < 2:
        return q_ref[:, row, index * 128 : (index + 1) * 128]
    if index < 10:
        return p_ref[row, :, (index - 2) * 128 : (index - 1) * 128].astype(F32)
    return u_ref[row, :, (index - 10) * 128 : (index - 9) * 128]


def adjoint_kernel(
    q_ref,
    p_ref,
    x_ref,
    above_ref,
    below_ref,
    left_ref,
    got_ref,
    gabove_ref,
    gbelow_ref,
    weights_ref,
    known_ref,
    u_ref,
    sums_ref,
    field_ref,
    slopes_ref,
    shifted_ref,
    rows_ref,
):
    field_ref[0:LEAD, :] = jnp.zeros((LEAD, LANES), F32)
    field_ref[FLAT - 8 : FLAT, :] = jnp.zeros((8, LANES), F32)
    slopes_ref[...] = jnp.zeros((FLAT, LANES), F32)
    for row in range(EXT):
        at = LEAD + row * PITCH
        line = line_of(x_ref, above_ref, below_ref, row)
        slopes_ref[at : at + SIDE, 0:192] = left_ref[row, :, LANES:].astype(F32)
        slopes_ref[at + SIDE : at + SIDE + COLS, 0:192] = line[:, LANES:]
        halves = []
        for layer in range(LAYERS):
            block = got_ref[LAYERS * row + layer].astype(F32)
            halves += [block[8:12, 96:128], block[12:16, 96:128]]
        slopes_ref[at + SIDE + COLS : at + SIDE + COLS + 4, 0:192] = jnp.concatenate(halves, axis=1)
    for row in range(EXT):
        at = LEAD + row * PITCH
        if row < HALO:
            source, base = gabove_ref, row * 8
        elif row < HALO + ROWS:
            source, base = got_ref, (row - HALO) * 8
        else:
            source, base = gbelow_ref, (row - HALO - ROWS) * 8
        blocks = [source[base + group].astype(F32) for group in range(8)]
        for q in range(4):
            field_ref[at + 16 * q : at + 16 * q + 16, :] = jnp.concatenate(
                [block[:, q * SLOTS : (q + 1) * SLOTS] for block in blocks], axis=1
            )
    top = field_ref[LEAD : LEAD + EXT * PITCH, :] * slope_lanes(
        slopes_ref, LAYERS - 1, LEAD, EXT * PITCH
    )
    field_ref[LEAD : LEAD + EXT * PITCH, :] = top.astype(BF16).astype(F32)
    for layer in range(LAYERS - 1, -1, -1):
        first = LAYERS - layer
        count = EXT - 2 * first
        total = convolve(field_ref, shifted_ref, weights_ref, layer, first, count, True)
        start = LEAD + first * PITCH
        if layer > 0:
            total = total * slope_lanes(slopes_ref, layer - 1, start, count * PITCH)
            total = total.astype(BF16).astype(F32)
        field_ref[start : start + count * PITCH, :] = total
    for row in range(ROWS):
        u_ref[row] = field_ref[pl.ds(LEAD + (HALO + row) * PITCH + SIDE, COLS), :]
    rows_ref[...] = jnp.zeros(rows_ref.shape, F32)
    for right in range(2):
        for half in range(2):
            totals = [None] * 12
            for row in range(ROWS):
                doubled = twice(tile_of(q_ref, p_ref, u_ref, row, 10 + right), half)
                for left in range(12):
                    product = tile_of(q_ref, p_ref, u_ref, row, left) * doubled
                    totals[left] = product if totals[left] is None else totals[left] + product
            for left in range(12):
                at = 20 + 2 * right + half
                rows_ref[left, at : at + 1, :] = jnp.sum(totals[left], axis=0, keepdims=True)
    gram = known_ref[...] + gram_rows([(index, 128) for index in range(12)], rows_ref)
    wide = jnp.concatenate([gram, jnp.zeros((24, 128 - 24), F32)], axis=1)
    sums_ref[...] = (
        wide[0:8]
        + pltpu.roll(wide[8:16], SLOTS, axis=1)
        + pltpu.roll(wide[16:24], 2 * SLOTS, axis=1)
    )


def finish_kernel(sums_ref, q_ref, p_ref, u_ref, next_ref, diag_ref, stored_ref, factor_ref):
    total = sums_ref[0]
    for index in range(1, sums_ref.shape[0]):
        total = total + sums_ref[index]
    total = total * (1.0 / (NLAT * NLON * CH))
    narrow = lane_ids((8, 128)) < SLOTS
    blocks = [
        jnp.where(narrow, total if k == 0 else pltpu.roll(total, 128 - SLOTS * k, axis=1), 0.0)
        for k in range(3)
    ]
    square = (128, 128)
    half = jnp.concatenate(blocks + [jnp.zeros((104, 128), F32)], axis=0)
    row, lane = row_ids(square), lane_ids(square)
    gram = jnp.where(row <= lane, half, jnp.transpose(half))
    known = VECS + STORED
    image = pltpu.roll(gram, 128 - known, axis=1)
    keep = lane < VECS
    coef = jnp.where(
        keep & (row < known), -image, jnp.where(keep & (row == lane + known), 1.0, 0.0)
    )
    diag_ref[...] = image[0:VECS, 0:VECS]
    stored_ref[...] = jnp.transpose(image)[0:VECS, VECS:known]
    applied = jnp.dot(gram, coef, precision=HIGHEST, preferred_element_type=F32)
    small = lax.dot_general(
        coef, applied, (((0,), (0,)), ((), ())), precision=HIGHEST, preferred_element_type=F32
    )
    entry = [[small[i : i + 1, j : j + 1] for j in range(VECS)] for i in range(VECS)]
    factor = [[None] * VECS for _ in range(VECS)]
    for i in range(VECS):
        value = entry[i][i]
        for k in range(i):
            value = value - factor[k][i] * factor[k][i]
        factor[i][i] = jnp.sqrt(value)
        for j in range(i + 1, VECS):
            value = entry[i][j]
            for k in range(i):
                value = value - factor[k][i] * factor[k][j]
            factor[i][j] = value / factor[i][i]
    inverse = [[None] * VECS for _ in range(VECS)]
    for j in range(VECS):
        inverse[j][j] = 1.0 / factor[j][j]
        for i in range(j - 1, -1, -1):
            value = None
            for k in range(i + 1, j + 1):
                term = factor[i][k] * inverse[k][j]
                value = term if value is None else value + term
            inverse[i][j] = -value / factor[i][i]
    upper = jnp.zeros(square, F32)
    solved = jnp.zeros(square, F32)
    for i in range(VECS):
        for j in range(i, VECS):
            here = (row == i) & (lane == j)
            upper = jnp.where(here, factor[i][j], upper)
            solved = jnp.where(here, inverse[i][j], solved)
    factor_ref[...] = upper[0:VECS, 0:VECS]
    mixed = jnp.dot(coef, solved, precision=HIGHEST, preferred_element_type=F32)
    low = lane_ids((1, 128)) < 64
    straight, crossed = [], []
    for out in range(2):
        choose = (row == 2 * out + lane // 64).astype(F32)
        lines = jnp.dot(mixed, choose, precision=HIGHEST, preferred_element_type=F32)
        straight.append([])
        crossed.append([])
        for index in range(12):
            a = lines[2 * index : 2 * index + 1]
            b = lines[2 * index + 1 : 2 * index + 2]
            straight[out].append(jnp.where(low, a, b))
            crossed[out].append(jnp.where(low, b, a))
    for at in range(ROWS):
        result = [None, None]
        for index in range(12):
            tile = tile_of(q_ref, p_ref, u_ref, at, index)
            other = pltpu.roll(tile, 64, axis=1)
            for out in range(2):
                part = tile * straight[out][index] + other * crossed[out][index]
                result[out] = part if result[out] is None else result[out] + part
        for out in range(2):
            next_ref[:, at, out * 128 : (out + 1) * 128] = result[out]


def call(kernel, outs, scratch=(), name=None, final=False, far=()):
    kinds = [shape(o.shape, o.dtype) if final else pltpu.VMEM(o.shape, o.dtype) for o in outs]

    def run(*args):
        placed = [
            a if k in far else pltpu.with_memory_space_constraint(a, pltpu.VMEM)
            for k, a in enumerate(args)
        ]
        return pl.pallas_call(
            kernel,
            out_shape=kinds,
            in_specs=[pl.BlockSpec() if k in far else VMEM for k in range(len(args))],
            out_specs=[VMEM] * len(outs),
            scratch_shapes=list(scratch),
            name=name,
        )(*placed)

    return run


def shape(dims, kind):
    return jax.ShapeDtypeStruct(dims, kind)


def per_device(ahead_table, back_table, state_block, stored_fields, slope_fields, kernels, gains):
    lat_count, lon_count = lax.axis_size("lat"), lax.axis_size("lon")
    down = [(i, i + 1) for i in range(lat_count - 1)]
    up = [(i + 1, i) for i in range(lat_count - 1)]
    east = [(i, (i + 1) % lon_count) for i in range(lon_count)]
    width = LANES + LAYERS * CH

    both = jnp.concatenate([state_block.astype(BF16), slope_fields], axis=2)
    native = jnp.transpose(state_block, (1, 0, 2))
    above = lax.ppermute(both, "lat", down)
    below = lax.ppermute(both, "lat", up)
    (last,) = call(sides_kernel, [shape((EXT, SIDE, width), BF16)], name="sides")(both, above, below)
    left = lax.ppermute(last, "lon", east)
    ahead_weights, back_weights = call(
        weights_kernel,
        [
            shape((LAYERS * 3, 3 * 128, 128), BF16),
            shape((LAYERS * 3, 128, 3 * 128), BF16),
        ],
        name="weights",
    )(kernels.reshape(LAYERS * 9, CH, CH), last)

    place = lax.axis_index("lon")
    row_index = lax.axis_index("lat") * ROWS + place // 8
    area = jnp.cos(jnp.pi * ((row_index.astype(F32) + 0.5) / NLAT - 0.5))
    wave = jnp.arange(768)
    wave_weight = jnp.where((wave == 0) | (wave == NLON // 2), 1.0 / NLON, 2.0 / NLON)
    wave_weight = jnp.where(wave < WAVES, wave_weight, 0.0).astype(F32)
    columns = jnp.pad(gains, ((0, 0), (0, 768 - WAVES))).T * wave_weight[:, None]
    chosen = jnp.where(place % 2 == 0, columns[:, 0:SLOTS], columns[:, SLOTS : 2 * SLOTS])
    chosen = chosen * (area * area)
    weight = jnp.concatenate([chosen] * 4, axis=1)

    work = [
        pltpu.VMEM((FLAT, LANES), F32),
        pltpu.VMEM((FLAT, LANES), F32),
        pltpu.VMEM((EXT * PITCH, 3 * LANES), BF16),
    ]
    (packed,) = call(forward_kernel, [shape((32, 16, 128), BF16)], work, name="forward")(
        both, above, below, left, ahead_weights
    )
    circles = lax.all_to_all(packed, "lon", 0, 0, tiled=True)
    (known,) = call(
        stored_kernel, [shape((24, 24), F32)], [pltpu.VMEM((10, 24, 128), F32)], name="known"
    )(native, stored_fields, packed)
    (filtered,) = call(
        filter_kernel, [shape((32, 16, 128), BF16)], [pltpu.VMEM((768, 128), BF16)], name="spectral", far=(0, 1, 2)
    )(circles, ahead_table, back_table, weight, known)
    got = lax.all_to_all(filtered, "lon", 0, 0, tiled=True)
    gabove = lax.ppermute(got[8:32], "lat", down)
    gbelow = lax.ppermute(got[0:24], "lat", up)
    image, sums = call(
        adjoint_kernel,
        [shape((ROWS, COLS, LANES), F32), shape((8, 128), F32)],
        work + [pltpu.VMEM((12, 24, 128), F32)],
        name="adjoint",
        far=(0, 1, 2, 3, 4, 5, 9),
    )(
        native,
        stored_fields,
        both,
        above,
        below,
        left,
        got,
        gabove,
        gbelow,
        back_weights,
        known,
    )
    spread = lax.all_to_all(
        jnp.broadcast_to(sums, (lat_count, 8, 128)), "lat", 0, 0, tiled=True
    )
    partial = spread.sum(0)
    spread = lax.all_to_all(
        jnp.broadcast_to(partial, (lon_count, 8, 128)), "lon", 0, 0, tiled=True
    )
    following, diag, stored, factor = call(
        finish_kernel,
        [
            shape((COLS, ROWS, LANES), F32),
            shape((VECS, VECS), F32),
            shape((VECS, STORED), F32),
            shape((VECS, VECS), F32),
        ],
        name="finish",
        final=True,
    )(spread, native, stored_fields, image)
    return jnp.transpose(following, (1, 0, 2)), diag, stored.T, factor


def solution(mesh):
    ahead, back = tables()
    return jax.shard_map(
        functools.partial(per_device, jnp.asarray(ahead), jnp.asarray(back)),
        mesh=mesh,
        in_specs=(P("lat", "lon", None), P("lat", "lon", None), P("lat", "lon", None), P(), P()),
        out_specs=(P("lat", "lon", None), P(), P(), P()),
        check_vma=False,
    )
```

```python
import functools

import jax
import jax.numpy as jnp
import numpy as np
from jax import lax
from jax.experimental import pallas as pl
from jax.experimental.pallas import tpu as pltpu
from jax.sharding import PartitionSpec as P

F32 = jnp.float32
BF16 = jnp.bfloat16
HIGHEST = lax.Precision.HIGHEST

ROWS, COLS, CH, VECS, STORED, LAYERS = 4, 45, 64, 4, 16, 3
NLAT, NLON, WAVES = 64, 1440, 721
LANES = VECS * CH
HALO = 3
EXT = ROWS + 2 * HALO
PITCH = 64
LEAD = 8
SIDE = 8
FLAT = LEAD + EXT * PITCH + 8
SLOTS = 32
FIELDS = VECS + STORED + VECS
VMEM = pl.BlockSpec(memory_space=pltpu.VMEM)


def lane_ids(shape):
    return lax.broadcasted_iota(jnp.int32, shape, len(shape) - 1)


def row_ids(shape):
    return lax.broadcasted_iota(jnp.int32, shape, len(shape) - 2)


def tables():
    wave = 4 * np.arange(192)[None, :] + np.arange(4)[:, None]
    live = wave < WAVES
    q, t, j = np.meshgrid(np.arange(3), np.arange(8), np.arange(16), indexing="ij")
    slot = (16 * q + j).reshape(-1)
    point = (45 * t).reshape(-1) - 3 + slot
    angle = 2 * np.pi * ((wave[:, :, None] * point) % NLON) / NLON
    keep = live[:, :, None] & (slot < COLS)
    ahead = np.concatenate([np.cos(angle) * keep, np.sin(angle) * keep], axis=2)
    q, t, j = np.meshgrid(np.arange(4), np.arange(8), np.arange(16), indexing="ij")
    slot = (16 * q + j).reshape(-1)
    point = (45 * t).reshape(-1) - SIDE + slot
    angle = 2 * np.pi * ((wave[:, None, :] * point[None, :, None]) % NLON) / NLON
    held = (slot >= SIDE - HALO) & (slot < SIDE + COLS + HALO)
    keep = live[:, None, :] & held[None, :, None]
    back = np.concatenate([np.cos(angle) * keep, np.sin(angle) * keep], axis=2)
    return ahead.astype(jnp.bfloat16), back.astype(jnp.bfloat16)


def line_of(odd_ref, x_ref, near_ref, far_ref, row):
    if HALO <= row < HALO + ROWS:
        return x_ref[row - HALO].astype(F32)
    at = row + ROWS - HALO if row < HALO else row - HALO - ROWS
    near, far = near_ref[at].astype(F32), far_ref[at].astype(F32)
    odd = odd_ref[0] == 1
    return jnp.where(odd, near, far) if row < HALO else jnp.where(odd, far, near)


def sides_kernel(odd_ref, x_ref, near_ref, far_ref, last_ref):
    for row in range(EXT):
        line = line_of(odd_ref, x_ref, near_ref, far_ref, row)
        last_ref[row] = line[COLS - SIDE : COLS].astype(BF16)


def weights_kernel(taps_ref, after_ref, ahead_ref, back_ref):
    none = jnp.zeros((CH, CH), F32)
    for layer in range(LAYERS):
        for up in range(3):
            for side in range(3):
                block = taps_ref[9 * layer + 3 * up + side].astype(F32)
                pair = jnp.concatenate(
                    [
                        jnp.concatenate([block, none], axis=1),
                        jnp.concatenate([none, block], axis=1),
                    ],
                    axis=0,
                ).astype(BF16)
                ahead_ref[3 * layer + up, 128 * side : 128 * side + 128, :] = pair
                back_ref[3 * layer + 2 - up, :, 256 - 128 * side : 384 - 128 * side] = pair


def slope_lanes(slopes_ref, layer, start, count):
    pair = slopes_ref[pl.ds(start, count), (layer // 2) * 128 : (layer // 2) * 128 + 128]
    other = pltpu.roll(pair, 64, axis=1)
    low = lane_ids(pair.shape) < 64
    both = jnp.where(low, pair, other) if layer % 2 == 0 else jnp.where(low, other, pair)
    return jnp.concatenate([both, both], axis=1)


def convolve(field_ref, shifted_ref, weights_ref, layer, first, count, turned):
    have = (count + 2) * PITCH
    start = LEAD + (first - 1) * PITCH
    for pair in range(2):
        for step in range(3):
            at = 384 * pair + 128 * step
            shifted_ref[0:have, at : at + 128] = field_ref[
                pl.ds(start + step - 1, have), 128 * pair : 128 * pair + 128
            ].astype(BF16)
    halves = []
    for pair in range(2):
        total = None
        for step in range(3):
            part = lax.dot_general(
                shifted_ref[step * PITCH : (step + count) * PITCH, 384 * pair : 384 * pair + 384],
                weights_ref[layer * 3 + step],
                (((1,), (1 if turned else 0,)), ((), ())),
                preferred_element_type=F32,
            )
            total = part if total is None else total + part
        halves.append(total)
    return jnp.concatenate(halves, axis=1)


def parcel(slopes_ref, index):
    if index >= EXT * LAYERS:
        return jnp.zeros((16, SLOTS), F32)
    row, layer = index // LAYERS, index % LAYERS
    at = LEAD + row * PITCH + SIDE
    block = slopes_ref[at : at + 8, (layer // 2) * 128 : (layer // 2) * 128 + 128]
    base = 64 * (layer % 2)
    return jnp.concatenate(
        [
            jnp.zeros((8, SLOTS), F32),
            block[0:4, base : base + SLOTS],
            block[0:4, base + SLOTS : base + 2 * SLOTS],
        ],
        axis=0,
    )


def forward_kernel(
    odd_ref,
    x_ref,
    near_ref,
    far_ref,
    left_ref,
    weights_ref,
    send_ref,
    field_ref,
    slopes_ref,
    shifted_ref,
):
    field_ref[...] = jnp.zeros((FLAT, LANES), F32)
    slopes_ref[...] = jnp.zeros((FLAT, LANES), F32)
    for row in range(EXT):
        at = LEAD + row * PITCH
        line = line_of(odd_ref, x_ref, near_ref, far_ref, row)
        side = left_ref[row].astype(F32)
        field_ref[at : at + SIDE, :] = side[:, 0:LANES]
        field_ref[at + SIDE : at + SIDE + COLS, :] = line[:, 0:LANES]
        slopes_ref[at : at + SIDE, 0:192] = side[:, LANES:]
        slopes_ref[at + SIDE : at + SIDE + COLS, 0:192] = line[:, LANES:]
    for layer in range(LAYERS):
        first = layer + 1
        count = EXT - 2 * first
        total = convolve(field_ref, shifted_ref, weights_ref, layer, first, count, False)
        start = LEAD + first * PITCH
        total = total * slope_lanes(slopes_ref, layer, start, count * PITCH)
        field_ref[start : start + count * PITCH, :] = total.astype(BF16).astype(F32)
    for row in range(ROWS):
        line = field_ref[pl.ds(LEAD + (HALO + row) * PITCH + SIDE - HALO, 48), :]
        for group in range(8):
            pieces = [
                line[16 * q : 16 * q + 16, group * SLOTS : (group + 1) * SLOTS] for q in range(3)
            ]
            pieces.append(parcel(slopes_ref, row * 8 + group))
            send_ref[row * 8 + group] = jnp.concatenate(pieces, axis=1).astype(BF16)


def filter_kernel(
    got_ref, ahead_ref, back_ref, gains_ref, known_ref, send_ref, work_ref
):
    quarter = [
        got_ref[8 * part : 8 * part + 8].astype(F32).reshape(128, 128) for part in range(4)
    ]
    even, odd = quarter[0] + quarter[2], quarter[1] + quarter[3]
    across, along = quarter[0] - quarter[2], quarter[1] - quarter[3]
    real = [even + odd, across, even - odd, across]
    imag = [None, -along, None, along]
    low = lane_ids((128, 128)) < SLOTS

    def turn(value, shift):
        return value if shift % 128 == 0 else pltpu.roll(value, shift % 128, axis=1)

    for kind in range(4):
        for q in range(3):
            a = real[kind]
            b = imag[kind]
            left, right = turn(a, -SLOTS * q), turn(a, SLOTS - SLOTS * q)
            if b is None:
                top = jnp.where(low, left, 0.0)
                bottom = jnp.where(low, 0.0, -right)
            else:
                top = jnp.where(low, left, turn(b, SLOTS - SLOTS * q))
                bottom = jnp.where(low, turn(b, -SLOTS * q), -right)
            work_ref[128 * q : 128 * q + 128, :] = top.astype(BF16)
            work_ref[384 + 128 * q : 512 + 128 * q, :] = bottom.astype(BF16)
        spectrum = jnp.dot(ahead_ref[kind], work_ref[...], preferred_element_type=F32)
        weight = gains_ref[pl.ds(kind, 192, stride=4), :]
        spectrum = spectrum * weight
        below = jnp.where(
            lane_ids((192, 128)) < SLOTS, -turn(spectrum, -SLOTS), turn(spectrum, SLOTS)
        )
        packed = jnp.concatenate([spectrum, below], axis=0).astype(BF16)
        part = jnp.dot(back_ref[kind], packed, preferred_element_type=F32)
        if kind == 0:
            zero = part
        elif kind == 1:
            one = part
        elif kind == 2:
            two = part
        else:
            three = part
    plus, minus = zero + two, zero - two
    swing = one + three
    turned = turn(three - one, -SLOTS)
    result = [plus + swing, minus + turned, plus - swing, minus - turned]
    lane = lane_ids((128, 128))
    for part in range(4):
        packed = result[part][0:128]
        for q in range(1, 4):
            packed = jnp.where(
                lane >= SLOTS * q, turn(result[part][128 * q : 128 * q + 128], SLOTS * q), packed
            )
        if part < 3:
            passing = got_ref[8 * part + 1 : 8 * part + 9]
        else:
            passing = jnp.concatenate([got_ref[25:32], got_ref[0:1]], axis=0)
        carried = (lane >= 96) & (row_ids((128, 128)) % 16 >= 8)
        packed = jnp.where(carried, passing.astype(F32).reshape(128, 128), packed)
        send_ref[8 * part : 8 * part + 8] = packed.reshape(8, 16, 128).astype(BF16)


def twice(tile, half):
    other = pltpu.roll(tile, 64, axis=1)
    low = lane_ids(tile.shape) < 64
    return jnp.where(low, tile, other) if half == 0 else jnp.where(low, other, tile)


def gram_rows(first, rows_ref):
    total = None
    for index, count in first:
        shape = (24, 128)
        pick = (row_ids(shape) == 2 * index + (lane_ids(shape) // 64)).astype(F32)
        rows = rows_ref[index]
        part = lax.dot_general(
            pick, rows, (((1,), (1,)), ((), ())), precision=HIGHEST, preferred_element_type=F32
        )
        total = part if total is None else total + part
    return total


def stored_kernel(q_ref, p_ref, after_ref, out_ref, rows_ref):
    rows_ref[...] = jnp.zeros(rows_ref.shape, F32)
    known = 10
    for right in range(known):
        for half in range(2):
            totals = [None] * (right + 1)
            for row in range(ROWS):
                tile = tile_of(q_ref, p_ref, None, row, right)
                doubled = twice(tile, half)
                for left in range(right + 1):
                    product = tile_of(q_ref, p_ref, None, row, left) * doubled
                    totals[left] = product if totals[left] is None else totals[left] + product
            for left in range(right + 1):
                rows_ref[left, 2 * right + half : 2 * right + half + 1, :] = jnp.sum(
                    totals[left], axis=0, keepdims=True
                )
    out_ref[...] = gram_rows([(index, 128) for index in range(known)], rows_ref)


def tile_of(q_ref, p_ref, u_ref, row, index):
    if index < 2:
        return q_ref[:, row, index * 128 : (index + 1) * 128]
    if index < 10:
        return p_ref[row, :, (index - 2) * 128 : (index - 1) * 128].astype(F32)
    return u_ref[row, :, (index - 10) * 128 : (index - 9) * 128]


def adjoint_kernel(
    odd_ref,
    q_ref,
    p_ref,
    x_ref,
    near_ref,
    far_ref,
    left_ref,
    got_ref,
    gnear_ref,
    gfar_ref,
    weights_ref,
    known_ref,
    u_ref,
    sums_ref,
    field_ref,
    slopes_ref,
    shifted_ref,
    rows_ref,
):
    field_ref[0:LEAD, :] = jnp.zeros((LEAD, LANES), F32)
    field_ref[FLAT - 8 : FLAT, :] = jnp.zeros((8, LANES), F32)
    slopes_ref[...] = jnp.zeros((FLAT, LANES), F32)
    for row in range(EXT):
        at = LEAD + row * PITCH
        line = line_of(odd_ref, x_ref, near_ref, far_ref, row)
        slopes_ref[at : at + SIDE, 0:192] = left_ref[row, :, LANES:].astype(F32)
        slopes_ref[at + SIDE : at + SIDE + COLS, 0:192] = line[:, LANES:]
        halves = []
        for layer in range(LAYERS):
            block = got_ref[LAYERS * row + layer].astype(F32)
            halves += [block[8:12, 96:128], block[12:16, 96:128]]
        slopes_ref[at + SIDE + COLS : at + SIDE + COLS + 4, 0:192] = jnp.concatenate(halves, axis=1)
    for row in range(EXT):
        at = LEAD + row * PITCH
        if HALO <= row < HALO + ROWS:
            base = (row - HALO) * 8
            blocks = [got_ref[base + group].astype(F32) for group in range(8)]
        else:
            base = row * 8 if row < HALO else (row - HALO - ROWS) * 8
            odd = odd_ref[0] == 1
            blocks = []
            for group in range(8):
                near = gnear_ref[base + group].astype(F32)
                far = gfar_ref[base + group].astype(F32)
                first, second = (near, far) if row < HALO else (far, near)
                blocks.append(jnp.where(odd, first, second))
        for q in range(4):
            field_ref[at + 16 * q : at + 16 * q + 16, :] = jnp.concatenate(
                [block[:, q * SLOTS : (q + 1) * SLOTS] for block in blocks], axis=1
            )
    top = field_ref[LEAD : LEAD + EXT * PITCH, :] * slope_lanes(
        slopes_ref, LAYERS - 1, LEAD, EXT * PITCH
    )
    field_ref[LEAD : LEAD + EXT * PITCH, :] = top.astype(BF16).astype(F32)
    for layer in range(LAYERS - 1, -1, -1):
        first = LAYERS - layer
        count = EXT - 2 * first
        total = convolve(field_ref, shifted_ref, weights_ref, layer, first, count, True)
        start = LEAD + first * PITCH
        if layer > 0:
            total = total * slope_lanes(slopes_ref, layer - 1, start, count * PITCH)
            total = total.astype(BF16).astype(F32)
        field_ref[start : start + count * PITCH, :] = total
    for row in range(ROWS):
        u_ref[row] = field_ref[pl.ds(LEAD + (HALO + row) * PITCH + SIDE, COLS), :]
    rows_ref[...] = jnp.zeros(rows_ref.shape, F32)
    for right in range(2):
        for half in range(2):
            totals = [None] * 12
            for row in range(ROWS):
                doubled = twice(tile_of(q_ref, p_ref, u_ref, row, 10 + right), half)
                for left in range(12):
                    product = tile_of(q_ref, p_ref, u_ref, row, left) * doubled
                    totals[left] = product if totals[left] is None else totals[left] + product
            for left in range(12):
                at = 20 + 2 * right + half
                rows_ref[left, at : at + 1, :] = jnp.sum(totals[left], axis=0, keepdims=True)
    gram = known_ref[...] + gram_rows([(index, 128) for index in range(12)], rows_ref)
    wide = jnp.concatenate([gram, jnp.zeros((24, 128 - 24), F32)], axis=1)
    sums_ref[...] = (
        wide[0:8]
        + pltpu.roll(wide[8:16], SLOTS, axis=1)
        + pltpu.roll(wide[16:24], 2 * SLOTS, axis=1)
    )


def finish_kernel(sums_ref, q_ref, p_ref, u_ref, next_ref, diag_ref, stored_ref, factor_ref):
    total = sums_ref[0]
    for index in range(1, sums_ref.shape[0]):
        total = total + sums_ref[index]
    total = total * (1.0 / (NLAT * NLON * CH))
    narrow = lane_ids((8, 128)) < SLOTS
    blocks = [
        jnp.where(narrow, total if k == 0 else pltpu.roll(total, 128 - SLOTS * k, axis=1), 0.0)
        for k in range(3)
    ]
    square = (128, 128)
    half = jnp.concatenate(blocks + [jnp.zeros((104, 128), F32)], axis=0)
    row, lane = row_ids(square), lane_ids(square)
    gram = jnp.where(row <= lane, half, jnp.transpose(half))
    known = VECS + STORED
    image = pltpu.roll(gram, 128 - known, axis=1)
    keep = lane < VECS
    coef = jnp.where(
        keep & (row < known), -image, jnp.where(keep & (row == lane + known), 1.0, 0.0)
    )
    diag_ref[...] = image[0:VECS, 0:VECS]
    stored_ref[...] = jnp.transpose(image)[0:VECS, VECS:known]
    applied = jnp.dot(gram, coef, precision=HIGHEST, preferred_element_type=F32)
    small = lax.dot_general(
        coef, applied, (((0,), (0,)), ((), ())), precision=HIGHEST, preferred_element_type=F32
    )
    entry = [[small[i : i + 1, j : j + 1] for j in range(VECS)] for i in range(VECS)]
    factor = [[None] * VECS for _ in range(VECS)]
    for i in range(VECS):
        value = entry[i][i]
        for k in range(i):
            value = value - factor[k][i] * factor[k][i]
        factor[i][i] = jnp.sqrt(value)
        for j in range(i + 1, VECS):
            value = entry[i][j]
            for k in range(i):
                value = value - factor[k][i] * factor[k][j]
            factor[i][j] = value / factor[i][i]
    inverse = [[None] * VECS for _ in range(VECS)]
    for j in range(VECS):
        inverse[j][j] = 1.0 / factor[j][j]
        for i in range(j - 1, -1, -1):
            value = None
            for k in range(i + 1, j + 1):
                term = factor[i][k] * inverse[k][j]
                value = term if value is None else value + term
            inverse[i][j] = -value / factor[i][i]
    upper = jnp.zeros(square, F32)
    solved = jnp.zeros(square, F32)
    for i in range(VECS):
        for j in range(i, VECS):
            here = (row == i) & (lane == j)
            upper = jnp.where(here, factor[i][j], upper)
            solved = jnp.where(here, inverse[i][j], solved)
    factor_ref[...] = upper[0:VECS, 0:VECS]
    mixed = jnp.dot(coef, solved, precision=HIGHEST, preferred_element_type=F32)
    low = lane_ids((1, 128)) < 64
    straight, crossed = [], []
    for out in range(2):
        choose = (row == 2 * out + lane // 64).astype(F32)
        lines = jnp.dot(mixed, choose, precision=HIGHEST, preferred_element_type=F32)
        straight.append([])
        crossed.append([])
        for index in range(12):
            a = lines[2 * index : 2 * index + 1]
            b = lines[2 * index + 1 : 2 * index + 2]
            straight[out].append(jnp.where(low, a, b))
            crossed[out].append(jnp.where(low, b, a))
    for at in range(ROWS):
        result = [None, None]
        for index in range(12):
            tile = tile_of(q_ref, p_ref, u_ref, at, index)
            other = pltpu.roll(tile, 64, axis=1)
            for out in range(2):
                part = tile * straight[out][index] + other * crossed[out][index]
                result[out] = part if result[out] is None else result[out] + part
        for out in range(2):
            next_ref[:, at, out * 128 : (out + 1) * 128] = result[out]


def call(kernel, outs, scratch=(), name=None, final=False, far=()):
    kinds = [shape(o.shape, o.dtype) if final else pltpu.VMEM(o.shape, o.dtype) for o in outs]

    def run(*args):
        placed, specs = [], []
        for index, value in enumerate(args):
            if value.dtype == jnp.int32:
                specs.append(pl.BlockSpec(memory_space=pltpu.SMEM))
            elif index in far:
                specs.append(pl.BlockSpec())
            else:
                specs.append(VMEM)
                value = pltpu.with_memory_space_constraint(value, pltpu.VMEM)
            placed.append(value)
        return pl.pallas_call(
            kernel,
            out_shape=kinds,
            in_specs=specs,
            out_specs=[VMEM] * len(outs),
            scratch_shapes=list(scratch),
            name=name,
        )(*placed)

    return run


def shape(dims, kind):
    return jax.ShapeDtypeStruct(dims, kind)


def per_device(ahead_table, back_table, state_block, stored_fields, slope_fields, kernels, gains):
    lat_count, lon_count = lax.axis_size("lat"), lax.axis_size("lon")
    near_pairs = [(i, i ^ 1) for i in range(lat_count)]
    far_pairs = [(i, i + 1) for i in range(1, lat_count - 1, 2)]
    far_pairs = far_pairs + [(b, a) for a, b in far_pairs]
    east = [(i, (i + 1) % lon_count) for i in range(lon_count)]
    width = LANES + LAYERS * CH

    both = jnp.concatenate([state_block.astype(BF16), slope_fields], axis=2)
    native = jnp.transpose(state_block, (1, 0, 2))
    parity = lax.axis_index("lat") % 2
    odd = jnp.full((1,), parity, jnp.int32)
    far = lax.ppermute(both, "lat", far_pairs)
    near = lax.ppermute(both, "lat", near_pairs)
    (last,) = call(sides_kernel, [shape((EXT, SIDE, width), BF16)], name="sides")(odd, both, near, far)
    left = lax.ppermute(last, "lon", east)
    ahead_weights, back_weights = call(
        weights_kernel,
        [
            shape((LAYERS * 3, 3 * 128, 128), BF16),
            shape((LAYERS * 3, 128, 3 * 128), BF16),
        ],
        name="weights",
    )(kernels.reshape(LAYERS * 9, CH, CH), last)

    place = lax.axis_index("lon")
    row_index = lax.axis_index("lat") * ROWS + place // 8
    area = jnp.cos(jnp.pi * ((row_index.astype(F32) + 0.5) / NLAT - 0.5))
    wave = jnp.arange(768)
    wave_weight = jnp.where((wave == 0) | (wave == NLON // 2), 1.0 / NLON, 2.0 / NLON)
    wave_weight = jnp.where(wave < WAVES, wave_weight, 0.0).astype(F32)
    columns = jnp.pad(gains, ((0, 0), (0, 768 - WAVES))).T * wave_weight[:, None]
    chosen = jnp.where(place % 2 == 0, columns[:, 0:SLOTS], columns[:, SLOTS : 2 * SLOTS])
    chosen = chosen * (area * area)
    weight = jnp.concatenate([chosen] * 4, axis=1)

    work = [
        pltpu.VMEM((FLAT, LANES), F32),
        pltpu.VMEM((FLAT, LANES), F32),
        pltpu.VMEM((EXT * PITCH, 3 * LANES), BF16),
    ]
    (packed,) = call(forward_kernel, [shape((32, 16, 128), BF16)], work, name="forward")(
        odd, both, near, far, left, ahead_weights
    )
    circles = lax.all_to_all(packed, "lon", 0, 0, tiled=True)
    (known,) = call(
        stored_kernel, [shape((24, 24), F32)], [pltpu.VMEM((10, 24, 128), F32)], name="known"
    )(native, stored_fields, packed)
    (filtered,) = call(
        filter_kernel, [shape((32, 16, 128), BF16)], [pltpu.VMEM((768, 128), BF16)], name="spectral", far=(0, 1, 2)
    )(circles, ahead_table, back_table, weight, known)
    got = lax.all_to_all(filtered, "lon", 0, 0, tiled=True)
    gfar = lax.ppermute(lax.dynamic_slice_in_dim(got, 8 * parity, 24), "lat", far_pairs)
    gnear = lax.ppermute(lax.dynamic_slice_in_dim(got, 8 - 8 * parity, 24), "lat", near_pairs)
    image, sums = call(
        adjoint_kernel,
        [shape((ROWS, COLS, LANES), F32), shape((8, 128), F32)],
        work + [pltpu.VMEM((12, 24, 128), F32)],
        name="adjoint",
        far=(1, 2, 3, 4, 5, 6, 10),
    )(
        odd,
        native,
        stored_fields,
        both,
        near,
        far,
        left,
        got,
        gnear,
        gfar,
        back_weights,
        known,
    )
    spread = lax.all_to_all(
        jnp.broadcast_to(sums, (lat_count, 8, 128)), "lat", 0, 0, tiled=True
    )
    partial = spread.sum(0)
    spread = lax.all_to_all(
        jnp.broadcast_to(partial, (lon_count, 8, 128)), "lon", 0, 0, tiled=True
    )
    following, diag, stored, factor = call(
        finish_kernel,
        [
            shape((COLS, ROWS, LANES), F32),
            shape((VECS, VECS), F32),
            shape((VECS, STORED), F32),
            shape((VECS, VECS), F32),
        ],
        name="finish",
        final=True,
    )(spread, native, stored_fields, image)
    return jnp.transpose(following, (1, 0, 2)), diag, stored.T, factor


def solution(mesh):
    ahead, back = tables()
    return jax.shard_map(
        functools.partial(per_device, jnp.asarray(ahead), jnp.asarray(back)),
        mesh=mesh,
        in_specs=(P("lat", "lon", None), P("lat", "lon", None), P("lat", "lon", None), P(), P()),
        out_specs=(P("lat", "lon", None), P(), P(), P()),
        check_vma=False,
    )
```

```python
import functools

import jax
import jax.numpy as jnp
import numpy as np
from jax import lax
from jax.experimental import pallas as pl
from jax.experimental.pallas import tpu as pltpu
from jax.sharding import PartitionSpec as P

F32 = jnp.float32
BF16 = jnp.bfloat16
HIGHEST = lax.Precision.HIGHEST

ROWS, COLS, CH, VECS, STORED, LAYERS = 4, 45, 64, 4, 16, 3
NLAT, NLON, WAVES = 64, 1440, 721
LANES = VECS * CH
HALO = 3
EXT = ROWS + 2 * HALO
PITCH = 64
LEAD = 8
SIDE = 8
FLAT = LEAD + EXT * PITCH + 8
SLOTS = 32
FIELDS = VECS + STORED + VECS
VMEM = pl.BlockSpec(memory_space=pltpu.VMEM)


def lane_ids(shape):
    return lax.broadcasted_iota(jnp.int32, shape, len(shape) - 1)


def row_ids(shape):
    return lax.broadcasted_iota(jnp.int32, shape, len(shape) - 2)


def tables():
    wave = 4 * np.arange(192)[None, :] + np.arange(4)[:, None]
    live = wave < WAVES
    q, t, j = np.meshgrid(np.arange(3), np.arange(8), np.arange(16), indexing="ij")
    slot = (16 * q + j).reshape(-1)
    point = (45 * t).reshape(-1) - 3 + slot
    angle = 2 * np.pi * ((wave[:, :, None] * point) % NLON) / NLON
    keep = live[:, :, None] & (slot < COLS)
    ahead = np.concatenate([np.cos(angle) * keep, np.sin(angle) * keep], axis=2)
    q, t, j = np.meshgrid(np.arange(4), np.arange(8), np.arange(16), indexing="ij")
    slot = (16 * q + j).reshape(-1)
    point = (45 * t).reshape(-1) - SIDE + slot
    angle = 2 * np.pi * ((wave[:, None, :] * point[None, :, None]) % NLON) / NLON
    held = (slot >= SIDE - HALO) & (slot < SIDE + COLS + HALO)
    keep = live[:, None, :] & held[None, :, None]
    back = np.concatenate([np.cos(angle) * keep, np.sin(angle) * keep], axis=2)
    return ahead.astype(jnp.bfloat16), back.astype(jnp.bfloat16)


def line_of(x_ref, above_ref, below_ref, row):
    if row < HALO:
        return above_ref[row + ROWS - HALO].astype(F32)
    if row < HALO + ROWS:
        return x_ref[row - HALO].astype(F32)
    return below_ref[row - HALO - ROWS].astype(F32)


def sides_kernel(x_ref, last_ref):
    for row in range(ROWS):
        last_ref[row] = x_ref[row].astype(F32)[COLS - SIDE : COLS].astype(BF16)


def weights_kernel(taps_ref, after_ref, ahead_ref, back_ref):
    none = jnp.zeros((CH, CH), F32)
    for layer in range(LAYERS):
        for up in range(3):
            for side in range(3):
                block = taps_ref[9 * layer + 3 * up + side].astype(F32)
                pair = jnp.concatenate(
                    [
                        jnp.concatenate([block, none], axis=1),
                        jnp.concatenate([none, block], axis=1),
                    ],
                    axis=0,
                ).astype(BF16)
                ahead_ref[3 * layer + up, 128 * side : 128 * side + 128, :] = pair
                back_ref[3 * layer + 2 - up, :, 256 - 128 * side : 384 - 128 * side] = pair


def slope_lanes(slopes_ref, layer, start, count):
    pair = slopes_ref[pl.ds(start, count), (layer // 2) * 128 : (layer // 2) * 128 + 128]
    other = pltpu.roll(pair, 64, axis=1)
    low = lane_ids(pair.shape) < 64
    both = jnp.where(low, pair, other) if layer % 2 == 0 else jnp.where(low, other, pair)
    return jnp.concatenate([both, both], axis=1)


def convolve(field_ref, shifted_ref, weights_ref, layer, first, count, turned):
    have = (count + 2) * PITCH
    start = LEAD + (first - 1) * PITCH
    for pair in range(2):
        for step in range(3):
            at = 384 * pair + 128 * step
            shifted_ref[0:have, at : at + 128] = field_ref[
                pl.ds(start + step - 1, have), 128 * pair : 128 * pair + 128
            ].astype(BF16)
    halves = []
    for pair in range(2):
        total = None
        for step in range(3):
            part = lax.dot_general(
                shifted_ref[step * PITCH : (step + count) * PITCH, 384 * pair : 384 * pair + 384],
                weights_ref[layer * 3 + step],
                (((1,), (1 if turned else 0,)), ((), ())),
                preferred_element_type=F32,
            )
            total = part if total is None else total + part
        halves.append(total)
    return jnp.concatenate(halves, axis=1)


def parcel(slopes_ref, index):
    if index >= EXT * LAYERS:
        return jnp.zeros((16, SLOTS), F32)
    row, layer = index // LAYERS, index % LAYERS
    at = LEAD + row * PITCH + SIDE
    block = slopes_ref[at : at + 8, (layer // 2) * 128 : (layer // 2) * 128 + 128]
    base = 64 * (layer % 2)
    return jnp.concatenate(
        [
            jnp.zeros((8, SLOTS), F32),
            block[0:4, base : base + SLOTS],
            block[0:4, base + SLOTS : base + 2 * SLOTS],
        ],
        axis=0,
    )


def forward_kernel(
    x_ref,
    above_ref,
    below_ref,
    left_ref,
    northwest_ref,
    southwest_ref,
    weights_ref,
    send_ref,
    field_ref,
    slopes_ref,
    shifted_ref,
):
    field_ref[...] = jnp.zeros((FLAT, LANES), F32)
    slopes_ref[...] = jnp.zeros((FLAT, LANES), F32)
    for row in range(EXT):
        at = LEAD + row * PITCH
        line = line_of(x_ref, above_ref, below_ref, row)
        side = line_of(left_ref, northwest_ref, southwest_ref, row)
        field_ref[at : at + SIDE, :] = side[:, 0:LANES]
        field_ref[at + SIDE : at + SIDE + COLS, :] = line[:, 0:LANES]
        slopes_ref[at : at + SIDE, 0:192] = side[:, LANES:]
        slopes_ref[at + SIDE : at + SIDE + COLS, 0:192] = line[:, LANES:]
    for layer in range(LAYERS):
        first = layer + 1
        count = EXT - 2 * first
        total = convolve(field_ref, shifted_ref, weights_ref, layer, first, count, False)
        start = LEAD + first * PITCH
        total = total * slope_lanes(slopes_ref, layer, start, count * PITCH)
        field_ref[start : start + count * PITCH, :] = total.astype(BF16).astype(F32)
    for row in range(ROWS):
        line = field_ref[pl.ds(LEAD + (HALO + row) * PITCH + SIDE - HALO, 48), :]
        for group in range(8):
            pieces = [
                line[16 * q : 16 * q + 16, group * SLOTS : (group + 1) * SLOTS] for q in range(3)
            ]
            pieces.append(parcel(slopes_ref, row * 8 + group))
            send_ref[row * 8 + group] = jnp.concatenate(pieces, axis=1).astype(BF16)


def filter_kernel(
    got_ref, ahead_ref, back_ref, gains_ref, known_ref, send_ref, work_ref
):
    quarter = [
        got_ref[8 * part : 8 * part + 8].astype(F32).reshape(128, 128) for part in range(4)
    ]
    even, odd = quarter[0] + quarter[2], quarter[1] + quarter[3]
    across, along = quarter[0] - quarter[2], quarter[1] - quarter[3]
    real = [even + odd, across, even - odd, across]
    imag = [None, -along, None, along]
    low = lane_ids((128, 128)) < SLOTS

    def turn(value, shift):
        return value if shift % 128 == 0 else pltpu.roll(value, shift % 128, axis=1)

    for kind in range(4):
        for q in range(3):
            a = real[kind]
            b = imag[kind]
            left, right = turn(a, -SLOTS * q), turn(a, SLOTS - SLOTS * q)
            if b is None:
                top = jnp.where(low, left, 0.0)
                bottom = jnp.where(low, 0.0, -right)
            else:
                top = jnp.where(low, left, turn(b, SLOTS - SLOTS * q))
                bottom = jnp.where(low, turn(b, -SLOTS * q), -right)
            work_ref[128 * q : 128 * q + 128, :] = top.astype(BF16)
            work_ref[384 + 128 * q : 512 + 128 * q, :] = bottom.astype(BF16)
        spectrum = jnp.dot(ahead_ref[kind], work_ref[...], preferred_element_type=F32)
        weight = gains_ref[pl.ds(kind, 192, stride=4), :]
        spectrum = spectrum * weight
        below = jnp.where(
            lane_ids((192, 128)) < SLOTS, -turn(spectrum, -SLOTS), turn(spectrum, SLOTS)
        )
        packed = jnp.concatenate([spectrum, below], axis=0).astype(BF16)
        part = jnp.dot(back_ref[kind], packed, preferred_element_type=F32)
        if kind == 0:
            zero = part
        elif kind == 1:
            one = part
        elif kind == 2:
            two = part
        else:
            three = part
    plus, minus = zero + two, zero - two
    swing = one + three
    turned = turn(three - one, -SLOTS)
    result = [plus + swing, minus + turned, plus - swing, minus - turned]
    lane = lane_ids((128, 128))
    for part in range(4):
        packed = result[part][0:128]
        for q in range(1, 4):
            packed = jnp.where(
                lane >= SLOTS * q, turn(result[part][128 * q : 128 * q + 128], SLOTS * q), packed
            )
        if part < 3:
            passing = got_ref[8 * part + 1 : 8 * part + 9]
        else:
            passing = jnp.concatenate([got_ref[25:32], got_ref[0:1]], axis=0)
        carried = (lane >= 96) & (row_ids((128, 128)) % 16 >= 8)
        packed = jnp.where(carried, passing.astype(F32).reshape(128, 128), packed)
        send_ref[8 * part : 8 * part + 8] = packed.reshape(8, 16, 128).astype(BF16)


def twice(tile, half):
    other = pltpu.roll(tile, 64, axis=1)
    low = lane_ids(tile.shape) < 64
    return jnp.where(low, tile, other) if half == 0 else jnp.where(low, other, tile)


def gram_rows(first, rows_ref):
    total = None
    for index, count in first:
        shape = (24, 128)
        pick = (row_ids(shape) == 2 * index + (lane_ids(shape) // 64)).astype(F32)
        rows = rows_ref[index]
        part = lax.dot_general(
            pick, rows, (((1,), (1,)), ((), ())), precision=HIGHEST, preferred_element_type=F32
        )
        total = part if total is None else total + part
    return total


def stored_kernel(q_ref, p_ref, after_ref, out_ref, rows_ref):
    rows_ref[...] = jnp.zeros(rows_ref.shape, F32)
    known = 10
    for right in range(known):
        for half in range(2):
            totals = [None] * (right + 1)
            for row in range(ROWS):
                tile = tile_of(q_ref, p_ref, None, row, right)
                doubled = twice(tile, half)
                for left in range(right + 1):
                    product = tile_of(q_ref, p_ref, None, row, left) * doubled
                    totals[left] = product if totals[left] is None else totals[left] + product
            for left in range(right + 1):
                rows_ref[left, 2 * right + half : 2 * right + half + 1, :] = jnp.sum(
                    totals[left], axis=0, keepdims=True
                )
    out_ref[...] = gram_rows([(index, 128) for index in range(known)], rows_ref)


def tile_of(q_ref, p_ref, u_ref, row, index):
    if index < 2:
        return q_ref[:, row, index * 128 : (index + 1) * 128]
    if index < 10:
        return p_ref[row, :, (index - 2) * 128 : (index - 1) * 128].astype(F32)
    return u_ref[row, :, (index - 10) * 128 : (index - 9) * 128]


def adjoint_kernel(
    q_ref,
    p_ref,
    x_ref,
    above_ref,
    below_ref,
    left_ref,
    northwest_ref,
    southwest_ref,
    got_ref,
    gabove_ref,
    gbelow_ref,
    weights_ref,
    known_ref,
    u_ref,
    sums_ref,
    field_ref,
    slopes_ref,
    shifted_ref,
    rows_ref,
):
    field_ref[0:LEAD, :] = jnp.zeros((LEAD, LANES), F32)
    field_ref[FLAT - 8 : FLAT, :] = jnp.zeros((8, LANES), F32)
    slopes_ref[...] = jnp.zeros((FLAT, LANES), F32)
    for row in range(EXT):
        at = LEAD + row * PITCH
        line = line_of(x_ref, above_ref, below_ref, row)
        side = line_of(left_ref, northwest_ref, southwest_ref, row)
        slopes_ref[at : at + SIDE, 0:192] = side[:, LANES:]
        slopes_ref[at + SIDE : at + SIDE + COLS, 0:192] = line[:, LANES:]
        halves = []
        for layer in range(LAYERS):
            block = got_ref[LAYERS * row + layer].astype(F32)
            halves += [block[8:12, 96:128], block[12:16, 96:128]]
        slopes_ref[at + SIDE + COLS : at + SIDE + COLS + 4, 0:192] = jnp.concatenate(halves, axis=1)
    for row in range(EXT):
        at = LEAD + row * PITCH
        if row < HALO:
            source, base = gabove_ref, row * 8
        elif row < HALO + ROWS:
            source, base = got_ref, (row - HALO) * 8
        else:
            source, base = gbelow_ref, (row - HALO - ROWS) * 8
        blocks = [source[base + group].astype(F32) for group in range(8)]
        for q in range(4):
            field_ref[at + 16 * q : at + 16 * q + 16, :] = jnp.concatenate(
                [block[:, q * SLOTS : (q + 1) * SLOTS] for block in blocks], axis=1
            )
    top = field_ref[LEAD : LEAD + EXT * PITCH, :] * slope_lanes(
        slopes_ref, LAYERS - 1, LEAD, EXT * PITCH
    )
    field_ref[LEAD : LEAD + EXT * PITCH, :] = top.astype(BF16).astype(F32)
    for layer in range(LAYERS - 1, -1, -1):
        first = LAYERS - layer
        count = EXT - 2 * first
        total = convolve(field_ref, shifted_ref, weights_ref, layer, first, count, True)
        start = LEAD + first * PITCH
        if layer > 0:
            total = total * slope_lanes(slopes_ref, layer - 1, start, count * PITCH)
            total = total.astype(BF16).astype(F32)
        field_ref[start : start + count * PITCH, :] = total
    for row in range(ROWS):
        u_ref[row] = field_ref[pl.ds(LEAD + (HALO + row) * PITCH + SIDE, COLS), :]
    rows_ref[...] = jnp.zeros(rows_ref.shape, F32)
    for right in range(2):
        for half in range(2):
            totals = [None] * 12
            for row in range(ROWS):
                doubled = twice(tile_of(q_ref, p_ref, u_ref, row, 10 + right), half)
                for left in range(12):
                    product = tile_of(q_ref, p_ref, u_ref, row, left) * doubled
                    totals[left] = product if totals[left] is None else totals[left] + product
            for left in range(12):
                at = 20 + 2 * right + half
                rows_ref[left, at : at + 1, :] = jnp.sum(totals[left], axis=0, keepdims=True)
    gram = known_ref[...] + gram_rows([(index, 128) for index in range(12)], rows_ref)
    wide = jnp.concatenate([gram, jnp.zeros((24, 128 - 24), F32)], axis=1)
    sums_ref[...] = (
        wide[0:8]
        + pltpu.roll(wide[8:16], SLOTS, axis=1)
        + pltpu.roll(wide[16:24], 2 * SLOTS, axis=1)
    )


def finish_kernel(sums_ref, q_ref, p_ref, u_ref, next_ref, diag_ref, stored_ref, factor_ref):
    total = sums_ref[0]
    for index in range(1, sums_ref.shape[0]):
        total = total + sums_ref[index]
    total = total * (1.0 / (NLAT * NLON * CH))
    narrow = lane_ids((8, 128)) < SLOTS
    blocks = [
        jnp.where(narrow, total if k == 0 else pltpu.roll(total, 128 - SLOTS * k, axis=1), 0.0)
        for k in range(3)
    ]
    square = (128, 128)
    half = jnp.concatenate(blocks + [jnp.zeros((104, 128), F32)], axis=0)
    row, lane = row_ids(square), lane_ids(square)
    gram = jnp.where(row <= lane, half, jnp.transpose(half))
    known = VECS + STORED
    image = pltpu.roll(gram, 128 - known, axis=1)
    keep = lane < VECS
    coef = jnp.where(
        keep & (row < known), -image, jnp.where(keep & (row == lane + known), 1.0, 0.0)
    )
    diag_ref[...] = image[0:VECS, 0:VECS]
    stored_ref[...] = jnp.transpose(image)[0:VECS, VECS:known]
    applied = jnp.dot(gram, coef, precision=HIGHEST, preferred_element_type=F32)
    small = lax.dot_general(
        coef, applied, (((0,), (0,)), ((), ())), precision=HIGHEST, preferred_element_type=F32
    )
    entry = [[small[i : i + 1, j : j + 1] for j in range(VECS)] for i in range(VECS)]
    factor = [[None] * VECS for _ in range(VECS)]
    for i in range(VECS):
        value = entry[i][i]
        for k in range(i):
            value = value - factor[k][i] * factor[k][i]
        factor[i][i] = jnp.sqrt(value)
        for j in range(i + 1, VECS):
            value = entry[i][j]
            for k in range(i):
                value = value - factor[k][i] * factor[k][j]
            factor[i][j] = value / factor[i][i]
    inverse = [[None] * VECS for _ in range(VECS)]
    for j in range(VECS):
        inverse[j][j] = 1.0 / factor[j][j]
        for i in range(j - 1, -1, -1):
            value = None
            for k in range(i + 1, j + 1):
                term = factor[i][k] * inverse[k][j]
                value = term if value is None else value + term
            inverse[i][j] = -value / factor[i][i]
    upper = jnp.zeros(square, F32)
    solved = jnp.zeros(square, F32)
    for i in range(VECS):
        for j in range(i, VECS):
            here = (row == i) & (lane == j)
            upper = jnp.where(here, factor[i][j], upper)
            solved = jnp.where(here, inverse[i][j], solved)
    factor_ref[...] = upper[0:VECS, 0:VECS]
    mixed = jnp.dot(coef, solved, precision=HIGHEST, preferred_element_type=F32)
    low = lane_ids((1, 128)) < 64
    straight, crossed = [], []
    for out in range(2):
        choose = (row == 2 * out + lane // 64).astype(F32)
        lines = jnp.dot(mixed, choose, precision=HIGHEST, preferred_element_type=F32)
        straight.append([])
        crossed.append([])
        for index in range(12):
            a = lines[2 * index : 2 * index + 1]
            b = lines[2 * index + 1 : 2 * index + 2]
            straight[out].append(jnp.where(low, a, b))
            crossed[out].append(jnp.where(low, b, a))
    for at in range(ROWS):
        result = [None, None]
        for index in range(12):
            tile = tile_of(q_ref, p_ref, u_ref, at, index)
            other = pltpu.roll(tile, 64, axis=1)
            for out in range(2):
                part = tile * straight[out][index] + other * crossed[out][index]
                result[out] = part if result[out] is None else result[out] + part
        for out in range(2):
            next_ref[:, at, out * 128 : (out + 1) * 128] = result[out]


def call(kernel, outs, scratch=(), name=None, final=False, far=()):
    kinds = [shape(o.shape, o.dtype) if final else pltpu.VMEM(o.shape, o.dtype) for o in outs]

    def run(*args):
        placed = [
            a if k in far else pltpu.with_memory_space_constraint(a, pltpu.VMEM)
            for k, a in enumerate(args)
        ]
        return pl.pallas_call(
            kernel,
            out_shape=kinds,
            in_specs=[pl.BlockSpec() if k in far else VMEM for k in range(len(args))],
            out_specs=[VMEM] * len(outs),
            scratch_shapes=list(scratch),
            name=name,
        )(*placed)

    return run


def shape(dims, kind):
    return jax.ShapeDtypeStruct(dims, kind)


def per_device(ahead_table, back_table, state_block, stored_fields, slope_fields, kernels, gains):
    lat_count, lon_count = lax.axis_size("lat"), lax.axis_size("lon")
    down = [(i, i + 1) for i in range(lat_count - 1)]
    up = [(i + 1, i) for i in range(lat_count - 1)]
    east = [(i, (i + 1) % lon_count) for i in range(lon_count)]
    width = LANES + LAYERS * CH

    both = jnp.concatenate([state_block.astype(BF16), slope_fields], axis=2)
    native = jnp.transpose(state_block, (1, 0, 2))
    (last,) = call(sides_kernel, [shape((ROWS, SIDE, width), BF16)], name="sides")(both)

    def toward(step):
        return [
            (lat * lon_count + lon, (lat + step) * lon_count + (lon + 1) % lon_count)
            for lat in range(lat_count)
            for lon in range(lon_count)
            if 0 <= lat + step < lat_count
        ]

    left = lax.ppermute(last, "lon", east)
    northwest = lax.ppermute(last, ("lat", "lon"), toward(1))
    southwest = lax.ppermute(last, ("lat", "lon"), toward(-1))
    above = lax.ppermute(both, "lat", down)
    below = lax.ppermute(both, "lat", up)
    ahead_weights, back_weights = call(
        weights_kernel,
        [
            shape((LAYERS * 3, 3 * 128, 128), BF16),
            shape((LAYERS * 3, 128, 3 * 128), BF16),
        ],
        name="weights",
    )(kernels.reshape(LAYERS * 9, CH, CH), last)

    place = lax.axis_index("lon")
    row_index = lax.axis_index("lat") * ROWS + place // 8
    area = jnp.cos(jnp.pi * ((row_index.astype(F32) + 0.5) / NLAT - 0.5))
    wave = jnp.arange(768)
    wave_weight = jnp.where((wave == 0) | (wave == NLON // 2), 1.0 / NLON, 2.0 / NLON)
    wave_weight = jnp.where(wave < WAVES, wave_weight, 0.0).astype(F32)
    columns = jnp.pad(gains, ((0, 0), (0, 768 - WAVES))).T * wave_weight[:, None]
    chosen = jnp.where(place % 2 == 0, columns[:, 0:SLOTS], columns[:, SLOTS : 2 * SLOTS])
    chosen = chosen * (area * area)
    weight = jnp.concatenate([chosen] * 4, axis=1)

    work = [
        pltpu.VMEM((FLAT, LANES), F32),
        pltpu.VMEM((FLAT, LANES), F32),
        pltpu.VMEM((EXT * PITCH, 3 * LANES), BF16),
    ]
    (packed,) = call(forward_kernel, [shape((32, 16, 128), BF16)], work, name="forward")(
        both, above, below, left, northwest, southwest, ahead_weights
    )
    circles = lax.all_to_all(packed, "lon", 0, 0, tiled=True)
    (known,) = call(
        stored_kernel, [shape((24, 24), F32)], [pltpu.VMEM((10, 24, 128), F32)], name="known"
    )(native, stored_fields, packed)
    (filtered,) = call(
        filter_kernel, [shape((32, 16, 128), BF16)], [pltpu.VMEM((768, 128), BF16)], name="spectral", far=(0, 1, 2)
    )(circles, ahead_table, back_table, weight, known)
    got = lax.all_to_all(filtered, "lon", 0, 0, tiled=True)
    gabove = lax.ppermute(got[8:32], "lat", down)
    gbelow = lax.ppermute(got[0:24], "lat", up)
    image, sums = call(
        adjoint_kernel,
        [shape((ROWS, COLS, LANES), F32), shape((8, 128), F32)],
        work + [pltpu.VMEM((12, 24, 128), F32)],
        name="adjoint",
        far=(0, 1, 2, 3, 4, 5, 6, 7, 11),
    )(
        native,
        stored_fields,
        both,
        above,
        below,
        left,
        northwest,
        southwest,
        got,
        gabove,
        gbelow,
        back_weights,
        known,
    )
    spread = lax.all_to_all(
        jnp.broadcast_to(sums, (lat_count, 8, 128)), "lat", 0, 0, tiled=True
    )
    partial = spread.sum(0)
    spread = lax.all_to_all(
        jnp.broadcast_to(partial, (lon_count, 8, 128)), "lon", 0, 0, tiled=True
    )
    following, diag, stored, factor = call(
        finish_kernel,
        [
            shape((COLS, ROWS, LANES), F32),
            shape((VECS, VECS), F32),
            shape((VECS, STORED), F32),
            shape((VECS, VECS), F32),
        ],
        name="finish",
        final=True,
    )(spread, native, stored_fields, image)
    return jnp.transpose(following, (1, 0, 2)), diag, stored.T, factor


def solution(mesh):
    ahead, back = tables()
    return jax.shard_map(
        functools.partial(per_device, jnp.asarray(ahead), jnp.asarray(back)),
        mesh=mesh,
        in_specs=(P("lat", "lon", None), P("lat", "lon", None), P("lat", "lon", None), P(), P()),
        out_specs=(P("lat", "lon", None), P(), P(), P()),
        check_vma=False,
    )
```

```python
import functools

import jax
import jax.numpy as jnp
import numpy as np
from jax import lax
from jax.experimental import pallas as pl
from jax.experimental.pallas import tpu as pltpu
from jax.sharding import PartitionSpec as P

F32 = jnp.float32
BF16 = jnp.bfloat16
HIGHEST = lax.Precision.HIGHEST

ROWS, COLS, CH, VECS, STORED, LAYERS = 4, 45, 64, 4, 16, 3
NLAT, NLON, WAVES = 64, 1440, 721
LANES = VECS * CH
HALO = 3
EXT = ROWS + 2 * HALO
PITCH = 64
LEAD = 8
SIDE = 8
FLAT = LEAD + EXT * PITCH + 8
SLOTS = 32
VMEM = pl.BlockSpec(memory_space=pltpu.VMEM)


def lane_ids(shape):
    return lax.broadcasted_iota(jnp.int32, shape, len(shape) - 1)


def row_ids(shape):
    return lax.broadcasted_iota(jnp.int32, shape, len(shape) - 2)


def tables():
    wave = 4 * np.arange(192)[None, :] + np.arange(4)[:, None]
    live = wave < WAVES
    q, t, j = np.meshgrid(np.arange(3), np.arange(8), np.arange(16), indexing="ij")
    slot = (16 * q + j).reshape(-1)
    point = (45 * t).reshape(-1) - 3 + slot
    angle = 2 * np.pi * ((wave[:, :, None] * point) % NLON) / NLON
    keep = live[:, :, None] & (slot < COLS)
    ahead = np.concatenate([np.cos(angle) * keep, np.sin(angle) * keep], axis=2)
    q, t, j = np.meshgrid(np.arange(4), np.arange(8), np.arange(16), indexing="ij")
    slot = (16 * q + j).reshape(-1)
    point = (45 * t).reshape(-1) - SIDE + slot
    angle = 2 * np.pi * ((wave[:, None, :] * point[None, :, None]) % NLON) / NLON
    held = (slot >= SIDE - HALO) & (slot < SIDE + COLS + HALO)
    keep = live[:, None, :] & held[None, :, None]
    back = np.concatenate([np.cos(angle) * keep, np.sin(angle) * keep], axis=2)
    return ahead.astype(jnp.bfloat16), back.astype(jnp.bfloat16)


def line_of(odd_ref, x_ref, near_ref, far_ref, row):
    if HALO <= row < HALO + ROWS:
        return x_ref[row - HALO].astype(F32)
    at = row + ROWS - HALO if row < HALO else row - HALO - ROWS
    near, far = near_ref[at].astype(F32), far_ref[at].astype(F32)
    odd = odd_ref[0] == 1
    return jnp.where(odd, near, far) if row < HALO else jnp.where(odd, far, near)


def sides_kernel(odd_ref, x_ref, near_ref, far_ref, last_ref):
    for row in range(EXT):
        line = line_of(odd_ref, x_ref, near_ref, far_ref, row)
        last_ref[row] = line[COLS - SIDE : COLS].astype(BF16)


def weights_kernel(taps_ref, after_ref, ahead_ref, back_ref):
    none = jnp.zeros((CH, CH), F32)
    for layer in range(LAYERS):
        for up in range(3):
            for side in range(3):
                block = taps_ref[9 * layer + 3 * up + side].astype(F32)
                pair = jnp.concatenate(
                    [
                        jnp.concatenate([block, none], axis=1),
                        jnp.concatenate([none, block], axis=1),
                    ],
                    axis=0,
                ).astype(BF16)
                ahead_ref[3 * layer + up, 128 * side : 128 * side + 128, :] = pair
                back_ref[3 * layer + 2 - up, :, 256 - 128 * side : 384 - 128 * side] = pair


def slope_lanes(slopes_ref, layer, start, count):
    pair = slopes_ref[pl.ds(start, count), (layer // 2) * 128 : (layer // 2) * 128 + 128]
    other = pltpu.roll(pair, 64, axis=1)
    low = lane_ids(pair.shape) < 64
    both = jnp.where(low, pair, other) if layer % 2 == 0 else jnp.where(low, other, pair)
    return jnp.concatenate([both, both], axis=1)


def convolve(field_ref, shifted_ref, weights_ref, layer, first, count, turned):
    have = (count + 2) * PITCH
    start = LEAD + (first - 1) * PITCH
    for pair in range(2):
        for step in range(3):
            at = 384 * pair + 128 * step
            shifted_ref[0:have, at : at + 128] = field_ref[
                pl.ds(start + step - 1, have), 128 * pair : 128 * pair + 128
            ].astype(BF16)
    halves = []
    for pair in range(2):
        total = None
        for step in range(3):
            part = lax.dot_general(
                shifted_ref[step * PITCH : (step + count) * PITCH, 384 * pair : 384 * pair + 384],
                weights_ref[layer * 3 + step],
                (((1,), (1 if turned else 0,)), ((), ())),
                preferred_element_type=F32,
            )
            total = part if total is None else total + part
        halves.append(total)
    return jnp.concatenate(halves, axis=1)


def parcel(slopes_ref, index):
    if index >= EXT * LAYERS:
        return jnp.zeros((16, SLOTS), F32)
    row, layer = index // LAYERS, index % LAYERS
    at = LEAD + row * PITCH + SIDE
    block = slopes_ref[at : at + 8, (layer // 2) * 128 : (layer // 2) * 128 + 128]
    base = 64 * (layer % 2)
    return jnp.concatenate(
        [
            jnp.zeros((8, SLOTS), F32),
            block[0:4, base : base + SLOTS],
            block[0:4, base + SLOTS : base + 2 * SLOTS],
        ],
        axis=0,
    )


def forward_kernel(
    odd_ref,
    x_ref,
    near_ref,
    far_ref,
    left_ref,
    weights_ref,
    send_ref,
    field_ref,
    slopes_ref,
    shifted_ref,
):
    field_ref[...] = jnp.zeros((FLAT, LANES), F32)
    slopes_ref[...] = jnp.zeros((FLAT, LANES), F32)
    for row in range(EXT):
        at = LEAD + row * PITCH
        line = line_of(odd_ref, x_ref, near_ref, far_ref, row)
        side = left_ref[row].astype(F32)
        field_ref[at : at + SIDE, :] = side[:, 0:LANES]
        field_ref[at + SIDE : at + SIDE + COLS, :] = line[:, 0:LANES]
        slopes_ref[at : at + SIDE, 0:192] = side[:, LANES:]
        slopes_ref[at + SIDE : at + SIDE + COLS, 0:192] = line[:, LANES:]
    for layer in range(LAYERS):
        first = layer + 1
        count = EXT - 2 * first
        total = convolve(field_ref, shifted_ref, weights_ref, layer, first, count, False)
        start = LEAD + first * PITCH
        total = total * slope_lanes(slopes_ref, layer, start, count * PITCH)
        field_ref[start : start + count * PITCH, :] = total.astype(BF16).astype(F32)
    for row in range(ROWS):
        line = field_ref[pl.ds(LEAD + (HALO + row) * PITCH + SIDE - HALO, 48), :]
        for group in range(8):
            pieces = [
                line[16 * q : 16 * q + 16, group * SLOTS : (group + 1) * SLOTS] for q in range(3)
            ]
            pieces.append(parcel(slopes_ref, row * 8 + group))
            send_ref[row * 8 + group] = jnp.concatenate(pieces, axis=1).astype(BF16)


def filter_kernel(
    got_ref, ahead_ref, back_ref, gains_ref, known_ref, send_ref, work_ref
):
    quarter = [
        got_ref[8 * part : 8 * part + 8].astype(F32).reshape(128, 128) for part in range(4)
    ]
    even, odd = quarter[0] + quarter[2], quarter[1] + quarter[3]
    across, along = quarter[0] - quarter[2], quarter[1] - quarter[3]
    real = [even + odd, across, even - odd, across]
    imag = [None, -along, None, along]
    low = lane_ids((128, 128)) < SLOTS

    def turn(value, shift):
        return value if shift % 128 == 0 else pltpu.roll(value, shift % 128, axis=1)

    for kind in range(4):
        for q in range(3):
            a = real[kind]
            b = imag[kind]
            left, right = turn(a, -SLOTS * q), turn(a, SLOTS - SLOTS * q)
            if b is None:
                top = jnp.where(low, left, 0.0)
                bottom = jnp.where(low, 0.0, -right)
            else:
                top = jnp.where(low, left, turn(b, SLOTS - SLOTS * q))
                bottom = jnp.where(low, turn(b, -SLOTS * q), -right)
            work_ref[128 * q : 128 * q + 128, :] = top.astype(BF16)
            work_ref[384 + 128 * q : 512 + 128 * q, :] = bottom.astype(BF16)
        spectrum = jnp.dot(ahead_ref[kind], work_ref[...], preferred_element_type=F32)
        weight = gains_ref[pl.ds(kind, 192, stride=4), :]
        spectrum = spectrum * weight
        below = jnp.where(
            lane_ids((192, 128)) < SLOTS, -turn(spectrum, -SLOTS), turn(spectrum, SLOTS)
        )
        packed = jnp.concatenate([spectrum, below], axis=0).astype(BF16)
        part = jnp.dot(back_ref[kind], packed, preferred_element_type=F32)
        if kind == 0:
            zero = part
        elif kind == 1:
            one = part
        elif kind == 2:
            two = part
        else:
            three = part
    plus, minus = zero + two, zero - two
    swing = one + three
    turned = turn(three - one, -SLOTS)
    result = [plus + swing, minus + turned, plus - swing, minus - turned]
    lane = lane_ids((128, 128))
    for part in range(4):
        packed = result[part][0:128]
        for q in range(1, 4):
            packed = jnp.where(
                lane >= SLOTS * q, turn(result[part][128 * q : 128 * q + 128], SLOTS * q), packed
            )
        if part < 3:
            passing = got_ref[8 * part + 1 : 8 * part + 9]
        else:
            passing = jnp.concatenate([got_ref[25:32], got_ref[0:1]], axis=0)
        carried = (lane >= 96) & (row_ids((128, 128)) % 16 >= 8)
        packed = jnp.where(carried, passing.astype(F32).reshape(128, 128), packed)
        send_ref[8 * part : 8 * part + 8] = packed.reshape(8, 16, 128).astype(BF16)


def twice(tile, half):
    other = pltpu.roll(tile, 64, axis=1)
    low = lane_ids(tile.shape) < 64
    return jnp.where(low, tile, other) if half == 0 else jnp.where(low, other, tile)


def gram_rows(rows_ref):
    wide = (24, rows_ref.shape[1])
    pick = (row_ids(wide) == lane_ids(wide) // 64).astype(F32)
    return lax.dot_general(
        pick,
        rows_ref[...],
        (((1,), (1,)), ((), ())),
        precision=HIGHEST,
        preferred_element_type=F32,
    )


def stored_kernel(q_ref, p_ref, after_ref, out_ref, rows_ref):
    rows_ref[...] = jnp.zeros(rows_ref.shape, F32)
    known = 10
    for right in range(known):
        for half in range(2):
            totals = [None] * (right + 1)
            for row in range(ROWS):
                tile = tile_of(q_ref, p_ref, None, row, right)
                doubled = twice(tile, half)
                for left in range(right + 1):
                    product = tile_of(q_ref, p_ref, None, row, left) * doubled
                    totals[left] = product if totals[left] is None else totals[left] + product
            for left in range(right + 1):
                rows_ref[2 * right + half : 2 * right + half + 1, 128 * left : 128 * left + 128] = jnp.sum(
                    totals[left], axis=0, keepdims=True
                )
    out_ref[...] = gram_rows(rows_ref)


def tile_of(q_ref, p_ref, u_ref, row, index):
    if index < 2:
        return q_ref[:, row, index * 128 : (index + 1) * 128]
    if index < 10:
        return p_ref[row, :, (index - 2) * 128 : (index - 1) * 128].astype(F32)
    return u_ref[row, :, (index - 10) * 128 : (index - 9) * 128]


def adjoint_kernel(
    odd_ref,
    q_ref,
    p_ref,
    x_ref,
    near_ref,
    far_ref,
    left_ref,
    got_ref,
    gnear_ref,
    gfar_ref,
    weights_ref,
    known_ref,
    u_ref,
    sums_ref,
    field_ref,
    slopes_ref,
    shifted_ref,
    rows_ref,
):
    field_ref[0:LEAD, :] = jnp.zeros((LEAD, LANES), F32)
    field_ref[FLAT - 8 : FLAT, :] = jnp.zeros((8, LANES), F32)
    slopes_ref[...] = jnp.zeros((FLAT, LANES), F32)
    for row in range(EXT):
        at = LEAD + row * PITCH
        line = line_of(odd_ref, x_ref, near_ref, far_ref, row)
        slopes_ref[at : at + SIDE, 0:192] = left_ref[row, :, LANES:].astype(F32)
        slopes_ref[at + SIDE : at + SIDE + COLS, 0:192] = line[:, LANES:]
        halves = []
        for layer in range(LAYERS):
            block = got_ref[LAYERS * row + layer].astype(F32)
            halves += [block[8:12, 96:128], block[12:16, 96:128]]
        slopes_ref[at + SIDE + COLS : at + SIDE + COLS + 4, 0:192] = jnp.concatenate(halves, axis=1)
    for row in range(EXT):
        at = LEAD + row * PITCH
        if HALO <= row < HALO + ROWS:
            base = (row - HALO) * 8
            blocks = [got_ref[base + group].astype(F32) for group in range(8)]
        else:
            base = (row + 1) * 8 if row < HALO else (row - HALO - ROWS) * 8
            odd = odd_ref[0] == 1
            blocks = []
            for group in range(8):
                near = gnear_ref[base + group].astype(F32)
                far = gfar_ref[base + group].astype(F32)
                first, second = (near, far) if row < HALO else (far, near)
                blocks.append(jnp.where(odd, first, second))
        for q in range(4):
            field_ref[at + 16 * q : at + 16 * q + 16, :] = jnp.concatenate(
                [block[:, q * SLOTS : (q + 1) * SLOTS] for block in blocks], axis=1
            )
    top = field_ref[LEAD : LEAD + EXT * PITCH, :] * slope_lanes(
        slopes_ref, LAYERS - 1, LEAD, EXT * PITCH
    )
    field_ref[LEAD : LEAD + EXT * PITCH, :] = top.astype(BF16).astype(F32)
    for layer in range(LAYERS - 1, -1, -1):
        first = LAYERS - layer
        count = EXT - 2 * first
        total = convolve(field_ref, shifted_ref, weights_ref, layer, first, count, True)
        start = LEAD + first * PITCH
        if layer > 0:
            total = total * slope_lanes(slopes_ref, layer - 1, start, count * PITCH)
            total = total.astype(BF16).astype(F32)
        field_ref[start : start + count * PITCH, :] = total
    for row in range(ROWS):
        u_ref[row] = field_ref[pl.ds(LEAD + (HALO + row) * PITCH + SIDE, COLS), :]
    rows_ref[...] = jnp.zeros(rows_ref.shape, F32)
    for right in range(2):
        for half in range(2):
            totals = [None] * 12
            for row in range(ROWS):
                doubled = twice(tile_of(q_ref, p_ref, u_ref, row, 10 + right), half)
                for left in range(12):
                    product = tile_of(q_ref, p_ref, u_ref, row, left) * doubled
                    totals[left] = product if totals[left] is None else totals[left] + product
            for left in range(12):
                at = 2 * right + half
                rows_ref[at : at + 1, 128 * left : 128 * left + 128] = jnp.sum(
                    totals[left], axis=0, keepdims=True
                )
    gram = gram_rows(rows_ref)[:, 0:VECS]
    wide = jnp.concatenate(
        [known_ref[:, 0:20], gram, jnp.zeros((24, 128 - 24), F32)], axis=1
    )
    sums_ref[...] = (
        wide[0:8]
        + pltpu.roll(wide[8:16], SLOTS, axis=1)
        + pltpu.roll(wide[16:24], 2 * SLOTS, axis=1)
    )


def finish_kernel(sums_ref, q_ref, p_ref, u_ref, next_ref, diag_ref, stored_ref, factor_ref):
    total = sums_ref[0]
    for index in range(1, sums_ref.shape[0]):
        total = total + sums_ref[index]
    total = total * (1.0 / (NLAT * NLON * CH))
    narrow = lane_ids((8, 128)) < SLOTS
    blocks = [
        jnp.where(narrow, total if k == 0 else pltpu.roll(total, 128 - SLOTS * k, axis=1), 0.0)
        for k in range(3)
    ]
    square = (128, 128)
    half = jnp.concatenate(blocks + [jnp.zeros((104, 128), F32)], axis=0)
    row, lane = row_ids(square), lane_ids(square)
    gram = jnp.where(row <= lane, half, jnp.transpose(half))
    known = VECS + STORED
    image = pltpu.roll(gram, 128 - known, axis=1)
    keep = lane < VECS
    coef = jnp.where(
        keep & (row < known), -image, jnp.where(keep & (row == lane + known), 1.0, 0.0)
    )
    diag_ref[...] = image[0:VECS, 0:VECS]
    stored_ref[...] = jnp.transpose(image)[0:VECS, VECS:known]
    applied = jnp.dot(gram, coef, precision=HIGHEST, preferred_element_type=F32)
    small = lax.dot_general(
        coef, applied, (((0,), (0,)), ((), ())), precision=HIGHEST, preferred_element_type=F32
    )
    entry = [[small[i : i + 1, j : j + 1] for j in range(VECS)] for i in range(VECS)]
    factor = [[None] * VECS for _ in range(VECS)]
    for i in range(VECS):
        value = entry[i][i]
        for k in range(i):
            value = value - factor[k][i] * factor[k][i]
        factor[i][i] = jnp.sqrt(value)
        for j in range(i + 1, VECS):
            value = entry[i][j]
            for k in range(i):
                value = value - factor[k][i] * factor[k][j]
            factor[i][j] = value / factor[i][i]
    inverse = [[None] * VECS for _ in range(VECS)]
    for j in range(VECS):
        inverse[j][j] = 1.0 / factor[j][j]
        for i in range(j - 1, -1, -1):
            value = None
            for k in range(i + 1, j + 1):
                term = factor[i][k] * inverse[k][j]
                value = term if value is None else value + term
            inverse[i][j] = -value / factor[i][i]
    upper = jnp.zeros(square, F32)
    solved = jnp.zeros(square, F32)
    for i in range(VECS):
        for j in range(i, VECS):
            here = (row == i) & (lane == j)
            upper = jnp.where(here, factor[i][j], upper)
            solved = jnp.where(here, inverse[i][j], solved)
    factor_ref[...] = upper[0:VECS, 0:VECS]
    mixed = jnp.dot(coef, solved, precision=HIGHEST, preferred_element_type=F32)
    low = lane_ids((1, 128)) < 64
    straight, crossed = [], []
    for out in range(2):
        choose = (row == 2 * out + lane // 64).astype(F32)
        lines = jnp.dot(mixed, choose, precision=HIGHEST, preferred_element_type=F32)
        straight.append([])
        crossed.append([])
        for index in range(12):
            a = lines[2 * index : 2 * index + 1]
            b = lines[2 * index + 1 : 2 * index + 2]
            straight[out].append(jnp.where(low, a, b))
            crossed[out].append(jnp.where(low, b, a))
    for at in range(ROWS):
        result = [None, None]
        for index in range(12):
            tile = tile_of(q_ref, p_ref, u_ref, at, index)
            other = pltpu.roll(tile, 64, axis=1)
            for out in range(2):
                part = tile * straight[out][index] + other * crossed[out][index]
                result[out] = part if result[out] is None else result[out] + part
        for out in range(2):
            next_ref[:, at, out * 128 : (out + 1) * 128] = result[out]


def call(kernel, outs, scratch=(), final=False, far=()):
    kinds = [shape(o.shape, o.dtype) if final else pltpu.VMEM(o.shape, o.dtype) for o in outs]

    def run(*args):
        placed, specs = [], []
        for index, value in enumerate(args):
            if value.dtype == jnp.int32:
                specs.append(pl.BlockSpec(memory_space=pltpu.SMEM))
            elif index in far:
                specs.append(pl.BlockSpec())
            else:
                specs.append(VMEM)
                value = pltpu.with_memory_space_constraint(value, pltpu.VMEM)
            placed.append(value)
        return pl.pallas_call(
            kernel,
            out_shape=kinds,
            in_specs=specs,
            out_specs=[VMEM] * len(outs),
            scratch_shapes=list(scratch),
        )(*placed)

    return run


def shape(dims, kind):
    return jax.ShapeDtypeStruct(dims, kind)


def per_device(ahead_table, back_table, state_block, stored_fields, slope_fields, kernels, gains):
    lat_count, lon_count = lax.axis_size("lat"), lax.axis_size("lon")
    near_pairs = [(i, i ^ 1) for i in range(lat_count)]
    far_pairs = [(i, i + 1) for i in range(1, lat_count - 1, 2)]
    far_pairs = far_pairs + [(b, a) for a, b in far_pairs]
    east = [(i, (i + 1) % lon_count) for i in range(lon_count)]
    width = LANES + LAYERS * CH

    both = jnp.concatenate([state_block.astype(BF16), slope_fields], axis=2)
    native = jnp.transpose(state_block, (1, 0, 2))
    parity = lax.axis_index("lat") % 2
    odd = jnp.full((1,), parity, jnp.int32)
    far = lax.ppermute(both, "lat", far_pairs)
    near = lax.ppermute(both, "lat", near_pairs)
    (last,) = call(sides_kernel, [shape((EXT, SIDE, width), BF16)])(odd, both, near, far)
    left = lax.ppermute(last, "lon", east)
    ahead_weights, back_weights = call(
        weights_kernel,
        [
            shape((LAYERS * 3, 3 * 128, 128), BF16),
            shape((LAYERS * 3, 128, 3 * 128), BF16),
        ],
    )(kernels.reshape(LAYERS * 9, CH, CH), last)

    place = lax.axis_index("lon")
    row_index = lax.axis_index("lat") * ROWS + place // 8
    area = jnp.cos(jnp.pi * ((row_index.astype(F32) + 0.5) / NLAT - 0.5))
    wave = jnp.arange(768)
    wave_weight = jnp.where((wave == 0) | (wave == NLON // 2), 1.0 / NLON, 2.0 / NLON)
    wave_weight = jnp.where(wave < WAVES, wave_weight, 0.0).astype(F32)
    columns = jnp.pad(gains, ((0, 0), (0, 768 - WAVES))).T * wave_weight[:, None]
    chosen = jnp.where(place % 2 == 0, columns[:, 0:SLOTS], columns[:, SLOTS : 2 * SLOTS])
    chosen = chosen * (area * area)
    weight = jnp.concatenate([chosen] * 4, axis=1)

    work = [
        pltpu.VMEM((FLAT, LANES), F32),
        pltpu.VMEM((FLAT, LANES), F32),
        pltpu.VMEM((EXT * PITCH, 3 * LANES), BF16),
    ]
    (packed,) = call(forward_kernel, [shape((32, 16, 128), BF16)], work)(
        odd, both, near, far, left, ahead_weights
    )
    circles = lax.all_to_all(packed, "lon", 0, 0, tiled=True)
    (known,) = call(
        stored_kernel, [shape((24, 24), F32)], [pltpu.VMEM((24, 10 * 128), F32)]
    )(native, stored_fields, packed)
    (filtered,) = call(
        filter_kernel, [shape((32, 16, 128), BF16)], [pltpu.VMEM((768, 128), BF16)], far=(0, 1, 2)
    )(circles, ahead_table, back_table, weight, known)
    got = lax.all_to_all(filtered, "lon", 0, 0, tiled=True)
    gfar = lax.ppermute(got, "lat", far_pairs)
    gnear = lax.ppermute(got, "lat", near_pairs)
    image, sums = call(
        adjoint_kernel,
        [shape((ROWS, COLS, LANES), F32), shape((8, 128), F32)],
        work + [pltpu.VMEM((8, 12 * 128), F32)],
        far=(1, 2, 3, 4, 5, 6, 10),
    )(
        odd,
        native,
        stored_fields,
        both,
        near,
        far,
        left,
        got,
        gnear,
        gfar,
        back_weights,
        known,
    )
    spread = lax.all_to_all(
        jnp.broadcast_to(sums, (lat_count, 8, 128)), "lat", 0, 0, tiled=True
    )
    partial = spread.sum(0)
    spread = lax.all_to_all(
        jnp.broadcast_to(partial, (lon_count, 8, 128)), "lon", 0, 0, tiled=True
    )
    following, diag, stored, factor = call(
        finish_kernel,
        [
            shape((COLS, ROWS, LANES), F32),
            shape((VECS, VECS), F32),
            shape((VECS, STORED), F32),
            shape((VECS, VECS), F32),
        ],
        final=True,
    )(spread, native, stored_fields, image)
    return jnp.transpose(following, (1, 0, 2)), diag, stored.T, factor


def solution(mesh):
    ahead, back = tables()
    return jax.shard_map(
        functools.partial(per_device, jnp.asarray(ahead), jnp.asarray(back)),
        mesh=mesh,
        in_specs=(P("lat", "lon", None), P("lat", "lon", None), P("lat", "lon", None), P(), P()),
        out_specs=(P("lat", "lon", None), P(), P(), P()),
        check_vma=False,
    )
```

```python
import functools

import jax
import jax.numpy as jnp
import numpy as np
from jax import lax
from jax.experimental import pallas as pl
from jax.experimental.pallas import tpu as pltpu
from jax.sharding import PartitionSpec as P

F32 = jnp.float32
BF16 = jnp.bfloat16
HIGHEST = lax.Precision.HIGHEST

ROWS, COLS, CH, VECS, STORED, LAYERS = 4, 45, 64, 4, 16, 3
NLAT, NLON, WAVES = 64, 1440, 721
LANES = VECS * CH
HALO = 3
EXT = ROWS + 2 * HALO
PITCH = 64
LEAD = 8
SIDE = 8
FLAT = LEAD + EXT * PITCH + 8
SLOTS = 32
VMEM = pl.BlockSpec(memory_space=pltpu.VMEM)


def lane_ids(shape):
    return lax.broadcasted_iota(jnp.int32, shape, len(shape) - 1)


def row_ids(shape):
    return lax.broadcasted_iota(jnp.int32, shape, len(shape) - 2)


def tables():
    wave = 4 * np.arange(192)[None, :] + np.arange(4)[:, None]
    live = wave < WAVES
    q, t, j = np.meshgrid(np.arange(3), np.arange(8), np.arange(16), indexing="ij")
    slot = (16 * q + j).reshape(-1)
    point = (45 * t).reshape(-1) - 3 + slot
    angle = 2 * np.pi * ((wave[:, :, None] * point) % NLON) / NLON
    keep = live[:, :, None] & (slot < COLS)
    ahead = np.concatenate([np.cos(angle) * keep, np.sin(angle) * keep], axis=2)
    q, t, j = np.meshgrid(np.arange(4), np.arange(8), np.arange(16), indexing="ij")
    slot = (16 * q + j).reshape(-1)
    point = (45 * t).reshape(-1) - SIDE + slot
    angle = 2 * np.pi * ((wave[:, None, :] * point[None, :, None]) % NLON) / NLON
    held = (slot >= SIDE - HALO) & (slot < SIDE + COLS + HALO)
    keep = live[:, None, :] & held[None, :, None]
    back = np.concatenate([np.cos(angle) * keep, np.sin(angle) * keep], axis=2)
    return ahead.astype(jnp.bfloat16), back.astype(jnp.bfloat16)


def pack_kernel(q_ref, s_ref, out_ref):
    slopes = s_ref[...].astype(F32)
    for row in range(ROWS):
        out_ref[row, :, 0:LANES] = q_ref[:, row, :].astype(BF16)
        out_ref[row, :, LANES:] = slopes[:, row, :].astype(BF16)


def line_of(odd_ref, x_ref, near_ref, far_ref, row):
    if HALO <= row < HALO + ROWS:
        return x_ref[row - HALO].astype(F32)
    at = row + ROWS - HALO if row < HALO else row - HALO - ROWS
    near, far = near_ref[at].astype(F32), far_ref[at].astype(F32)
    odd = odd_ref[0] == 1
    return jnp.where(odd, near, far) if row < HALO else jnp.where(odd, far, near)


def sides_kernel(odd_ref, x_ref, near_ref, far_ref, last_ref):
    for row in range(EXT):
        line = line_of(odd_ref, x_ref, near_ref, far_ref, row)
        last_ref[row] = line[COLS - SIDE : COLS].astype(BF16)


def weights_kernel(taps_ref, after_ref, ahead_ref, back_ref):
    none = jnp.zeros((CH, CH), F32)
    for layer in range(LAYERS):
        for up in range(3):
            for side in range(3):
                block = taps_ref[9 * layer + 3 * up + side].astype(F32)
                pair = jnp.concatenate(
                    [
                        jnp.concatenate([block, none], axis=1),
                        jnp.concatenate([none, block], axis=1),
                    ],
                    axis=0,
                ).astype(BF16)
                ahead_ref[3 * layer + up, 128 * side : 128 * side + 128, :] = pair
                back_ref[3 * layer + 2 - up, :, 256 - 128 * side : 384 - 128 * side] = pair


def slope_lanes(slopes_ref, layer, start, count):
    pair = slopes_ref[pl.ds(start, count), (layer // 2) * 128 : (layer // 2) * 128 + 128]
    other = pltpu.roll(pair, 64, axis=1)
    low = lane_ids(pair.shape) < 64
    both = jnp.where(low, pair, other) if layer % 2 == 0 else jnp.where(low, other, pair)
    return jnp.concatenate([both, both], axis=1)


def convolve(field_ref, shifted_ref, weights_ref, layer, first, count, turned):
    have = (count + 2) * PITCH
    start = LEAD + (first - 1) * PITCH
    for pair in range(2):
        for step in range(3):
            at = 384 * pair + 128 * step
            shifted_ref[0:have, at : at + 128] = field_ref[
                pl.ds(start + step - 1, have), 128 * pair : 128 * pair + 128
            ].astype(BF16)
    halves = []
    for pair in range(2):
        total = None
        for step in range(3):
            part = lax.dot_general(
                shifted_ref[step * PITCH : (step + count) * PITCH, 384 * pair : 384 * pair + 384],
                weights_ref[layer * 3 + step],
                (((1,), (1 if turned else 0,)), ((), ())),
                preferred_element_type=F32,
            )
            total = part if total is None else total + part
        halves.append(total)
    return jnp.concatenate(halves, axis=1)


def parcel(slopes_ref, index):
    if index >= EXT * LAYERS:
        return jnp.zeros((16, SLOTS), F32)
    row, layer = index // LAYERS, index % LAYERS
    at = LEAD + row * PITCH + SIDE
    block = slopes_ref[at : at + 8, (layer // 2) * 128 : (layer // 2) * 128 + 128]
    base = 64 * (layer % 2)
    return jnp.concatenate(
        [
            jnp.zeros((8, SLOTS), F32),
            block[0:4, base : base + SLOTS],
            block[0:4, base + SLOTS : base + 2 * SLOTS],
        ],
        axis=0,
    )


def forward_kernel(
    odd_ref,
    x_ref,
    near_ref,
    far_ref,
    left_ref,
    weights_ref,
    send_ref,
    field_ref,
    slopes_ref,
    shifted_ref,
):
    field_ref[...] = jnp.zeros((FLAT, LANES), F32)
    slopes_ref[...] = jnp.zeros((FLAT, LANES), F32)
    for row in range(EXT):
        at = LEAD + row * PITCH
        line = line_of(odd_ref, x_ref, near_ref, far_ref, row)
        side = left_ref[row].astype(F32)
        field_ref[at : at + SIDE, :] = side[:, 0:LANES]
        field_ref[at + SIDE : at + SIDE + COLS, :] = line[:, 0:LANES]
        slopes_ref[at : at + SIDE, 0:192] = side[:, LANES:]
        slopes_ref[at + SIDE : at + SIDE + COLS, 0:192] = line[:, LANES:]
    for layer in range(LAYERS):
        first = layer + 1
        count = EXT - 2 * first
        total = convolve(field_ref, shifted_ref, weights_ref, layer, first, count, False)
        start = LEAD + first * PITCH
        total = total * slope_lanes(slopes_ref, layer, start, count * PITCH)
        field_ref[start : start + count * PITCH, :] = total.astype(BF16).astype(F32)
    for row in range(ROWS):
        line = field_ref[pl.ds(LEAD + (HALO + row) * PITCH + SIDE - HALO, 48), :]
        for group in range(8):
            pieces = [
                line[16 * q : 16 * q + 16, group * SLOTS : (group + 1) * SLOTS] for q in range(3)
            ]
            pieces.append(parcel(slopes_ref, row * 8 + group))
            send_ref[row * 8 + group] = jnp.concatenate(pieces, axis=1).astype(BF16)


def filter_kernel(
    got_ref,
    ahead_far,
    back_far,
    gains_ref,
    known_ref,
    send_ref,
    work_ref,
    ahead_ref,
    back_ref,
    arrived,
):
    loads = []
    for kind in range(4):
        for index, (far, here) in enumerate(((ahead_far, ahead_ref), (back_far, back_ref))):
            load = pltpu.make_async_copy(far.at[kind], here.at[kind], arrived.at[2 * kind + index])
            load.start()
            loads.append(load)
    quarter = [
        got_ref[8 * part : 8 * part + 8].astype(F32).reshape(128, 128) for part in range(4)
    ]
    even, odd = quarter[0] + quarter[2], quarter[1] + quarter[3]
    across, along = quarter[0] - quarter[2], quarter[1] - quarter[3]
    real = [even + odd, across, even - odd, across]
    imag = [None, -along, None, along]
    low = lane_ids((128, 128)) < SLOTS

    def turn(value, shift):
        return value if shift % 128 == 0 else pltpu.roll(value, shift % 128, axis=1)

    for kind in range(4):
        for q in range(3):
            a = real[kind]
            b = imag[kind]
            left, right = turn(a, -SLOTS * q), turn(a, SLOTS - SLOTS * q)
            if b is None:
                top = jnp.where(low, left, 0.0)
                bottom = jnp.where(low, 0.0, -right)
            else:
                top = jnp.where(low, left, turn(b, SLOTS - SLOTS * q))
                bottom = jnp.where(low, turn(b, -SLOTS * q), -right)
            work_ref[kind, 128 * q : 128 * q + 128, :] = top.astype(BF16)
            work_ref[kind, 384 + 128 * q : 512 + 128 * q, :] = bottom.astype(BF16)
    for load in loads:
        load.wait()
    for kind in range(4):
        spectrum = jnp.dot(ahead_ref[kind], work_ref[kind], preferred_element_type=F32)
        weight = gains_ref[pl.ds(kind, 192, stride=4), :]
        spectrum = spectrum * weight
        below = jnp.where(
            lane_ids((192, 128)) < SLOTS, -turn(spectrum, -SLOTS), turn(spectrum, SLOTS)
        )
        packed = jnp.concatenate([spectrum, below], axis=0).astype(BF16)
        part = jnp.dot(back_ref[kind], packed, preferred_element_type=F32)
        if kind == 0:
            zero = part
        elif kind == 1:
            one = part
        elif kind == 2:
            two = part
        else:
            three = part
    plus, minus = zero + two, zero - two
    swing = one + three
    turned = turn(three - one, -SLOTS)
    result = [plus + swing, minus + turned, plus - swing, minus - turned]
    lane = lane_ids((128, 128))
    for part in range(4):
        packed = result[part][0:128]
        for q in range(1, 4):
            packed = jnp.where(
                lane >= SLOTS * q, turn(result[part][128 * q : 128 * q + 128], SLOTS * q), packed
            )
        if part < 3:
            passing = got_ref[8 * part + 1 : 8 * part + 9]
        else:
            passing = jnp.concatenate([got_ref[25:32], got_ref[0:1]], axis=0)
        carried = (lane >= 96) & (row_ids((128, 128)) % 16 >= 8)
        packed = jnp.where(carried, passing.astype(F32).reshape(128, 128), packed)
        send_ref[8 * part : 8 * part + 8] = packed.reshape(8, 16, 128).astype(BF16)


def twice(tile, half):
    other = pltpu.roll(tile, 64, axis=1)
    low = lane_ids(tile.shape) < 64
    return jnp.where(low, tile, other) if half == 0 else jnp.where(low, other, tile)


def gram_rows(rows_ref):
    wide = (24, rows_ref.shape[1])
    pick = (row_ids(wide) == lane_ids(wide) // 64).astype(F32)
    return lax.dot_general(
        pick,
        rows_ref[...],
        (((1,), (1,)), ((), ())),
        precision=HIGHEST,
        preferred_element_type=F32,
    )


def stored_kernel(q_ref, p_ref, after_ref, out_ref, rows_ref):
    rows_ref[...] = jnp.zeros(rows_ref.shape, F32)
    known = 10
    for right in range(known):
        for half in range(2):
            totals = [None] * (right + 1)
            for row in range(ROWS):
                tile = tile_of(q_ref, p_ref, None, row, right)
                doubled = twice(tile, half)
                for left in range(right + 1):
                    product = tile_of(q_ref, p_ref, None, row, left) * doubled
                    totals[left] = product if totals[left] is None else totals[left] + product
            for left in range(right + 1):
                rows_ref[2 * right + half : 2 * right + half + 1, 128 * left : 128 * left + 128] = jnp.sum(
                    totals[left], axis=0, keepdims=True
                )
    out_ref[...] = gram_rows(rows_ref)


def tile_of(q_ref, p_ref, u_ref, row, index):
    if index < 2:
        return q_ref[:, row, index * 128 : (index + 1) * 128]
    if index < 10:
        return p_ref[row, :, (index - 2) * 128 : (index - 1) * 128].astype(F32)
    return u_ref[row, :, (index - 10) * 128 : (index - 9) * 128]


def adjoint_kernel(
    odd_ref,
    q_ref,
    p_ref,
    x_ref,
    near_ref,
    far_ref,
    left_ref,
    got_ref,
    gnear_ref,
    gfar_ref,
    weights_ref,
    known_ref,
    u_ref,
    sums_ref,
    field_ref,
    slopes_ref,
    shifted_ref,
    rows_ref,
):
    field_ref[0:LEAD, :] = jnp.zeros((LEAD, LANES), F32)
    field_ref[FLAT - 8 : FLAT, :] = jnp.zeros((8, LANES), F32)
    slopes_ref[...] = jnp.zeros((FLAT, LANES), F32)
    for row in range(EXT):
        at = LEAD + row * PITCH
        line = line_of(odd_ref, x_ref, near_ref, far_ref, row)
        slopes_ref[at : at + SIDE, 0:192] = left_ref[row, :, LANES:].astype(F32)
        slopes_ref[at + SIDE : at + SIDE + COLS, 0:192] = line[:, LANES:]
        halves = []
        for layer in range(LAYERS):
            block = got_ref[LAYERS * row + layer].astype(F32)
            halves += [block[8:12, 96:128], block[12:16, 96:128]]
        slopes_ref[at + SIDE + COLS : at + SIDE + COLS + 4, 0:192] = jnp.concatenate(halves, axis=1)
    for row in range(EXT):
        at = LEAD + row * PITCH
        if HALO <= row < HALO + ROWS:
            base = (row - HALO) * 8
            blocks = [got_ref[base + group].astype(F32) for group in range(8)]
        else:
            base = (row + 1) * 8 if row < HALO else (row - HALO - ROWS) * 8
            odd = odd_ref[0] == 1
            blocks = []
            for group in range(8):
                near = gnear_ref[base + group].astype(F32)
                far = gfar_ref[base + group].astype(F32)
                first, second = (near, far) if row < HALO else (far, near)
                blocks.append(jnp.where(odd, first, second))
        for q in range(4):
            field_ref[at + 16 * q : at + 16 * q + 16, :] = jnp.concatenate(
                [block[:, q * SLOTS : (q + 1) * SLOTS] for block in blocks], axis=1
            )
    top = field_ref[LEAD : LEAD + EXT * PITCH, :] * slope_lanes(
        slopes_ref, LAYERS - 1, LEAD, EXT * PITCH
    )
    field_ref[LEAD : LEAD + EXT * PITCH, :] = top.astype(BF16).astype(F32)
    for layer in range(LAYERS - 1, -1, -1):
        first = LAYERS - layer
        count = EXT - 2 * first
        total = convolve(field_ref, shifted_ref, weights_ref, layer, first, count, True)
        start = LEAD + first * PITCH
        if layer > 0:
            total = total * slope_lanes(slopes_ref, layer - 1, start, count * PITCH)
            total = total.astype(BF16).astype(F32)
        field_ref[start : start + count * PITCH, :] = total
    for row in range(ROWS):
        u_ref[row] = field_ref[pl.ds(LEAD + (HALO + row) * PITCH + SIDE, COLS), :]
    rows_ref[...] = jnp.zeros(rows_ref.shape, F32)
    for right in range(2):
        for half in range(2):
            totals = [None] * 12
            for row in range(ROWS):
                doubled = twice(tile_of(q_ref, p_ref, u_ref, row, 10 + right), half)
                for left in range(12):
                    product = tile_of(q_ref, p_ref, u_ref, row, left) * doubled
                    totals[left] = product if totals[left] is None else totals[left] + product
            for left in range(12):
                at = 2 * right + half
                rows_ref[at : at + 1, 128 * left : 128 * left + 128] = jnp.sum(
                    totals[left], axis=0, keepdims=True
                )
    gram = gram_rows(rows_ref)[:, 0:VECS]
    wide = jnp.concatenate(
        [known_ref[:, 0:20], gram, jnp.zeros((24, 128 - 24), F32)], axis=1
    )
    sums_ref[...] = (
        wide[0:8]
        + pltpu.roll(wide[8:16], SLOTS, axis=1)
        + pltpu.roll(wide[16:24], 2 * SLOTS, axis=1)
    )


def finish_kernel(sums_ref, q_ref, p_ref, u_ref, next_ref, diag_ref, stored_ref, factor_ref):
    total = sums_ref[0]
    for index in range(1, sums_ref.shape[0]):
        total = total + sums_ref[index]
    total = total * (1.0 / (NLAT * NLON * CH))
    narrow = lane_ids((8, 128)) < SLOTS
    blocks = [
        jnp.where(narrow, total if k == 0 else pltpu.roll(total, 128 - SLOTS * k, axis=1), 0.0)
        for k in range(3)
    ]
    square = (128, 128)
    half = jnp.concatenate(blocks + [jnp.zeros((104, 128), F32)], axis=0)
    row, lane = row_ids(square), lane_ids(square)
    gram = jnp.where(row <= lane, half, jnp.transpose(half))
    known = VECS + STORED
    image = pltpu.roll(gram, 128 - known, axis=1)
    keep = lane < VECS
    coef = jnp.where(
        keep & (row < known), -image, jnp.where(keep & (row == lane + known), 1.0, 0.0)
    )
    diag_ref[...] = image[0:VECS, 0:VECS]
    stored_ref[...] = jnp.transpose(image)[0:VECS, VECS:known]
    applied = jnp.dot(gram, coef, precision=HIGHEST, preferred_element_type=F32)
    small = lax.dot_general(
        coef, applied, (((0,), (0,)), ((), ())), precision=HIGHEST, preferred_element_type=F32
    )
    entry = [[small[i : i + 1, j : j + 1] for j in range(VECS)] for i in range(VECS)]
    factor = [[None] * VECS for _ in range(VECS)]
    for i in range(VECS):
        value = entry[i][i]
        for k in range(i):
            value = value - factor[k][i] * factor[k][i]
        factor[i][i] = jnp.sqrt(value)
        for j in range(i + 1, VECS):
            value = entry[i][j]
            for k in range(i):
                value = value - factor[k][i] * factor[k][j]
            factor[i][j] = value / factor[i][i]
    inverse = [[None] * VECS for _ in range(VECS)]
    for j in range(VECS):
        inverse[j][j] = 1.0 / factor[j][j]
        for i in range(j - 1, -1, -1):
            value = None
            for k in range(i + 1, j + 1):
                term = factor[i][k] * inverse[k][j]
                value = term if value is None else value + term
            inverse[i][j] = -value / factor[i][i]
    upper = jnp.zeros(square, F32)
    solved = jnp.zeros(square, F32)
    for i in range(VECS):
        for j in range(i, VECS):
            here = (row == i) & (lane == j)
            upper = jnp.where(here, factor[i][j], upper)
            solved = jnp.where(here, inverse[i][j], solved)
    factor_ref[...] = upper[0:VECS, 0:VECS]
    mixed = jnp.dot(coef, solved, precision=HIGHEST, preferred_element_type=F32)
    low = lane_ids((1, 128)) < 64
    straight, crossed = [], []
    for out in range(2):
        choose = (row == 2 * out + lane // 64).astype(F32)
        lines = jnp.dot(mixed, choose, precision=HIGHEST, preferred_element_type=F32)
        straight.append([])
        crossed.append([])
        for index in range(12):
            a = lines[2 * index : 2 * index + 1]
            b = lines[2 * index + 1 : 2 * index + 2]
            straight[out].append(jnp.where(low, a, b))
            crossed[out].append(jnp.where(low, b, a))
    for at in range(ROWS):
        result = [None, None]
        for index in range(12):
            tile = tile_of(q_ref, p_ref, u_ref, at, index)
            other = pltpu.roll(tile, 64, axis=1)
            for out in range(2):
                part = tile * straight[out][index] + other * crossed[out][index]
                result[out] = part if result[out] is None else result[out] + part
        for out in range(2):
            next_ref[:, at, out * 128 : (out + 1) * 128] = result[out]


def call(kernel, outs, scratch=(), final=False, far=(), raw=()):
    kinds = [shape(o.shape, o.dtype) if final else pltpu.VMEM(o.shape, o.dtype) for o in outs]

    def run(*args):
        placed, specs = [], []
        for index, value in enumerate(args):
            if value.dtype == jnp.int32:
                specs.append(pl.BlockSpec(memory_space=pltpu.SMEM))
            elif index in raw:
                specs.append(pl.BlockSpec(memory_space=pl.ANY))
            elif index in far:
                specs.append(pl.BlockSpec())
            else:
                specs.append(VMEM)
                value = pltpu.with_memory_space_constraint(value, pltpu.VMEM)
            placed.append(value)
        return pl.pallas_call(
            kernel,
            out_shape=kinds,
            in_specs=specs,
            out_specs=[VMEM] * len(outs),
            scratch_shapes=list(scratch),
        )(*placed)

    return run


def shape(dims, kind):
    return jax.ShapeDtypeStruct(dims, kind)


def per_device(ahead_table, back_table, state_block, stored_fields, slope_fields, kernels, gains):
    lat_count, lon_count = lax.axis_size("lat"), lax.axis_size("lon")
    near_pairs = [(i, i ^ 1) for i in range(lat_count)]
    far_pairs = [(i, i + 1) for i in range(1, lat_count - 1, 2)]
    far_pairs = far_pairs + [(b, a) for a, b in far_pairs]
    east = [(i, (i + 1) % lon_count) for i in range(lon_count)]
    width = LANES + LAYERS * CH

    native = jnp.transpose(state_block, (1, 0, 2))
    (both,) = call(pack_kernel, [shape((ROWS, COLS, width), BF16)], far=(0, 1))(
        native, jnp.transpose(slope_fields, (1, 0, 2))
    )
    parity = lax.axis_index("lat") % 2
    odd = jnp.full((1,), parity, jnp.int32)
    far = lax.ppermute(both, "lat", far_pairs)
    near = lax.ppermute(both, "lat", near_pairs)
    (last,) = call(sides_kernel, [shape((EXT, SIDE, width), BF16)])(odd, both, near, far)
    left = lax.ppermute(last, "lon", east)
    ahead_weights, back_weights = call(
        weights_kernel,
        [
            shape((LAYERS * 3, 3 * 128, 128), BF16),
            shape((LAYERS * 3, 128, 3 * 128), BF16),
        ],
    )(kernels.reshape(LAYERS * 9, CH, CH), last)

    place = lax.axis_index("lon")
    row_index = lax.axis_index("lat") * ROWS + place // 8
    area = jnp.cos(jnp.pi * ((row_index.astype(F32) + 0.5) / NLAT - 0.5))
    wave = jnp.arange(768)
    wave_weight = jnp.where((wave == 0) | (wave == NLON // 2), 1.0 / NLON, 2.0 / NLON)
    wave_weight = jnp.where(wave < WAVES, wave_weight, 0.0).astype(F32)
    columns = jnp.pad(gains, ((0, 0), (0, 768 - WAVES))).T * wave_weight[:, None]
    chosen = jnp.where(place % 2 == 0, columns[:, 0:SLOTS], columns[:, SLOTS : 2 * SLOTS])
    chosen = chosen * (area * area)
    weight = jnp.concatenate([chosen] * 4, axis=1)

    work = [
        pltpu.VMEM((FLAT, LANES), F32),
        pltpu.VMEM((FLAT, LANES), F32),
        pltpu.VMEM((EXT * PITCH, 3 * LANES), BF16),
    ]
    (packed,) = call(forward_kernel, [shape((32, 16, 128), BF16)], work)(
        odd, both, near, far, left, ahead_weights
    )
    circles = lax.all_to_all(packed, "lon", 0, 0, tiled=True)
    (known,) = call(
        stored_kernel, [shape((24, 24), F32)], [pltpu.VMEM((24, 10 * 128), F32)]
    )(native, stored_fields, packed)
    (filtered,) = call(
        filter_kernel,
        [shape((32, 16, 128), BF16)],
        [
            pltpu.VMEM((4, 768, 128), BF16),
            pltpu.VMEM(ahead_table.shape, BF16),
            pltpu.VMEM(back_table.shape, BF16),
            pltpu.SemaphoreType.DMA((8,)),
        ],
        far=(0,),
        raw=(1, 2),
    )(circles, ahead_table, back_table, weight, known)
    got = lax.all_to_all(filtered, "lon", 0, 0, tiled=True)
    gfar = lax.ppermute(got, "lat", far_pairs)
    gnear = lax.ppermute(got, "lat", near_pairs)
    image, sums = call(
        adjoint_kernel,
        [shape((ROWS, COLS, LANES), F32), shape((8, 128), F32)],
        work + [pltpu.VMEM((8, 12 * 128), F32)],
        far=(1, 2, 3, 4, 5, 6, 10),
    )(
        odd,
        native,
        stored_fields,
        both,
        near,
        far,
        left,
        got,
        gnear,
        gfar,
        back_weights,
        known,
    )
    spread = lax.all_to_all(
        jnp.broadcast_to(sums, (lat_count, 8, 128)), "lat", 0, 0, tiled=True
    )
    partial = spread.sum(0)
    spread = lax.all_to_all(
        jnp.broadcast_to(partial, (lon_count, 8, 128)), "lon", 0, 0, tiled=True
    )
    following, diag, stored, factor = call(
        finish_kernel,
        [
            shape((COLS, ROWS, LANES), F32),
            shape((VECS, VECS), F32),
            shape((VECS, STORED), F32),
            shape((VECS, VECS), F32),
        ],
        final=True,
    )(spread, native, stored_fields, image)
    return jnp.transpose(following, (1, 0, 2)), diag, stored.T, factor


def solution(mesh):
    ahead, back = tables()
    return jax.shard_map(
        functools.partial(per_device, jnp.asarray(ahead), jnp.asarray(back)),
        mesh=mesh,
        in_specs=(P("lat", "lon", None), P("lat", "lon", None), P("lat", "lon", None), P(), P()),
        out_specs=(P("lat", "lon", None), P(), P(), P()),
        check_vma=False,
    )
```

```python
import functools

import jax
import jax.numpy as jnp
import numpy as np
from jax import lax
from jax.experimental import pallas as pl
from jax.experimental.pallas import tpu as pltpu
from jax.sharding import PartitionSpec as P

F32 = jnp.float32
BF16 = jnp.bfloat16
HIGHEST = lax.Precision.HIGHEST

ROWS, COLS, CH, VECS, STORED, LAYERS = 4, 45, 64, 4, 16, 3
NLAT, NLON, WAVES = 64, 1440, 721
LANES = VECS * CH
HALO = 3
EXT = ROWS + 2 * HALO
PITCH = 64
LEAD = 8
SIDE = 8
FLAT = LEAD + EXT * PITCH + 8
SLOTS = 32
VMEM = pl.BlockSpec(memory_space=pltpu.VMEM)


def lane_ids(shape):
    return lax.broadcasted_iota(jnp.int32, shape, len(shape) - 1)


def row_ids(shape):
    return lax.broadcasted_iota(jnp.int32, shape, len(shape) - 2)


def tables():
    wave = 4 * np.arange(192)[None, :] + np.arange(4)[:, None]
    live = wave < WAVES
    q, t, j = np.meshgrid(np.arange(3), np.arange(8), np.arange(16), indexing="ij")
    slot = (16 * q + j).reshape(-1)
    point = (45 * t).reshape(-1) - 3 + slot
    angle = 2 * np.pi * ((wave[:, :, None] * point) % NLON) / NLON
    keep = live[:, :, None] & (slot < COLS)
    ahead = np.concatenate([np.cos(angle) * keep, np.sin(angle) * keep], axis=2)
    q, t, j = np.meshgrid(np.arange(4), np.arange(8), np.arange(16), indexing="ij")
    slot = (16 * q + j).reshape(-1)
    point = (45 * t).reshape(-1) - SIDE + slot
    angle = 2 * np.pi * ((wave[:, None, :] * point[None, :, None]) % NLON) / NLON
    held = (slot >= SIDE - HALO) & (slot < SIDE + COLS + HALO)
    keep = live[:, None, :] & held[None, :, None]
    back = np.concatenate([np.cos(angle) * keep, np.sin(angle) * keep], axis=2)
    return ahead.astype(jnp.bfloat16), back.astype(jnp.bfloat16)


def pack_kernel(q_ref, s_ref, out_ref):
    slopes = s_ref[...].astype(F32)
    for row in range(ROWS):
        out_ref[row, :, 0:LANES] = q_ref[:, row, :].astype(BF16)
        out_ref[row, :, LANES:] = slopes[:, row, :].astype(BF16)


def line_of(odd_ref, x_ref, near_ref, far_ref, row):
    if HALO <= row < HALO + ROWS:
        return x_ref[row - HALO].astype(F32)
    at = row + ROWS - HALO if row < HALO else row - HALO - ROWS
    near, far = near_ref[at].astype(F32), far_ref[at].astype(F32)
    odd = odd_ref[0] == 1
    return jnp.where(odd, near, far) if row < HALO else jnp.where(odd, far, near)


def sides_kernel(odd_ref, x_ref, near_ref, far_ref, last_ref):
    for row in range(EXT):
        line = line_of(odd_ref, x_ref, near_ref, far_ref, row)
        last_ref[row] = line[COLS - SIDE : COLS].astype(BF16)


def weights_kernel(taps_ref, after_ref, ahead_ref, back_ref):
    none = jnp.zeros((CH, CH), F32)
    for layer in range(LAYERS):
        for up in range(3):
            for side in range(3):
                block = taps_ref[9 * layer + 3 * up + side].astype(F32)
                pair = jnp.concatenate(
                    [
                        jnp.concatenate([block, none], axis=1),
                        jnp.concatenate([none, block], axis=1),
                    ],
                    axis=0,
                ).astype(BF16)
                ahead_ref[3 * layer + up, 128 * side : 128 * side + 128, :] = pair
                back_ref[3 * layer + 2 - up, :, 256 - 128 * side : 384 - 128 * side] = pair


def slope_lanes(slopes_ref, layer, start, count):
    pair = slopes_ref[pl.ds(start, count), (layer // 2) * 128 : (layer // 2) * 128 + 128]
    other = pltpu.roll(pair, 64, axis=1)
    low = lane_ids(pair.shape) < 64
    both = jnp.where(low, pair, other) if layer % 2 == 0 else jnp.where(low, other, pair)
    return jnp.concatenate([both, both], axis=1)


def convolve(field_ref, shifted_ref, weights_ref, layer, first, count, turned):
    have = (count + 2) * PITCH
    start = LEAD + (first - 1) * PITCH
    for pair in range(2):
        for step in range(3):
            at = 384 * pair + 128 * step
            shifted_ref[0:have, at : at + 128] = field_ref[
                pl.ds(start + step - 1, have), 128 * pair : 128 * pair + 128
            ].astype(BF16)
    halves = []
    for pair in range(2):
        total = None
        for step in range(3):
            part = lax.dot_general(
                shifted_ref[step * PITCH : (step + count) * PITCH, 384 * pair : 384 * pair + 384],
                weights_ref[layer * 3 + step],
                (((1,), (1 if turned else 0,)), ((), ())),
                preferred_element_type=F32,
            )
            total = part if total is None else total + part
        halves.append(total)
    return jnp.concatenate(halves, axis=1)


def parcel(slopes_ref, index):
    if index >= EXT * LAYERS:
        return jnp.zeros((16, SLOTS), F32)
    row, layer = index // LAYERS, index % LAYERS
    at = LEAD + row * PITCH + SIDE
    block = slopes_ref[at : at + 8, (layer // 2) * 128 : (layer // 2) * 128 + 128]
    base = 64 * (layer % 2)
    return jnp.concatenate(
        [
            jnp.zeros((8, SLOTS), F32),
            block[0:4, base : base + SLOTS],
            block[0:4, base + SLOTS : base + 2 * SLOTS],
        ],
        axis=0,
    )


def forward_kernel(
    odd_ref,
    x_ref,
    near_ref,
    far_ref,
    left_ref,
    weights_ref,
    send_ref,
    field_ref,
    slopes_ref,
    shifted_ref,
):
    field_ref[...] = jnp.zeros((FLAT, LANES), F32)
    slopes_ref[...] = jnp.zeros((FLAT, LANES), F32)
    for row in range(EXT):
        at = LEAD + row * PITCH
        line = line_of(odd_ref, x_ref, near_ref, far_ref, row)
        side = left_ref[row].astype(F32)
        field_ref[at : at + SIDE, :] = side[:, 0:LANES]
        field_ref[at + SIDE : at + SIDE + COLS, :] = line[:, 0:LANES]
        slopes_ref[at : at + SIDE, 0:192] = side[:, LANES:]
        slopes_ref[at + SIDE : at + SIDE + COLS, 0:192] = line[:, LANES:]
    for layer in range(LAYERS):
        first = layer + 1
        count = EXT - 2 * first
        total = convolve(field_ref, shifted_ref, weights_ref, layer, first, count, False)
        start = LEAD + first * PITCH
        total = total * slope_lanes(slopes_ref, layer, start, count * PITCH)
        field_ref[start : start + count * PITCH, :] = total.astype(BF16).astype(F32)
    for row in range(ROWS):
        line = field_ref[pl.ds(LEAD + (HALO + row) * PITCH + SIDE - HALO, 48), :]
        for group in range(8):
            pieces = [
                line[16 * q : 16 * q + 16, group * SLOTS : (group + 1) * SLOTS] for q in range(3)
            ]
            pieces.append(parcel(slopes_ref, row * 8 + group))
            send_ref[row * 8 + group] = jnp.concatenate(pieces, axis=1).astype(BF16)


def filter_kernel(
    got_ref, ahead_ref, back_ref, gains_ref, known_ref, send_ref, work_ref
):
    quarter = [
        got_ref[8 * part : 8 * part + 8].astype(F32).reshape(128, 128) for part in range(4)
    ]
    even, odd = quarter[0] + quarter[2], quarter[1] + quarter[3]
    across, along = quarter[0] - quarter[2], quarter[1] - quarter[3]
    real = [even + odd, across, even - odd, across]
    imag = [None, -along, None, along]
    low = lane_ids((128, 128)) < SLOTS

    def turn(value, shift):
        return value if shift % 128 == 0 else pltpu.roll(value, shift % 128, axis=1)

    for kind in range(4):
        for q in range(3):
            a = real[kind]
            b = imag[kind]
            left, right = turn(a, -SLOTS * q), turn(a, SLOTS - SLOTS * q)
            if b is None:
                top = jnp.where(low, left, 0.0)
                bottom = jnp.where(low, 0.0, -right)
            else:
                top = jnp.where(low, left, turn(b, SLOTS - SLOTS * q))
                bottom = jnp.where(low, turn(b, -SLOTS * q), -right)
            work_ref[128 * q : 128 * q + 128, :] = top.astype(BF16)
            work_ref[384 + 128 * q : 512 + 128 * q, :] = bottom.astype(BF16)
        spectrum = jnp.dot(ahead_ref[kind], work_ref[...], preferred_element_type=F32)
        weight = gains_ref[pl.ds(kind, 192, stride=4), :]
        spectrum = spectrum * weight
        below = jnp.where(
            lane_ids((192, 128)) < SLOTS, -turn(spectrum, -SLOTS), turn(spectrum, SLOTS)
        )
        packed = jnp.concatenate([spectrum, below], axis=0).astype(BF16)
        part = jnp.dot(back_ref[kind], packed, preferred_element_type=F32)
        if kind == 0:
            zero = part
        elif kind == 1:
            one = part
        elif kind == 2:
            two = part
        else:
            three = part
    plus, minus = zero + two, zero - two
    swing = one + three
    turned = turn(three - one, -SLOTS)
    result = [plus + swing, minus + turned, plus - swing, minus - turned]
    lane = lane_ids((128, 128))
    for part in range(4):
        packed = result[part][0:128]
        for q in range(1, 4):
            packed = jnp.where(
                lane >= SLOTS * q, turn(result[part][128 * q : 128 * q + 128], SLOTS * q), packed
            )
        if part < 3:
            passing = got_ref[8 * part + 1 : 8 * part + 9]
        else:
            passing = jnp.concatenate([got_ref[25:32], got_ref[0:1]], axis=0)
        carried = (lane >= 96) & (row_ids((128, 128)) % 16 >= 8)
        packed = jnp.where(carried, passing.astype(F32).reshape(128, 128), packed)
        send_ref[8 * part : 8 * part + 8] = packed.reshape(8, 16, 128).astype(BF16)


def twice(tile, half):
    other = pltpu.roll(tile, 64, axis=1)
    low = lane_ids(tile.shape) < 64
    return jnp.where(low, tile, other) if half == 0 else jnp.where(low, other, tile)


def gram_rows(rows_ref):
    wide = (24, rows_ref.shape[1])
    pick = (row_ids(wide) == lane_ids(wide) // 64).astype(F32)
    return lax.dot_general(
        pick,
        rows_ref[...],
        (((1,), (1,)), ((), ())),
        precision=HIGHEST,
        preferred_element_type=F32,
    )


def stored_kernel(q_ref, p_ref, after_ref, out_ref, rows_ref):
    rows_ref[...] = jnp.zeros(rows_ref.shape, F32)
    known = 10
    for right in range(known):
        for half in range(2):
            totals = [None] * (right + 1)
            for row in range(ROWS):
                tile = tile_of(q_ref, p_ref, None, row, right)
                doubled = twice(tile, half)
                for left in range(right + 1):
                    product = tile_of(q_ref, p_ref, None, row, left) * doubled
                    totals[left] = product if totals[left] is None else totals[left] + product
            for left in range(right + 1):
                rows_ref[2 * right + half : 2 * right + half + 1, 128 * left : 128 * left + 128] = jnp.sum(
                    totals[left], axis=0, keepdims=True
                )
    out_ref[...] = gram_rows(rows_ref)


def tile_of(q_ref, p_ref, u_ref, row, index):
    if index < 2:
        return q_ref[:, row, index * 128 : (index + 1) * 128]
    if index < 10:
        return p_ref[row, :, (index - 2) * 128 : (index - 1) * 128].astype(F32)
    return u_ref[row, :, (index - 10) * 128 : (index - 9) * 128]


def adjoint_kernel(
    odd_ref,
    q_ref,
    p_ref,
    x_ref,
    near_ref,
    far_ref,
    left_ref,
    got_ref,
    gnear_ref,
    gfar_ref,
    weights_ref,
    known_ref,
    u_ref,
    sums_ref,
    field_ref,
    slopes_ref,
    shifted_ref,
    rows_ref,
):
    field_ref[0:LEAD, :] = jnp.zeros((LEAD, LANES), F32)
    field_ref[FLAT - 8 : FLAT, :] = jnp.zeros((8, LANES), F32)
    slopes_ref[...] = jnp.zeros((FLAT, LANES), F32)
    for row in range(EXT):
        at = LEAD + row * PITCH
        line = line_of(odd_ref, x_ref, near_ref, far_ref, row)
        slopes_ref[at : at + SIDE, 0:192] = left_ref[row, :, LANES:].astype(F32)
        slopes_ref[at + SIDE : at + SIDE + COLS, 0:192] = line[:, LANES:]
        halves = []
        for layer in range(LAYERS):
            block = got_ref[LAYERS * row + layer].astype(F32)
            halves += [block[8:12, 96:128], block[12:16, 96:128]]
        slopes_ref[at + SIDE + COLS : at + SIDE + COLS + 4, 0:192] = jnp.concatenate(halves, axis=1)
    for row in range(EXT):
        at = LEAD + row * PITCH
        if HALO <= row < HALO + ROWS:
            base = (row - HALO) * 8
            blocks = [got_ref[base + group].astype(F32) for group in range(8)]
        else:
            base = (row + 1) * 8 if row < HALO else (row - HALO - ROWS) * 8
            odd = odd_ref[0] == 1
            blocks = []
            for group in range(8):
                near = gnear_ref[base + group].astype(F32)
                far = gfar_ref[base + group].astype(F32)
                first, second = (near, far) if row < HALO else (far, near)
                blocks.append(jnp.where(odd, first, second))
        for q in range(4):
            field_ref[at + 16 * q : at + 16 * q + 16, :] = jnp.concatenate(
                [block[:, q * SLOTS : (q + 1) * SLOTS] for block in blocks], axis=1
            )
    top = field_ref[LEAD : LEAD + EXT * PITCH, :] * slope_lanes(
        slopes_ref, LAYERS - 1, LEAD, EXT * PITCH
    )
    field_ref[LEAD : LEAD + EXT * PITCH, :] = top.astype(BF16).astype(F32)
    for layer in range(LAYERS - 1, -1, -1):
        first = LAYERS - layer
        count = EXT - 2 * first
        total = convolve(field_ref, shifted_ref, weights_ref, layer, first, count, True)
        start = LEAD + first * PITCH
        if layer > 0:
            total = total * slope_lanes(slopes_ref, layer - 1, start, count * PITCH)
            total = total.astype(BF16).astype(F32)
        field_ref[start : start + count * PITCH, :] = total
    for row in range(ROWS):
        u_ref[row] = field_ref[pl.ds(LEAD + (HALO + row) * PITCH + SIDE, COLS), :]
    rows_ref[...] = jnp.zeros(rows_ref.shape, F32)
    for right in range(2):
        for half in range(2):
            totals = [None] * 12
            for row in range(ROWS):
                doubled = twice(tile_of(q_ref, p_ref, u_ref, row, 10 + right), half)
                for left in range(12):
                    product = tile_of(q_ref, p_ref, u_ref, row, left) * doubled
                    totals[left] = product if totals[left] is None else totals[left] + product
            for left in range(12):
                at = 2 * right + half
                rows_ref[at : at + 1, 128 * left : 128 * left + 128] = jnp.sum(
                    totals[left], axis=0, keepdims=True
                )
    gram = gram_rows(rows_ref)[:, 0:VECS]
    wide = jnp.concatenate(
        [known_ref[:, 0:20], gram, jnp.zeros((24, 128 - 24), F32)], axis=1
    )
    sums_ref[...] = (
        wide[0:8]
        + pltpu.roll(wide[8:16], SLOTS, axis=1)
        + pltpu.roll(wide[16:24], 2 * SLOTS, axis=1)
    )


def finish_kernel(sums_ref, q_ref, p_ref, u_ref, next_ref, diag_ref, stored_ref, factor_ref):
    total = sums_ref[0]
    for index in range(1, sums_ref.shape[0]):
        total = total + sums_ref[index]
    total = total * (1.0 / (NLAT * NLON * CH))
    narrow = lane_ids((8, 128)) < SLOTS
    blocks = [
        jnp.where(narrow, total if k == 0 else pltpu.roll(total, 128 - SLOTS * k, axis=1), 0.0)
        for k in range(3)
    ]
    square = (128, 128)
    half = jnp.concatenate(blocks + [jnp.zeros((104, 128), F32)], axis=0)
    gram = jnp.where(row_ids(square) <= lane_ids(square), half, jnp.transpose(half))[0:32]
    tall = (32, 128)
    row, lane = row_ids(tall), lane_ids(tall)
    known = VECS + STORED
    image = pltpu.roll(gram, 128 - known, axis=1)
    keep = lane < VECS
    coef = jnp.where(
        keep & (row < known), -image, jnp.where(keep & (row == lane + known), 1.0, 0.0)
    )
    diag_ref[...] = image[0:VECS, 0:VECS]
    stored_ref[...] = jnp.transpose(half)[known : known + VECS, VECS:known]
    applied = jnp.dot(gram[:, 0:32], coef, precision=HIGHEST, preferred_element_type=F32)
    small = lax.dot_general(
        coef[:, 0:8],
        applied,
        (((0,), (0,)), ((), ())),
        precision=HIGHEST,
        preferred_element_type=F32,
    )
    entry = [[small[i : i + 1, j : j + 1] for j in range(VECS)] for i in range(VECS)]
    factor = [[None] * VECS for _ in range(VECS)]
    for i in range(VECS):
        value = entry[i][i]
        for k in range(i):
            value = value - factor[k][i] * factor[k][i]
        factor[i][i] = jnp.sqrt(value)
        for j in range(i + 1, VECS):
            value = entry[i][j]
            for k in range(i):
                value = value - factor[k][i] * factor[k][j]
            factor[i][j] = value / factor[i][i]
    inverse = [[None] * VECS for _ in range(VECS)]
    for j in range(VECS):
        inverse[j][j] = 1.0 / factor[j][j]
        for i in range(j - 1, -1, -1):
            value = None
            for k in range(i + 1, j + 1):
                term = factor[i][k] * inverse[k][j]
                value = term if value is None else value + term
            inverse[i][j] = -value / factor[i][i]
    flat = (8, 128)
    row, lane = row_ids(flat), lane_ids(flat)
    upper = jnp.zeros(flat, F32)
    solved = jnp.zeros(flat, F32)
    for i in range(VECS):
        for j in range(i, VECS):
            here = (row == i) & (lane == j)
            upper = jnp.where(here, factor[i][j], upper)
            solved = jnp.where(here, inverse[i][j], solved)
    factor_ref[...] = upper[0:VECS, 0:VECS]
    mixed = jnp.dot(coef[:, 0:8], solved, precision=HIGHEST, preferred_element_type=F32)
    low = lane_ids((1, 128)) < 64
    straight, crossed = [], []
    for out in range(2):
        choose = (row == 2 * out + lane // 64).astype(F32)
        lines = jnp.dot(mixed[:, 0:8], choose, precision=HIGHEST, preferred_element_type=F32)
        straight.append([])
        crossed.append([])
        for index in range(12):
            a = lines[2 * index : 2 * index + 1]
            b = lines[2 * index + 1 : 2 * index + 2]
            straight[out].append(jnp.where(low, a, b))
            crossed[out].append(jnp.where(low, b, a))
    for at in range(ROWS):
        result = [None, None]
        for index in range(12):
            tile = tile_of(q_ref, p_ref, u_ref, at, index)
            other = pltpu.roll(tile, 64, axis=1)
            for out in range(2):
                part = tile * straight[out][index] + other * crossed[out][index]
                result[out] = part if result[out] is None else result[out] + part
        for out in range(2):
            next_ref[:, at, out * 128 : (out + 1) * 128] = result[out]


def call(kernel, outs, scratch=(), final=False, far=()):
    kinds = [shape(o.shape, o.dtype) if final else pltpu.VMEM(o.shape, o.dtype) for o in outs]

    def run(*args):
        placed, specs = [], []
        for index, value in enumerate(args):
            if value.dtype == jnp.int32:
                specs.append(pl.BlockSpec(memory_space=pltpu.SMEM))
            elif index in far:
                specs.append(pl.BlockSpec())
            else:
                specs.append(VMEM)
                value = pltpu.with_memory_space_constraint(value, pltpu.VMEM)
            placed.append(value)
        return pl.pallas_call(
            kernel,
            out_shape=kinds,
            in_specs=specs,
            out_specs=[VMEM] * len(outs),
            scratch_shapes=list(scratch),
        )(*placed)

    return run


def shape(dims, kind):
    return jax.ShapeDtypeStruct(dims, kind)


def per_device(ahead_table, back_table, state_block, stored_fields, slope_fields, kernels, gains):
    lat_count, lon_count = lax.axis_size("lat"), lax.axis_size("lon")
    near_pairs = [(i, i ^ 1) for i in range(lat_count)]
    far_pairs = [(i, i + 1) for i in range(1, lat_count - 1, 2)]
    far_pairs = far_pairs + [(b, a) for a, b in far_pairs]
    east = [(i, (i + 1) % lon_count) for i in range(lon_count)]
    width = LANES + LAYERS * CH

    native = jnp.transpose(state_block, (1, 0, 2))
    (both,) = call(pack_kernel, [shape((ROWS, COLS, width), BF16)], far=(0, 1))(
        native, jnp.transpose(slope_fields, (1, 0, 2))
    )
    parity = lax.axis_index("lat") % 2
    odd = jnp.full((1,), parity, jnp.int32)
    far = lax.ppermute(both, "lat", far_pairs)
    near = lax.ppermute(both, "lat", near_pairs)
    (last,) = call(sides_kernel, [shape((EXT, SIDE, width), BF16)])(odd, both, near, far)
    left = lax.ppermute(last, "lon", east)
    ahead_weights, back_weights = call(
        weights_kernel,
        [
            shape((LAYERS * 3, 3 * 128, 128), BF16),
            shape((LAYERS * 3, 128, 3 * 128), BF16),
        ],
    )(kernels.reshape(LAYERS * 9, CH, CH), last)

    place = lax.axis_index("lon")
    row_index = lax.axis_index("lat") * ROWS + place // 8
    area = jnp.cos(jnp.pi * ((row_index.astype(F32) + 0.5) / NLAT - 0.5))
    wave = jnp.arange(768)
    wave_weight = jnp.where((wave == 0) | (wave == NLON // 2), 1.0 / NLON, 2.0 / NLON)
    wave_weight = jnp.where(wave < WAVES, wave_weight, 0.0).astype(F32)
    columns = jnp.pad(gains, ((0, 0), (0, 768 - WAVES))).T * wave_weight[:, None]
    chosen = jnp.where(place % 2 == 0, columns[:, 0:SLOTS], columns[:, SLOTS : 2 * SLOTS])
    chosen = chosen * (area * area)
    weight = jnp.concatenate([chosen] * 4, axis=1)

    work = [
        pltpu.VMEM((FLAT, LANES), F32),
        pltpu.VMEM((FLAT, LANES), F32),
        pltpu.VMEM((EXT * PITCH, 3 * LANES), BF16),
    ]
    (packed,) = call(forward_kernel, [shape((32, 16, 128), BF16)], work)(
        odd, both, near, far, left, ahead_weights
    )
    circles = lax.all_to_all(packed, "lon", 0, 0, tiled=True)
    (known,) = call(
        stored_kernel, [shape((24, 24), F32)], [pltpu.VMEM((24, 10 * 128), F32)]
    )(native, stored_fields, packed)
    (filtered,) = call(
        filter_kernel, [shape((32, 16, 128), BF16)], [pltpu.VMEM((768, 128), BF16)], far=(0, 1, 2)
    )(circles, ahead_table, back_table, weight, known)
    got = lax.all_to_all(filtered, "lon", 0, 0, tiled=True)
    gfar = lax.ppermute(got, "lat", far_pairs)
    gnear = lax.ppermute(got, "lat", near_pairs)
    image, sums = call(
        adjoint_kernel,
        [shape((ROWS, COLS, LANES), F32), shape((8, 128), F32)],
        work + [pltpu.VMEM((8, 12 * 128), F32)],
        far=(1, 2, 3, 4, 5, 6, 10),
    )(
        odd,
        native,
        stored_fields,
        both,
        near,
        far,
        left,
        got,
        gnear,
        gfar,
        back_weights,
        known,
    )
    spread = lax.all_to_all(
        jnp.broadcast_to(sums, (lat_count, 8, 128)), "lat", 0, 0, tiled=True
    )
    partial = spread.sum(0)
    spread = lax.all_to_all(
        jnp.broadcast_to(partial, (lon_count, 8, 128)), "lon", 0, 0, tiled=True
    )
    following, diag, stored, factor = call(
        finish_kernel,
        [
            shape((COLS, ROWS, LANES), F32),
            shape((VECS, VECS), F32),
            shape((VECS, STORED), F32),
            shape((VECS, VECS), F32),
        ],
        final=True,
    )(spread, native, stored_fields, image)
    return jnp.transpose(following, (1, 0, 2)), diag, stored.T, factor


def solution(mesh):
    ahead, back = tables()
    return jax.shard_map(
        functools.partial(per_device, jnp.asarray(ahead), jnp.asarray(back)),
        mesh=mesh,
        in_specs=(P("lat", "lon", None), P("lat", "lon", None), P("lat", "lon", None), P(), P()),
        out_specs=(P("lat", "lon", None), P(), P(), P()),
        check_vma=False,
    )
```
